32 devices in a mesh: dp: 8 (over z, x), mp: 4 (over y, core).
Axes of the slice: x: 2, y: 2, z: 4, core: 2. Of those that a mesh axis runs over, the one named last changes fastest.
Arguments:
- token_ids: int32 [64, 512], P('dp'), may hold values from 0 to 30719
- seg_split: int32 [64], P('dp'), may hold values from 1 to 255
- lengths: int32 [64], P('dp'), may hold values from 256 to 512, as said below
- mlm_pos: int32 [64, 80], P('dp'), may hold values from 1 to 255
- mlm_labels: int32 [64, 80], P('dp'), may hold values from 0 to 30719
- sop_labels: int32 [64], P('dp'), may hold values from 0 to 1
- owner: int32 [8], replicated, may hold values from 0 to 7, as said below
- step_count: int32 [1], replicated, may hold values from 1 to 20
- table: float32 [30720, 768], P(('dp', 'mp')), may hold values from -0.6134347 to 0.6134347
- table_m: float32 [30720, 768], P(('dp', 'mp')), may hold values from -2.3841858e-06 to 2.3841858e-06
- table_v: float32 [30720, 768], P(('dp', 'mp')), may hold values from 1.4128509e-14 to 5.6514035e-14
- unit_master: float32 [16, 768, 768], P('dp', 'mp')
- unit_m: float32 [16, 768, 768], P('dp', 'mp'), may hold values from -2.3841858e-06 to 2.3841858e-06
- unit_v: float32 [16, 768, 768], P('dp', 'mp'), may hold values from 1.4128509e-14 to 5.6514035e-14
- small: float32 [522, 768], replicated
- small_m: float32 [522, 768], replicated, may hold values from -6.67572e-06 to 6.67572e-06
- small_v: float32 [522, 768], replicated, may hold values from 8.979885e-14 to 3.591954e-13
- taps: float32 [9, 384], replicated, may hold values from -0.75 to 0.75
- taps_m: float32 [9, 384], replicated, may hold values from -2.2888184e-05 to 2.2888184e-05
- taps_v: float32 [9, 384], replicated, may hold values from 1.1574074e-12 to 4.6296296e-12
Outputs:
- loss: float32 [], replicated
- grad_norm: float32 [], replicated
- table_new: float32 [30720, 768], P(('dp', 'mp'))
- table_m_new: float32 [30720, 768], P(('dp', 'mp'))
- table_v_new: float32 [30720, 768], P(('dp', 'mp'))
- table_copy: bfloat16 [30720, 768], P(('dp', 'mp'))
- unit_new: float32 [16, 768, 768], P('dp', 'mp')
- unit_m_new: float32 [16, 768, 768], P('dp', 'mp')
- unit_v_new: float32 [16, 768, 768], P('dp', 'mp')
- unit_copy: bfloat16 [16, 768, 768], P('dp', 'mp')
- small_new: float32 [522, 768], replicated
- small_m_new: float32 [522, 768], replicated
- small_v_new: float32 [522, 768], replicated
- taps_new: float32 [9, 384], replicated
- taps_m_new: float32 [9, 384], replicated
- taps_v_new: float32 [9, 384], replicated
The draws below stay inside these ranges and needn't reach their ends.
Inputs may be any that keep to these rules, and one draw needn't show every extreme that they name: Tokens at positions from lengths on are padding; the first sequence is full. `owner`: every index of dp keeps at most 2 of the 8 layer matrices, and two indices keep exactly 2; slots beyond an index's matrices are unused. `mlm_pos`: masked positions lie below every length and may repeat.
All inputs are finite; a program needn't handle non-finite values.
Results may differ from the reference program's by a relative error of at most 0.0029.
The reference program's roundings to bfloat16 on the way count: a program that leaves them out, or rounds other values in their place, can miss the bound.
Values may be sent and summed in bfloat16 or wider, within the bound.
No kernel may reach another device: no remote copies, remote signals or barrier semaphores. Data moves between devices by JAX's collectives and lax.ppermute only.
A program may use at most 384 MiB of HBM per device.

```python
import math
import jax
import jax.numpy as jnp
import numpy as np
from jax import lax

D = 768
HEADS = 12
DH = 64
V = 30720
KW = 9
LEN = 512
P_SIZE = 80
NUNIT = 8
CAP = 2
SEQS = 64
NCONV = 6
SROWS = 522
SLOTS = 16
N_DP = 8
N_MP = 4


def owner_list(key):
    chosen = jax.random.permutation(jax.random.fold_in(key, 1), N_DP)[:6]
    pattern = jnp.array([0, 0, 1, 1, 2, 3, 4, 5], jnp.int32)
    order = jax.random.permutation(jax.random.fold_in(key, 2), NUNIT)
    return chosen[pattern[order]].astype(jnp.int32)


def common_sign(key):
    flips = jax.random.bernoulli(jax.random.fold_in(key, 21), 0.5, (D,))
    return jnp.where(flips, 1.0, -1.0).astype(jnp.float32)


def draw_owner(key, part):
    return owner_list(jax.random.fold_in(key, 11))


def draw_lengths(key, part):
    drawn = jax.random.randint(key, (SEQS,), LEN // 2, LEN + 1).astype(jnp.int32)
    return drawn.at[0].set(LEN)


def draw_table(key, part):
    place = jnp.arange(V, dtype=jnp.float32)[:, None] / V
    jitter = jax.random.uniform(jax.random.fold_in(key, 5), (V, 1), jnp.float32, 0.7, 1.4)
    entries = jnp.clip(jax.random.normal(jax.random.fold_in(key, 6), (V, D), jnp.float32), -4.0, 4.0)
    row_scale = 0.6 * jnp.exp(place * 1.6094379)
    general = entries * row_scale * jitter * D ** (-0.5)
    planted_count = max(V // 320, 1)
    chosen_rows = jax.random.permutation(jax.random.fold_in(key, 22), V)[:planted_count]
    planted = jnp.zeros((V,), jnp.float32).at[chosen_rows].set(1.0)
    row_norm = jax.random.uniform(jax.random.fold_in(key, 23), (V, 1), jnp.float32, 1.0, 1.2)
    spread_part = jnp.clip(jax.random.normal(jax.random.fold_in(key, 24), (V, D), jnp.float32), -4.0, 4.0)
    aligned = row_norm * (0.95 * common_sign(key)[None, :] + 0.3 * spread_part) * D ** (-0.5)
    return jnp.where(planted[:, None] > 0.5, aligned, general)


def draw_unit_master(key, part):
    owner = owner_list(jax.random.fold_in(key, 11))
    count = owner.shape[0]
    earlier = jnp.arange(count)[:, None] > jnp.arange(count)[None, :]
    slot_rank = jnp.sum(jnp.logical_and(earlier, owner[:, None] == owner[None, :]), axis=1).astype(jnp.int32)
    slot_index = owner * CAP + slot_rank
    base = D ** (-0.5)
    unit_scale = jnp.array([1.0, 1.0, 1.0, 4.0, 1.41421356, 1.41421356, 1.0, 1.0], jnp.float32) * base
    slot_scale = jnp.full((SLOTS,), base, jnp.float32).at[slot_index].set(unit_scale)
    noise = jax.random.normal(jax.random.fold_in(key, 3), (SLOTS, D, D), jnp.float32)
    return noise * slot_scale[:, None, None]


def draw_small(key, part):
    noise = jax.random.normal(key, (SROWS, D), jnp.float32)
    gains = 1.0 + 0.1 * noise[0:3]
    offsets = 0.1 * noise[3:6]
    offsets = offsets.at[2].add(0.4 * common_sign(key))
    places = 0.5 * noise[6:LEN + 8]
    sentence = noise[LEN + 8:LEN + 10] * (2.0 * D ** (-0.5))
    return jnp.concatenate([gains, offsets, places, sentence], axis=0)


def touch_ends(values, stream_key, smallest, top_value):
    longest = values.shape.index(max(values.shape))
    spots = []
    for shift in (0, 1):
        where = [jax.random.randint(jax.random.fold_in(stream_key, axis), (), 0, length) for axis, length in enumerate(values.shape)]
        where[longest] = (where[longest] + shift) % values.shape[longest]
        spots.append(tuple(where))
    return values.at[spots[0]].set(smallest).at[spots[1]].set(top_value)


def level_of(own_key, extent, cuts, least, top_value):
    level = 1.0
    for axis_at, parts in cuts:
        draws = jax.random.uniform(jax.random.fold_in(jax.random.fold_in(own_key, 6), axis_at), (parts,), jnp.float32, least / len(cuts), top_value / len(cuts))
        level = level * jnp.repeat(jnp.exp(draws), extent[axis_at] // parts).reshape((-1,) + (1,) * (len(extent) - 1 - axis_at))
    return level


def rank_bounds(count, lean):
    loads = [(1 << 20) // math.isqrt(grade ** lean) + 1 for grade in range(1, count + 1)]
    scale = 1 + sum(loads) // (1 << 30)
    return np.cumsum(np.array([max(1, weight // scale) for weight in loads]))


def ranked_ids(key, dims, count, lean):
    listing = rank_bounds(count, lean)
    ticket = jax.random.randint(jax.random.fold_in(key, 1), dims, 0, int(listing[count - 1]))
    rank = jnp.searchsorted(jnp.asarray(listing, jnp.int32), ticket, side="right")
    return jax.random.permutation(jax.random.fold_in(key, 2), count)[rank].astype(jnp.int32)


def centred(stream_key, shape, scale, reach, shards=(), kind=jnp.bfloat16):
    result = jax.random.normal(stream_key, shape, jnp.float32) * scale
    if len(shards) > 0:
        result = level_of(stream_key, shape, shards, -0.22, 0.18) * result
    return jnp.clip(result, min=-reach, max=reach).astype(kind)


def setup_inputs(seed: int = 0) -> dict:
    splits = jax.random.split(jax.random.key(seed), 21)
    token_ids = touch_ends(ranked_ids(splits[0], (SEQS, LEN), V, 2), jax.random.fold_in(splits[0], 3), 0, V - 1).astype(jnp.int32)
    seg_split = touch_ends(jax.random.randint(splits[1], (SEQS,), 1, LEN // 2), jax.random.fold_in(splits[1], 1), 1, (LEN // 2) - 1).astype(jnp.int32)
    lengths = draw_lengths(jax.random.fold_in(splits[20], 71), 0)
    mlm_pos = touch_ends(jax.random.randint(splits[3], (SEQS, P_SIZE), 1, LEN // 2), jax.random.fold_in(splits[3], 1), 1, (LEN // 2) - 1).astype(jnp.int32)
    mlm_labels = touch_ends(ranked_ids(splits[4], (SEQS, P_SIZE), V, 2), jax.random.fold_in(splits[4], 3), 0, V - 1).astype(jnp.int32)
    sop_labels = touch_ends(jax.random.randint(splits[5], (SEQS,), 0, 2), jax.random.fold_in(splits[5], 1), 0, 1).astype(jnp.int32)
    owner = draw_owner(jax.random.fold_in(splits[20], 71), 0)
    step_count = jax.random.randint(splits[7], (1,), 1, 21).astype(jnp.int32)
    table = draw_table(jax.random.fold_in(splits[20], 71), 0)
    table_m = centred(splits[9], (V, D), (0.11 * 0.02 / (V * D + 8 * D * D) ** 0.5), 2.384185791015625e-06, ((0, 32),), jnp.float32)
    table_v = jnp.clip(jnp.exp(math.log(5.651403485267513e-14) - 1.3862944 * jax.random.uniform(splits[10], (V, D), jnp.float32) ** level_of(splits[10], (V, D), ((0, 32),), -0.2, 0.2)), 1.4128508713168782e-14, 5.651403485267513e-14)
    unit_master = draw_unit_master(jax.random.fold_in(splits[20], 71), 0)
    unit_m = centred(splits[12], (SLOTS, D, D), (0.11 * 0.02 / (V * D + 8 * D * D) ** 0.5), 2.384185791015625e-06, ((0, 8), (1, 4)), jnp.float32)
    unit_v = jnp.clip(jnp.exp(math.log(5.651403485267513e-14) - 1.3862944 * jax.random.uniform(splits[13], (SLOTS, D, D), jnp.float32) ** level_of(splits[13], (SLOTS, D, D), ((0, 8), (1, 4)), -0.2, 0.2)), 1.4128508713168782e-14, 5.651403485267513e-14)
    small = draw_small(jax.random.fold_in(splits[20], 71), 0)
    small_m = centred(splits[15], (SROWS, D), (0.11 * 0.006 / (SROWS * D) ** 0.5), 6.67572021484375e-06, (), jnp.float32)
    small_v = jnp.clip(jnp.exp(jax.random.uniform(splits[16], (SROWS, D), jnp.float32, math.log(8.979884842446814e-14), math.log(3.5919539369787257e-13))), 8.979884842446814e-14, 3.5919539369787257e-13)
    taps = centred(splits[17], (KW, NCONV * DH), DH ** -0.5, 0.75, (), jnp.float32)
    taps_m = centred(splits[18], (KW, NCONV * DH), (0.11 * 0.002 / (KW * NCONV * DH) ** 0.5), 2.288818359375e-05, (), jnp.float32)
    taps_v = jnp.clip(jnp.exp(jax.random.uniform(splits[19], (KW, NCONV * DH), jnp.float32, math.log(1.1574073947515084e-12), math.log(4.629629579006034e-12))), 1.1574073947515084e-12, 4.629629579006034e-12)
    return {"token_ids": token_ids, "seg_split": seg_split, "lengths": lengths, "mlm_pos": mlm_pos, "mlm_labels": mlm_labels, "sop_labels": sop_labels, "owner": owner, "step_count": step_count, "table": table, "table_m": table_m, "table_v": table_v, "unit_master": unit_master, "unit_m": unit_m, "unit_v": unit_v, "small": small, "small_m": small_m, "small_v": small_v, "taps": taps, "taps_m": taps_m, "taps_v": taps_v}


@jax.custom_vjp
def low(v):
    return lax.optimization_barrier(v.astype(jnp.bfloat16)).astype(jnp.float32)

@jax.custom_vjp
def low_back(v):
    return v

def low_keep(v):
    return (low(v), None)

def low_pass(kept, grad):
    return (grad,)

def back_keep(v):
    return (v, None)

def back_low(kept, grad):
    return (low(grad),)
low.defvjp(low_keep, low_pass)
low_back.defvjp(back_keep, back_low)
highest = lax.Precision.HIGHEST
beta_one = 0.9
beta_two = 0.999
adam_eps = 1e-08
learn_rate = 0.03
weight_decay = 0.01
clip_bound = 0.02
norm_eps = 1e-06

def both_ways(value):
    return low(low_back(value))

def matmul(left, right):
    return jnp.dot(left, right, precision=highest)

def layer_norm(stream, gain, offset):
    center = lax.optimization_barrier(jnp.mean(stream, axis=-1, keepdims=True))
    shifted = stream - center
    spread = lax.optimization_barrier(jnp.mean(shifted * shifted, axis=-1, keepdims=True))
    return shifted * lax.rsqrt(spread + norm_eps) * gain + offset

def embed_rows(word_rows, params, split_at):
    length = word_rows.shape[-2]
    second = (jnp.arange(length)[None, :] > split_at[:, None]).astype(jnp.float32)[..., None]
    summed = word_rows + params[6:6 + length] + params[6 + length] * (1.0 - second) + params[7 + length] * second
    return layer_norm(summed, params[0], params[3])

def conv_head(queries, key_rows, values, taps_head):
    length = queries.shape[0]
    width = taps_head.shape[0]
    logits = jnp.dot(queries * key_rows, taps_head.T, precision=highest)
    kernel = jax.nn.softmax(logits, axis=-1)
    padded = jnp.pad(values, ((width // 2, width // 2), (0, 0)))
    total = jnp.zeros_like(values)
    for offset in range(width):
        total = total + kernel[:, offset:offset + 1] * padded[offset:offset + length]
    return total

def attend_head(queries, key_rows, values, valid_len):
    scale = 1.0 / math.sqrt(queries.shape[1])
    scores = low_back(matmul(queries, key_rows.T) * scale)
    allowed = jnp.arange(key_rows.shape[0])[None, :] < valid_len
    scores = jnp.where(allowed, scores, -1e+30)
    probs = jax.nn.softmax(scores, axis=-1)
    return matmul(low(probs), values)

def sequence_loss(table_low, units_low, params, taps, item):
    ids, split_at, valid_len, positions, labels, sop_label = item
    word_rows = table_low[ids]
    embedded = embed_rows(word_rows[None], params, split_at[None])[0]
    low_in = low(embedded)
    queries = both_ways(matmul(low_in, units_low[0].T))
    key_rows = both_ways(matmul(low_in, units_low[1].T))
    values = both_ways(matmul(low_in, units_low[2].T))
    per_shard = HEADS // N_MP
    outputs = []
    conv_count = 0
    for head in range(HEADS):
        cols = slice(head * DH, (head + 1) * DH)
        if head % per_shard < per_shard - head // per_shard:
            outputs.append(attend_head(queries[:, cols], key_rows[:, cols], values[:, cols], valid_len))
        else:
            taps_head = taps[:, conv_count * DH:(conv_count + 1) * DH]
            outputs.append(conv_head(queries[:, cols], key_rows[:, cols], values[:, cols], taps_head))
            conv_count += 1
    mixed = both_ways(jnp.concatenate(outputs, axis=1))
    projected = both_ways(matmul(mixed, units_low[3].T))
    attended = layer_norm(embedded + projected, params[1], params[4])
    low_mid = low(attended)
    part = D // N_MP
    ffn_sum = jnp.zeros_like(attended)
    for shard_index in range(N_MP):
        group = shard_index // 2
        rows = slice(shard_index * part, (shard_index + 1) * part)
        cols = slice(2 * part * group, 2 * part * (group + 1))
        weight_in = jnp.concatenate([units_low[4][rows], units_low[5][rows]], axis=0)
        weight_out = jnp.concatenate([units_low[6][rows], units_low[7][rows]], axis=0)
        hidden_pre = low_back(matmul(low_mid[:, cols], weight_in))
        hidden = low(jax.nn.gelu(hidden_pre, approximate=False))
        ffn_sum = ffn_sum.at[:, cols].add(matmul(hidden, weight_out.T))
    ffn_out = low_back(ffn_sum)
    final_rows = layer_norm(attended + ffn_out, params[2], params[5])
    picked = low(final_rows[positions])
    logits = low_back(matmul(picked, table_low.T))
    chosen = jnp.take_along_axis(logits, labels[:, None], axis=1)[:, 0]
    mlm_sum = jnp.sum(jax.nn.logsumexp(logits, axis=-1) - chosen)
    sop_logits = matmul(final_rows[0:1], params[LEN + 8:LEN + 10].T)[0]
    sop_term = jax.nn.logsumexp(sop_logits) - sop_logits[sop_label]
    return mlm_sum / (SEQS * P_SIZE) + sop_term / SEQS

def forward(table, units, params, taps, items):
    table_low = low(table)
    units_low = low(units)

    def step_fn(total, item):
        return (total + sequence_loss(table_low, units_low, params, taps, item), None)
    total, _ = lax.scan(jax.checkpoint(step_fn), jnp.zeros((), jnp.float32), items)
    return total

def slot_table(owner):
    count = owner.shape[0]
    earlier = jnp.arange(count)[:, None] > jnp.arange(count)[None, :]
    slot_rank = lax.optimization_barrier(jnp.sum(jnp.logical_and(earlier, owner[:, None] == owner[None, :]), axis=1)).astype(jnp.int32)
    slot_index = owner * CAP + slot_rank
    return (jnp.arange(SLOTS)[:, None] == slot_index[None, :]).astype(jnp.float32)

def adam(weight, first, second, grad, count):
    first_new = beta_one * first + (1.0 - beta_one) * grad
    second_new = beta_two * second + (1.0 - beta_two) * grad * grad
    corr_one = 1.0 - jnp.power(beta_one, count)
    corr_two = 1.0 - jnp.power(beta_two, count)
    step = first_new / corr_one / (jnp.sqrt(second_new / corr_two) + adam_eps)
    return (weight - learn_rate * (step + weight_decay * weight), first_new, second_new)

def reference(token_ids, seg_split, lengths, mlm_pos, mlm_labels, sop_labels, owner, step_count, table, table_m, table_v, unit_master, unit_m, unit_v, small, small_m, small_v, taps, taps_m, taps_v):
    selector = slot_table(owner)
    units = jnp.einsum('sk,sij->kij', selector, unit_master, precision=highest)
    items = (token_ids, seg_split, lengths, mlm_pos, mlm_labels, sop_labels)

    def loss_of(table_arg, units_arg, small_arg, taps_arg):
        return forward(table_arg, units_arg, small_arg, taps_arg, items)
    loss, pullback = jax.vjp(loss_of, table, units, small, taps)
    grad_table, grad_units, grad_small, grad_taps = pullback(jnp.ones((), jnp.float32))
    square = jnp.sum(grad_table * grad_table) + jnp.sum(grad_units * grad_units) + jnp.sum(grad_small * grad_small) + jnp.sum(grad_taps * grad_taps)
    grad_norm = jnp.sqrt(square)
    scale = clip_bound / jnp.maximum(grad_norm, clip_bound)
    count = step_count[0].astype(jnp.float32)
    table_new, table_m_new, table_v_new = adam(table, table_m, table_v, grad_table * scale, count)
    grad_slots = jnp.einsum('sk,kij->sij', selector, grad_units, precision=highest)
    used = lax.optimization_barrier(jnp.sum(selector, axis=1))[:, None, None]
    unit_new, unit_m_new, unit_v_new = adam(unit_master, unit_m, unit_v, grad_slots * scale, count)
    unit_new = unit_new * used
    unit_m_new = unit_m_new * used
    unit_v_new = unit_v_new * used
    small_new, small_m_new, small_v_new = adam(small, small_m, small_v, grad_small * scale, count)
    taps_new, taps_m_new, taps_v_new = adam(taps, taps_m, taps_v, grad_taps * scale, count)
    return (loss, grad_norm, table_new, table_m_new, table_v_new, table_new.astype(jnp.bfloat16), unit_new, unit_m_new, unit_v_new, unit_new.astype(jnp.bfloat16), small_new, small_m_new, small_v_new, taps_new, taps_m_new, taps_v_new)
```

```python
import math
from functools import partial

import jax
import jax.numpy as jnp
from jax import lax
from jax.sharding import Mesh, PartitionSpec as P

DH = 64
HEADS = 12
PER = 3
ATTN = tuple(h for h in range(HEADS) if h % PER < PER - h // PER)
CONV = tuple(h for h in range(HEADS) if h % PER >= PER - h // PER)

DP = ("dh", "dl")
MP = ("mh", "ml")
ALL = DP + MP
VG = ("dl", "mh", "ml")
RG = ("dh",)

f32 = jnp.float32
bf16 = jnp.bfloat16
i32 = jnp.int32
highest = lax.Precision.HIGHEST
beta_one = 0.9
beta_two = 0.999
adam_eps = 1e-08
learn_rate = 0.03
weight_decay = 0.01
clip_bound = 0.02
norm_eps = 1e-06


def dot_right(left, right):
    return lax.dot_general(left, right, (((1,), (1,)), ((), ())), preferred_element_type=f32)


def dot_left(left, right):
    return lax.dot_general(left, right, (((0,), (0,)), ((), ())), preferred_element_type=f32)


def dot_plain(left, right):
    return lax.dot_general(left, right, (((1,), (0,)), ((), ())), preferred_element_type=f32)


def halves(x):
    high = lax.reduce_precision(x, 8, 7)
    return high.astype(bf16), (x - high).astype(bf16)


def select_sum(chosen, values):
    high, low = halves(values)
    return dot_left(chosen, high) + dot_left(chosen, low)


def layer_norm(stream, gain, offset):
    center = jnp.mean(stream, axis=-1, keepdims=True)
    shifted = stream - center
    spread = jnp.mean(shifted * shifted, axis=-1, keepdims=True)
    return shifted * lax.rsqrt(spread + norm_eps) * gain + offset


def norm_piece(stream, params, index):
    return layer_norm(stream, params[index], params[index + 3])


def embed_rows(word_rows, params, split_at):
    length = word_rows.shape[-2]
    second = (jnp.arange(length)[None, :] > split_at[:, None]).astype(f32)[..., None]
    summed = (
        word_rows
        + params[6 : 6 + length]
        + params[6 + length] * (1.0 - second)
        + params[7 + length] * second
    )
    return layer_norm(summed, params[0], params[3])


def conv_heads(queries, key_rows, values, taps):
    length = queries.shape[1]
    width = taps.shape[1]
    logits = jnp.einsum("bthd,hod->btho", queries * key_rows, taps, precision=highest)
    kernel = jax.nn.softmax(logits, axis=-1)
    half = width // 2
    padded = jnp.pad(values, ((0, 0), (half, half), (0, 0), (0, 0)))
    total = jnp.zeros_like(values)
    for offset in range(width):
        total = total + kernel[..., offset : offset + 1] * padded[:, offset : offset + length]
    return total


def exact_gelu(values):
    return jax.nn.gelu(values, approximate=False)


def sop_loss(cls_rows, params, labels, denom, length):
    logits = jnp.dot(cls_rows, params[length + 8 : length + 10].T, precision=highest)
    chosen = jnp.take_along_axis(logits, labels[:, None], axis=1)[:, 0]
    return jnp.sum(jax.nn.logsumexp(logits, axis=-1) - chosen) / denom


def adam(weight, first, second, grad, count):
    first_new = beta_one * first + (1.0 - beta_one) * grad
    second_new = beta_two * second + (1.0 - beta_two) * grad * grad
    corr_one = 1.0 - jnp.power(beta_one, count)
    corr_two = 1.0 - jnp.power(beta_two, count)
    step = first_new / corr_one / (jnp.sqrt(second_new / corr_two) + adam_eps)
    return (weight - learn_rate * (step + weight_decay * weight), first_new, second_new)


def everyone(x, axes):
    count = lax.axis_size(axes)
    return lax.all_to_all(jnp.broadcast_to(x, (count,) + x.shape), axes, 0, 0, tiled=True)


def pick_heads(x, heads):
    return jnp.stack([x[:, :, h * DH : (h + 1) * DH] for h in heads], axis=2)


def attention_scores(queries, key_rows, lengths):
    scores = jnp.einsum("bqhd,bkhd->bhqk", queries, key_rows, preferred_element_type=f32)
    allowed = jnp.arange(key_rows.shape[1])[None, :] < lengths[:, None]
    return jnp.where(allowed[:, None, None, :], scores / math.sqrt(DH), -1e30)


def slots_of(ids, vblock, devices):
    owner = ids // vblock
    here = jnp.arange(ids.shape[0])
    same = ids[None, :] == ids[:, None]
    first = jnp.sum(jnp.logical_and(same, here[None, :] < here[:, None]), axis=1) == 0
    below = jnp.logical_and(owner[None, :] == owner[:, None], ids[None, :] < ids[:, None])
    rank = jnp.sum(jnp.logical_and(below, first[None, :]), axis=1).astype(i32)
    return owner, first, rank


def fetch_round(turn, capacity, devices, owner, first, rank, local, low_table):
    slot = jnp.where(rank // capacity == turn, owner * capacity + rank % capacity, -1)
    seats = jnp.arange(devices * capacity)
    chosen = jnp.logical_and(seats[:, None] == slot[None, :], first[None, :])
    request = jnp.sum(jnp.where(chosen, local[None, :] + 1, 0), axis=1) - 1
    message = jnp.full((devices, 128), jnp.max(rank), i32)
    message = message.at[:, :capacity].set(request.reshape(devices, capacity))
    got = lax.all_to_all(message, ALL, 0, 0, tiled=True)
    asked = got[:, :capacity].reshape(-1)
    served = (asked[:, None] == jnp.arange(low_table.shape[0])[None, :]).astype(bf16)
    rows = dot_plain(served, low_table).astype(bf16)
    rows = lax.all_to_all(rows, ALL, 0, 0, tiled=True)
    mine = (slot[:, None] == seats[None, :]).astype(bf16)
    return dot_plain(mine, rows), mine, served, jnp.max(got[:, capacity])


def return_round(mine, served, grad_word):
    sent = select_sum(mine, grad_word)
    got = lax.all_to_all(sent, ALL, 0, 0, tiled=True)
    return select_sum(served, got)


def body(
    token_ids,
    seg_split,
    lengths,
    mlm_pos,
    mlm_labels,
    sop_labels,
    owner,
    step_count,
    table,
    table_m,
    table_v,
    unit_master,
    unit_m,
    unit_v,
    small,
    small_m,
    small_v,
    taps,
    taps_m,
    taps_v,
):
    mp_count = lax.axis_size(MP)
    dp_count = lax.axis_size(DP)
    devices = mp_count * dp_count
    mp_index = lax.axis_index(MP)
    dp_index = lax.axis_index(DP)
    group_seqs, length = token_ids.shape
    width = small.shape[1]
    part = unit_master.shape[1]
    vblock = table.shape[0]
    cap_slots = unit_master.shape[0]
    matrices = owner.shape[0]
    seqs = group_seqs // mp_count
    tokens = seqs * length
    masks = mlm_pos.shape[1]
    total_seqs = group_seqs * dp_count
    count_all = total_seqs * masks

    def my(x):
        return lax.dynamic_slice_in_dim(x, mp_index * seqs, seqs, 0)

    token_ids, seg_split, lengths = my(token_ids), my(seg_split), my(lengths)
    mlm_pos, mlm_labels, sop_labels = my(mlm_pos), my(mlm_labels), my(sop_labels)

    earlier = jnp.arange(matrices)[:, None] > jnp.arange(matrices)[None, :]
    slot_rank = jnp.sum(jnp.logical_and(earlier, owner[:, None] == owner[None, :]), axis=1)
    slot_index = owner * cap_slots + slot_rank
    selector = jnp.logical_and(
        owner[None, :] == dp_index, slot_rank[None, :] == jnp.arange(cap_slots)[:, None]
    ).astype(f32)
    all_slots = lax.all_gather(unit_master.astype(bf16), DP, axis=0, tiled=True)
    picked = jnp.stack(
        [lax.dynamic_index_in_dim(all_slots, slot_index[k], 0, False) for k in range(matrices)]
    )
    gathered = lax.all_gather(picked, MP, axis=0)
    units = [gathered[:, k].reshape(mp_count * part, width) for k in range(matrices)]
    low_table = table.astype(bf16)
    vocab = lax.all_gather(low_table, RG, axis=0, tiled=True)

    ids = token_ids.reshape(-1)
    capacity = max(8, -(-1280 // devices))
    home, first, rank = slots_of(ids, vblock, devices)
    local = ids % vblock
    fetch = partial(
        fetch_round,
        capacity=capacity,
        devices=devices,
        owner=home,
        first=first,
        rank=rank,
        local=local,
        low_table=low_table,
    )
    word_rows, mine, served, top_rank = fetch(0)
    turns = top_rank // capacity + 1

    def more(state):
        return state[0] < turns

    def fetch_more(state):
        return (state[0] + 1, state[1] + fetch(state[0])[0])

    _, word_rows = lax.while_loop(more, fetch_more, (jnp.int32(1), word_rows))

    embedded, embed_pull = jax.vjp(
        partial(embed_rows, split_at=seg_split), word_rows.reshape(seqs, length, width), small
    )
    embedded = embedded.reshape(tokens, width)
    low_in = embedded.astype(bf16)
    qkv = [dot_right(low_in, units[k]).astype(bf16).reshape(seqs, length, width) for k in range(3)]
    qa, ka, va = [pick_heads(x, ATTN) for x in qkv]
    qc, kc, vc = [pick_heads(x, CONV).astype(f32) for x in qkv]
    scores = attention_scores(qa, ka, lengths)
    probs = jax.nn.softmax(scores, axis=-1)
    low_probs = probs.astype(bf16)
    out_a = jnp.einsum("bhqk,bkhd->bqhd", low_probs, va, preferred_element_type=f32)
    taps_heads = jnp.moveaxis(taps.reshape(taps.shape[0], len(CONV), DH), 1, 0)
    out_c, conv_pull = jax.vjp(conv_heads, qc, kc, vc, taps_heads)
    pieces = [None] * HEADS
    for at, head in enumerate(ATTN):
        pieces[head] = out_a[:, :, at]
    for at, head in enumerate(CONV):
        pieces[head] = out_c[:, :, at]
    heads = jnp.concatenate(pieces, axis=-1).reshape(tokens, width).astype(bf16)
    projected = dot_right(heads, units[3]).astype(bf16).astype(f32)
    attended, norm_one_pull = jax.vjp(partial(norm_piece, index=1), embedded + projected, small)
    low_mid = attended.astype(bf16)
    hidden_pre, ffn = [], []
    w_in, w_out, hidden, gelu_pull = [], [], [], []
    for s in range(mp_count):
        rows = slice(s * part, (s + 1) * part)
        w_in.append(jnp.concatenate([units[4][rows], units[5][rows]], axis=0))
        w_out.append(jnp.concatenate([units[6][rows], units[7][rows]], axis=0))
        g = s // 2
        low_group = low_mid[:, 2 * part * g : 2 * part * (g + 1)]
        pre = dot_plain(low_group, w_in[s])
        act, pull = jax.vjp(exact_gelu, pre)
        hidden.append(act.astype(bf16))
        gelu_pull.append(pull)
        ffn.append(dot_right(hidden[s], w_out[s]))
    ffn_out = jnp.concatenate([ffn[0] + ffn[1], ffn[2] + ffn[3]], axis=1)
    final_rows, norm_two_pull = jax.vjp(partial(norm_piece, index=2), attended + ffn_out, small)

    positions = (jnp.arange(seqs)[:, None] * length + mlm_pos).reshape(-1)
    at_mask = (positions[:, None] == jnp.arange(tokens)[None, :]).astype(bf16)
    masked_rows = dot_plain(at_mask, final_rows.astype(bf16)).astype(bf16)
    all_masked = lax.all_gather(masked_rows, VG, axis=0, tiled=True)
    all_labels = everyone(mlm_labels.reshape(-1), VG).reshape(-1)
    logits = dot_right(all_masked, vocab)
    copies = lax.axis_size(RG)
    group_count = lax.axis_size(VG)
    block = all_labels // vblock
    label_mine = block % group_count == lax.axis_index(VG)
    label_row = block // group_count * vblock + all_labels % vblock
    onehot = jnp.logical_and(
        jnp.arange(copies * vblock)[None, :] == label_row[:, None], label_mine[:, None]
    )
    top = jnp.max(logits, axis=1)
    total = jnp.sum(jnp.exp(logits - top[:, None]), axis=1)
    target = jnp.sum(jnp.where(onehot, logits, 0.0), axis=1)
    stats = everyone(jnp.stack([top, total, target]), VG)
    top_all = jnp.max(stats[:, 0], axis=0)
    total_all = jnp.sum(stats[:, 1] * jnp.exp(stats[:, 0] - top_all), axis=0)
    log_sum = top_all + jnp.log(total_all)
    mlm_part = jnp.sum(log_sum - jnp.sum(stats[:, 2], axis=0)) / count_all / group_count
    grad_logits = (
        (jnp.exp(logits - log_sum[:, None]) - onehot.astype(f32)) / count_all
    ).astype(bf16)
    grad_masked = lax.psum_scatter(
        dot_plain(grad_logits, vocab), VG, scatter_dimension=0, tiled=True
    )
    grad_table = lax.psum_scatter(
        dot_left(grad_logits, all_masked), RG, scatter_dimension=0, tiled=True
    )
    cls_index = jnp.arange(seqs) * length
    sop_part, sop_pull = jax.vjp(
        partial(sop_loss, labels=sop_labels, denom=total_seqs, length=length),
        final_rows[cls_index],
        small,
    )
    grad_cls, grad_small_sop = sop_pull(jnp.ones((), f32))
    grad_final = select_sum(at_mask, grad_masked).reshape(seqs, length, width)
    grad_final = jnp.concatenate(
        [grad_final[:, :1] + grad_cls[:, None], grad_final[:, 1:]], axis=1
    ).reshape(tokens, width)

    grad_sum_two, grad_small_two = norm_two_pull(grad_final)
    grad_ffn = grad_sum_two.astype(bf16)
    grad_in, grad_in_w, grad_out_w = [], [], []
    for s in range(mp_count):
        cols = slice(2 * part * (s // 2), 2 * part * (s // 2 + 1))
        grad_group = grad_ffn[:, cols]
        grad_hidden = dot_plain(grad_group, w_out[s])
        grad_out_w.append(dot_left(grad_group, hidden[s]))
        grad_pre = gelu_pull[s](grad_hidden)[0].astype(bf16)
        grad_in_w.append(dot_left(low_mid[:, cols], grad_pre))
        grad_in.append(dot_right(grad_pre, w_in[s]))
    grad_attended = grad_sum_two + jnp.concatenate(
        [grad_in[0] + grad_in[1], grad_in[2] + grad_in[3]], axis=1
    )
    grad_sum_one, grad_small_one = norm_one_pull(grad_attended)
    grad_proj = grad_sum_one.astype(bf16)
    grad_proj_w = dot_left(grad_proj, heads)
    grad_heads = dot_plain(grad_proj, units[3]).astype(bf16).reshape(seqs, length, width)
    ga = pick_heads(grad_heads, ATTN)
    gc = pick_heads(grad_heads, CONV).astype(f32)
    grad_probs = jnp.einsum("bqhd,bkhd->bhqk", ga, va, preferred_element_type=f32)
    grad_scores = (
        probs * (grad_probs - jnp.sum(probs * grad_probs, axis=-1, keepdims=True))
    ).astype(bf16)
    scale = 1.0 / math.sqrt(DH)
    dqa = jnp.einsum("bhqk,bkhd->bqhd", grad_scores, ka, preferred_element_type=f32) * scale
    dka = jnp.einsum("bhqk,bqhd->bkhd", grad_scores, qa, preferred_element_type=f32) * scale
    dva = jnp.einsum("bhqk,bqhd->bkhd", low_probs, ga, preferred_element_type=f32)
    dqc, dkc, dvc, grad_taps = conv_pull(gc)
    grad_taps = jnp.moveaxis(grad_taps, 0, 1).reshape(taps.shape)
    grad_qkv = []
    for attn_part, conv_part in ((dqa, dqc), (dka, dkc), (dva, dvc)):
        pieces = [None] * HEADS
        for at, head in enumerate(ATTN):
            pieces[head] = attn_part[:, :, at]
        for at, head in enumerate(CONV):
            pieces[head] = conv_part[:, :, at]
        grad_qkv.append(jnp.concatenate(pieces, axis=-1).reshape(tokens, width).astype(bf16))
    grad_qkv_w = [dot_left(g, low_in) for g in grad_qkv]
    grad_embedded = grad_sum_one + sum(dot_plain(grad_qkv[k], units[k]) for k in range(3))
    grad_word, grad_small_zero = embed_pull(grad_embedded.reshape(seqs, length, width))
    grad_word = grad_word.reshape(tokens, width)

    words = return_round(mine, served, grad_word)

    def return_more(state):
        _, mine_r, served_r, _ = fetch(state[0])
        return (state[0] + 1, state[1] + return_round(mine_r, served_r, grad_word))

    _, words = lax.while_loop(more, return_more, (jnp.int32(1), words))
    grad_table_own = grad_table + words

    def stack_parts(pieces):
        return jnp.stack([p.reshape(mp_count, part, width) for p in pieces], axis=1)

    in_w = jnp.stack([g.reshape(2, part, width) for g in grad_in_w])
    out_w = jnp.stack([g.reshape(2, part, width) for g in grad_out_w])
    grad_units = jnp.concatenate(
        [stack_parts(grad_qkv_w + [grad_proj_w]), in_w, out_w], axis=1
    ).reshape(mp_count * matrices * part, width)
    units_part = lax.psum_scatter(grad_units, MP, scatter_dimension=0, tiled=True)
    units_part = units_part.reshape(matrices, part * width)
    seat = (slot_index[None, :] == jnp.arange(dp_count * cap_slots)[:, None]).astype(f32)
    slotted = sum(seat[:, k, None] * units_part[k][None, :] for k in range(matrices))
    grad_slots = lax.psum_scatter(
        slotted.reshape(dp_count * cap_slots, part, width), DP, scatter_dimension=0, tiled=True
    )
    grad_small = grad_small_zero + grad_small_one + grad_small_two + grad_small_sop
    small_sum, taps_sum, loss = lax.psum((grad_small, grad_taps, mlm_part + sop_part), ALL)
    square = (
        jnp.sum(grad_table_own * grad_table_own)
        + jnp.sum(grad_slots * grad_slots)
        + (jnp.sum(taps_sum * taps_sum) + jnp.sum(small_sum * small_sum)) / devices
    )
    squares = everyone(jnp.full((128,), square, f32), ALL)
    grad_norm = jnp.sqrt(jnp.sum(squares[:, 0]))
    scale = clip_bound / jnp.maximum(grad_norm, clip_bound)
    count = step_count[0].astype(f32)
    table_new, table_m_new, table_v_new = adam(
        table, table_m, table_v, grad_table_own * scale, count
    )
    used = jnp.sum(selector, axis=1)[:, None, None]
    unit_new, unit_m_new, unit_v_new = adam(unit_master, unit_m, unit_v, grad_slots * scale, count)
    unit_new = unit_new * used
    unit_m_new = unit_m_new * used
    unit_v_new = unit_v_new * used
    small_new, small_m_new, small_v_new = adam(small, small_m, small_v, small_sum * scale, count)
    taps_new, taps_m_new, taps_v_new = adam(taps, taps_m, taps_v, taps_sum * scale, count)
    return (
        loss,
        grad_norm,
        table_new,
        table_m_new,
        table_v_new,
        table_new.astype(bf16),
        unit_new,
        unit_m_new,
        unit_v_new,
        unit_new.astype(bf16),
        small_new,
        small_m_new,
        small_v_new,
        taps_new,
        taps_m_new,
        taps_v_new,
    )


def solution(mesh):
    dp, mp = mesh.devices.shape
    fine = Mesh(mesh.devices.reshape(dp // 2, 2, mp // 2, 2), ALL)
    rows = P(DP)
    vocab = P(ALL)
    slots = P(DP, MP)
    placed = (rows,) * 6 + (P(),) * 2 + (vocab,) * 3 + (slots,) * 3 + (P(),) * 6
    return jax.shard_map(
        body,
        mesh=fine,
        in_specs=placed,
        out_specs=(P(),) * 2 + (vocab,) * 4 + (slots,) * 4 + (P(),) * 6,
        check_vma=False,
    )
```

```python
import math
from functools import partial

import jax
import jax.numpy as jnp
from jax import lax
from jax.experimental import pallas as pl
from jax.experimental.pallas import tpu as pltpu
from jax.sharding import Mesh, PartitionSpec as P

DH = 64
HEADS = 12
PER = 3
ATTN = tuple(h for h in range(HEADS) if h % PER < PER - h // PER)
CONV = tuple(h for h in range(HEADS) if h % PER >= PER - h // PER)

FIRST = min(CONV) // 2 * 2

DP = ("dh", "dl")
MP = ("mh", "ml")
ALL = DP + MP
VG = ("dh", "mh")
RG = ("dl", "ml")
CHIPS = ("dh", "dl", "mh")

f32 = jnp.float32
bf16 = jnp.bfloat16
i32 = jnp.int32
highest = lax.Precision.HIGHEST
beta_one = 0.9
beta_two = 0.999
adam_eps = 1e-08
learn_rate = 0.03
weight_decay = 0.01
clip_bound = 0.02
norm_eps = 1e-06
VMEM = 60 << 20


def dot_right(left, right):
    return lax.dot_general(left, right, (((1,), (1,)), ((), ())), preferred_element_type=f32)


def dot_left(left, right):
    return lax.dot_general(left, right, (((0,), (0,)), ((), ())), preferred_element_type=f32)


def dot_plain(left, right):
    return lax.dot_general(left, right, (((1,), (0,)), ((), ())), preferred_element_type=f32)


def halves(x):
    high = lax.reduce_precision(x, 8, 7)
    return high.astype(bf16), (x - high).astype(bf16)


def select_sum(chosen, values):
    high, low = halves(values)
    return dot_left(chosen, high) + dot_left(chosen, low)


def sop_loss(cls_rows, params, labels, denom, length):
    logits = jnp.dot(cls_rows, params[length + 8 : length + 10].T, precision=highest)
    chosen = jnp.take_along_axis(logits, labels[:, None], axis=1)[:, 0]
    return jnp.sum(jax.nn.logsumexp(logits, axis=-1) - chosen) / denom


def adam(weight, first, second, grad, count):
    first_new = beta_one * first + (1.0 - beta_one) * grad
    second_new = beta_two * second + (1.0 - beta_two) * grad * grad
    corr_one = 1.0 - jnp.power(beta_one, count)
    corr_two = 1.0 - jnp.power(beta_two, count)
    step = first_new / corr_one / (jnp.sqrt(second_new / corr_two) + adam_eps)
    return (weight - learn_rate * (step + weight_decay * weight), first_new, second_new)


def everyone(x, axes):
    count = lax.axis_size(axes)
    return lax.all_to_all(jnp.broadcast_to(x, (count,) + x.shape), axes, 0, 0, tiled=True)


def swap(x, axis, bit):
    count = lax.axis_size(axis)
    return lax.ppermute(x, axis, [(i, i ^ (1 << bit)) for i in range(count)])


def bits_of(axis):
    return lax.axis_size(axis).bit_length() - 1


def fold(x, axis, bit, dim):
    me = (lax.axis_index(axis) >> bit) & 1
    sent = lax.dynamic_index_in_dim(x, 1 - me, dim, False)
    kept = lax.dynamic_index_in_dim(x, me, dim, False)
    return kept + swap(sent, axis, bit)


def grow(x, axis):
    for bit in range(bits_of(axis)):
        x = jnp.concatenate([x, swap(x, axis, bit)], axis=0)
    return x


def shrink(x, axis):
    for bit in reversed(range(bits_of(axis))):
        half = x.shape[0] // 2
        x = x[:half] + swap(x[half:], axis, bit)
    return x


def relative(x, index):
    for bit in range(x.shape[0].bit_length() - 1):
        y = x.reshape((x.shape[0] >> (bit + 1), 2, 1 << bit) + x.shape[1:])
        x = jnp.where((index >> bit) & 1 == 1, y[:, ::-1], y).reshape(x.shape)
    return x


def rows_norm(x):
    center = jnp.mean(x, axis=-1, keepdims=True)
    shifted = x - center
    inv = lax.rsqrt(jnp.mean(shifted * shifted, axis=-1, keepdims=True) + norm_eps)
    return shifted * inv, inv


def erf(x):
    x = jnp.clip(x, -3.832506856900711, 3.832506856900711)
    y = x * x
    top = jnp.float32(0.00022905065861350646)
    for c in (0.0034082910107109506, 0.050955695062380861, 0.18520832239976145, 1.128379143519084):
        top = top * y + c
    low = jnp.float32(-1.1791602954361697e-7)
    for c in (
        0.000023547966471313185,
        0.0010179625278914885,
        0.014070470171167667,
        0.11098505178285362,
        0.49746925110067538,
        1.0,
    ):
        low = low * y + c
    return x * top / low


def head_mask(rows, groups):
    row = lax.broadcasted_iota(i32, (rows, groups * DH), 0)
    col = lax.broadcasted_iota(i32, (rows, groups * DH), 1)
    return lax.rem(row, groups) == lax.div(col, DH)


def split3(x):
    a = x.astype(bf16)
    r = x - a.astype(f32)
    b = r.astype(bf16)
    c = (r - b.astype(f32)).astype(bf16)
    return a, b, c


def dot_exact(a, b, dims):
    return lax.dot_general(a, b, (dims, ((), ())), precision=highest, preferred_element_type=f32)


def conv_kernel_rows(prod, taps_ref, groups):
    width = taps_ref.shape[0]
    spread = jnp.concatenate(
        [jnp.broadcast_to(taps_ref[o : o + 1, :], (groups, prod.shape[1])) for o in range(width)], axis=0
    )
    spread = jnp.where(head_mask(width * groups, groups), spread, 0.0)
    logits = dot_exact(spread, prod, ((1,), (1,)))
    parts = [logits[o * groups : (o + 1) * groups] for o in range(width)]
    top = parts[0]
    for p in parts[1:]:
        top = jnp.maximum(top, p)
    weights = [jnp.exp(p - top) for p in parts]
    total = weights[0]
    for w in weights[1:]:
        total = total + w
    inv = 1.0 / total
    return [w * inv for w in weights], spread


def spread_rows(rows, groups):
    three = jnp.concatenate(split3(rows), axis=0)
    ones = head_mask(3 * groups, groups).astype(bf16)
    return lax.dot_general(three, ones, (((0,), (0,)), ((), ())), preferred_element_type=f32)


def forward_heads(
    split_ref, length_ref, word_ref, places_ref, edge_ref, taps_ref, units_ref,
    emb_ref, qkv_ref, lse_ref, heads_ref, pad_ref,
):
    at = pl.program_id(0)
    length, width = word_ref.shape[1:]
    later = lax.broadcasted_iota(i32, (length, 1), 0) > split_ref[at]
    summed = word_ref[0].astype(f32) + places_ref[...]
    summed = summed + jnp.where(later, edge_ref[7:8, :], edge_ref[6:7, :])
    normed, _ = rows_norm(summed)
    embedded = normed * edge_ref[0:1, :] + edge_ref[3:4, :]
    emb_ref[0] = embedded
    low_in = embedded.astype(bf16)
    part = units_ref.shape[2]
    for k in range(3):
        unit = units_ref[:, k].reshape(width, width)
        qkv_ref[0, :, k * width : (k + 1) * width] = dot_right(low_in, unit).astype(bf16)
    allowed = lax.broadcasted_iota(i32, (length, length), 1) < length_ref[at]
    lanes = lax.broadcasted_iota(i32, (length, 128), 1)
    lse = jnp.zeros((length, 128), f32)
    outs = {}
    for n, h in enumerate(ATTN):
        q = qkv_ref[0, :, h * DH : (h + 1) * DH]
        k = qkv_ref[0, :, width + h * DH : width + (h + 1) * DH]
        v = qkv_ref[0, :, 2 * width + h * DH : 2 * width + (h + 1) * DH]
        scores = jnp.where(allowed, dot_right(q, k) * (1.0 / math.sqrt(DH)), -1e30)
        top = jnp.max(scores, axis=1, keepdims=True)
        weights = jnp.exp(scores - top)
        total = jnp.sum(weights, axis=1, keepdims=True)
        probs = (weights * (1.0 / total)).astype(bf16)
        outs[h] = dot_plain(probs, v).astype(bf16)
        lse = jnp.where(lanes == n, top + jnp.log(total), lse)
    lse_ref[0] = lse
    groups = HEADS - FIRST
    base = FIRST * DH
    q = qkv_ref[0, :, base:width].astype(f32)
    k = qkv_ref[0, :, width + base : 2 * width].astype(f32)
    kernel, _ = conv_kernel_rows(q * k, taps_ref, groups)
    taps = len(kernel)
    pad_ref[0:8, :] = jnp.zeros((8, width - base), f32)
    pad_ref[8 + length : 16 + length, :] = jnp.zeros((8, width - base), f32)
    pad_ref[8 : 8 + length, :] = qkv_ref[0, :, 2 * width + base :].astype(f32)
    total = jnp.zeros((length, width - base), f32)
    for o in range(taps):
        start = 8 + o - taps // 2
        total = total + spread_rows(kernel[o], groups) * pad_ref[start : start + length, :]
    total = total.astype(bf16)
    for h in CONV:
        outs[h] = total[:, (h - FIRST) * DH : (h - FIRST + 1) * DH]
    heads_ref[0] = jnp.concatenate([outs[h] for h in range(HEADS)], axis=1)


def ffn_weights(units_ref, s, first):
    return jnp.concatenate([units_ref[s, first], units_ref[s, first + 1]], axis=0)


def forward_ffn(
    pos_ref, heads_ref, emb_ref, edge_ref, units_ref, one_ref, two_ref, mask_ref, cls_ref
):
    length, width = emb_ref.shape[1:]
    mp_count, part = units_ref.shape[0], units_ref.shape[2]
    unit = units_ref[:, 0].reshape(width, width)
    projected = dot_right(heads_ref[0], unit).astype(bf16).astype(f32)
    one = emb_ref[0] + projected
    one_ref[0] = one
    normed, _ = rows_norm(one)
    attended = normed * edge_ref[1:2, :] + edge_ref[4:5, :]
    low_mid = attended.astype(bf16)
    for g in range(2):
        cols = slice(2 * part * g, 2 * part * (g + 1))
        total = None
        for s in (2 * g, 2 * g + 1):
            pre = dot_plain(low_mid[:, cols], ffn_weights(units_ref, s, 1))
            hidden = (pre * (0.5 + 0.5 * erf(pre * math.sqrt(0.5)))).astype(bf16)
            out = dot_right(hidden, ffn_weights(units_ref, s, 3))
            total = out if total is None else total + out
        two_ref[0, :, cols] = attended[:, cols] + total
    normed, _ = rows_norm(two_ref[0])
    final = normed * edge_ref[2:3, :] + edge_ref[5:6, :]
    masks = mask_ref.shape[1]
    picked = lax.broadcasted_iota(i32, (masks, length), 1) == pos_ref[0][:, 0:1]
    mask_ref[0] = dot_plain(picked.astype(bf16), final.astype(bf16)).astype(bf16)
    cls_ref[0] = final[0:8]


def norm_grad(grad, normed, inv, gain):
    scaled = grad * gain
    mean = jnp.mean(scaled, axis=-1, keepdims=True)
    along = jnp.mean(scaled * normed, axis=-1, keepdims=True)
    return inv * (scaled - mean - normed * along)


def down(x):
    return jnp.sum(x, axis=0, keepdims=True)


def backward_ffn(
    pos_ref, grad_ref, cls_ref, one_ref, two_ref, heads_ref, edge_ref, units_ref,
    sum_ref, back_ref, wide_ref, edges_ref,
):
    at = pl.program_id(0)
    length, width = one_ref.shape[1:]
    mp_count, part = units_ref.shape[0], units_ref.shape[2]

    @pl.when(at == 0)
    def _():
        wide_ref[...] = jnp.zeros_like(wide_ref)
        edges_ref[...] = jnp.zeros_like(edges_ref)

    masks = grad_ref.shape[1]
    picked = (lax.broadcasted_iota(i32, (masks, length), 1) == pos_ref[0][:, 0:1]).astype(bf16)
    high = grad_ref[0].astype(bf16)
    low = (grad_ref[0] - high.astype(f32)).astype(bf16)
    grad = dot_left(picked, high) + dot_left(picked, low)
    rows = lax.broadcasted_iota(i32, (length, 1), 0)
    grad = grad + jnp.where(rows == 0, cls_ref[0][0:1, :], 0.0)
    normed, inv = rows_norm(two_ref[0])
    edges_ref[2:3, :] += down(grad * normed)
    edges_ref[5:6, :] += down(grad)
    grad_two = norm_grad(grad, normed, inv, edge_ref[2:3, :])
    low_two = grad_two.astype(bf16)
    normed, inv = rows_norm(one_ref[0])
    low_mid = (normed * edge_ref[1:2, :] + edge_ref[4:5, :]).astype(bf16)
    backs = []
    for g in range(2):
        cols = slice(2 * part * g, 2 * part * (g + 1))
        total = None
        for s in (2 * g, 2 * g + 1):
            w_in = ffn_weights(units_ref, s, 1)
            w_out = ffn_weights(units_ref, s, 3)
            pre = dot_plain(low_mid[:, cols], w_in)
            half = 0.5 + 0.5 * erf(pre * math.sqrt(0.5))
            hidden = (pre * half).astype(bf16)
            slope = half + pre * (jnp.exp(-0.5 * pre * pre) * (1.0 / math.sqrt(2.0 * math.pi)))
            grad_hidden = dot_plain(low_two[:, cols], w_out)
            w = dot_left(low_two[:, cols], hidden)
            wide_ref[s, 3] += w[:part]
            wide_ref[s, 4] += w[part:]
            grad_pre = (grad_hidden * slope).astype(bf16)
            w = dot_left(low_mid[:, cols], grad_pre)
            wide_ref[s, 1] += w[:part]
            wide_ref[s, 2] += w[part:]
            back = dot_right(grad_pre, w_in)
            total = back if total is None else total + back
        backs.append(total)
    grad = grad_two + jnp.concatenate(backs, axis=1)
    edges_ref[1:2, :] += down(grad * normed)
    edges_ref[4:5, :] += down(grad)
    grad_one = norm_grad(grad, normed, inv, edge_ref[1:2, :])
    sum_ref[0] = grad_one
    low_one = grad_one.astype(bf16)
    wide_ref[:, 0] += dot_left(low_one, heads_ref[0]).reshape(mp_count, part, width)
    unit = units_ref[:, 0].reshape(width, width)
    back_ref[0] = dot_plain(low_one, unit).astype(bf16)


def backward_heads(
    split_ref, length_ref, word_ref, places_ref, edge_ref, taps_ref, units_ref,
    qkv_ref, lse_ref, back_ref, sum_ref,
    gword_ref, gplaces_ref, gedge_ref, gtaps_ref, wide_ref,
    pad_ref, shift_ref,
):
    at = pl.program_id(0)
    length, width = word_ref.shape[1:]

    @pl.when(at == 0)
    def _():
        wide_ref[...] = jnp.zeros_like(wide_ref)
        gplaces_ref[...] = jnp.zeros_like(gplaces_ref)
        gedge_ref[...] = jnp.zeros_like(gedge_ref)
        gtaps_ref[...] = jnp.zeros_like(gtaps_ref)

    groups = HEADS - FIRST
    base = FIRST * DH
    span = width - base
    q = qkv_ref[0, :, base:width].astype(f32)
    k = qkv_ref[0, :, width + base : 2 * width].astype(f32)
    prod = q * k
    kernel, spread = conv_kernel_rows(prod, taps_ref, groups)
    taps = len(kernel)
    out = back_ref[0, :, base:].astype(f32)
    pad_ref[0:8, :] = jnp.zeros((8, span), f32)
    pad_ref[8 + length : 16 + length, :] = jnp.zeros((8, span), f32)
    pad_ref[8 : 8 + length, :] = qkv_ref[0, :, 2 * width + base :].astype(f32)
    shift_ref[0:8, :] = jnp.zeros((8, span), f32)
    shift_ref[8 + length : 16 + length, :] = jnp.zeros((8, span), f32)
    grad_values = jnp.zeros((length, span), f32)
    lanes = 128
    dots = jnp.zeros((length, lanes), f32)
    column = lax.broadcasted_iota(i32, (span, lanes), 0)
    lane = lax.broadcasted_iota(i32, (span, lanes), 1)
    for o in range(taps):
        start = 8 + o - taps // 2
        moved = out * pad_ref[start : start + length, :]
        high = moved.astype(bf16)
        low = (moved - high.astype(f32)).astype(bf16)
        ones = (lane == o * groups + lax.div(column, DH)).astype(bf16)
        dots = dots + dot_plain(high, ones) + dot_plain(low, ones)
        shift_ref[8 : 8 + length, :] = spread_rows(kernel[o], groups) * out
        back = 8 + taps // 2 - o
        grad_values = grad_values + shift_ref[back : back + length, :]
    dots = dots.T
    parts = [dots[o * groups : (o + 1) * groups] for o in range(taps)]
    along = kernel[0] * parts[0]
    for o in range(1, taps):
        along = along + kernel[o] * parts[o]
    grad_logits = jnp.concatenate([kernel[o] * (parts[o] - along) for o in range(taps)], axis=0)
    grad_prod = dot_exact(grad_logits, spread, ((0,), (0,)))
    grad_taps = dot_exact(grad_logits, prod, ((1,), (0,)))
    grad_taps = jnp.where(head_mask(taps * groups, groups), grad_taps, 0.0)
    for o in range(taps):
        gtaps_ref[o : o + 1, :] += down(grad_taps[o * groups : (o + 1) * groups])
    grads = [(grad_prod * k).astype(bf16), (grad_prod * q).astype(bf16), grad_values.astype(bf16)]
    pieces = [[None] * HEADS for _ in range(3)]
    for h in CONV:
        for n in range(3):
            pieces[n][h] = grads[n][:, (h - FIRST) * DH : (h - FIRST + 1) * DH]

    allowed = lax.broadcasted_iota(i32, (length, length), 1) < length_ref[at]
    scale = 1.0 / math.sqrt(DH)
    for n, h in enumerate(ATTN):
        qh = qkv_ref[0, :, h * DH : (h + 1) * DH]
        kh = qkv_ref[0, :, width + h * DH : width + (h + 1) * DH]
        vh = qkv_ref[0, :, 2 * width + h * DH : 2 * width + (h + 1) * DH]
        gh = back_ref[0, :, h * DH : (h + 1) * DH]
        scores = jnp.where(allowed, dot_right(qh, kh) * scale, -1e30)
        probs = jnp.exp(scores - lse_ref[0][:, n : n + 1])
        grad_probs = dot_right(gh, vh)
        total = jnp.sum(probs * grad_probs, axis=1, keepdims=True)
        grad_scores = (probs * (grad_probs - total)).astype(bf16)
        pieces[0][h] = (dot_plain(grad_scores, kh) * scale).astype(bf16)
        pieces[1][h] = (dot_left(grad_scores, qh) * scale).astype(bf16)
        pieces[2][h] = dot_left(probs.astype(bf16), gh).astype(bf16)
    later = lax.broadcasted_iota(i32, (length, 1), 0) > split_ref[at]
    summed = word_ref[0].astype(f32) + places_ref[...]
    summed = summed + jnp.where(later, edge_ref[7:8, :], edge_ref[6:7, :])
    normed, inv = rows_norm(summed)
    low_in = (normed * edge_ref[0:1, :] + edge_ref[3:4, :]).astype(bf16)
    grad = sum_ref[0]
    for n in range(3):
        g = jnp.concatenate(pieces[n], axis=1)
        wide_ref[:, n] += dot_left(g, low_in).reshape(units_ref.shape[0], -1, width)
        grad = grad + dot_plain(g, units_ref[:, n].reshape(width, width))
    gedge_ref[0:1, :] += down(grad * normed)
    gedge_ref[3:4, :] += down(grad)
    grad = norm_grad(grad, normed, inv, edge_ref[0:1, :])
    gword_ref[0] = grad
    gplaces_ref[...] += grad
    second = down(jnp.where(later, grad, 0.0))
    gedge_ref[6:7, :] += down(grad) - second
    gedge_ref[7:8, :] += second


def whole(shape):
    return pl.BlockSpec(shape, lambda b, *_: (0,) * len(shape))


def fixed(shape):
    return pl.BlockSpec(shape, lambda b, *_: (0,) * len(shape), pipeline_mode=pl.Buffered(1))


def each(shape):
    return pl.BlockSpec((1,) + shape, lambda b, *_: (b,) + (0,) * len(shape))


def run(kernel, scalars, ins, outs, scratch, flops, name):
    arrays = [x for x, _ in ins]
    seqs = next(x.shape[0] for x, spec in ins if spec.block_shape[0] == 1 and x.ndim == 3)
    shapes = [jax.ShapeDtypeStruct(shape, dtype) for (shape, dtype), _ in outs]
    moved = sum(math.prod(x.shape) * x.dtype.itemsize for x in arrays + shapes)
    return pl.pallas_call(
        kernel,
        out_shape=shapes,
        grid_spec=pltpu.PrefetchScalarGridSpec(
            num_scalar_prefetch=len(scalars),
            grid=(seqs,),
            in_specs=[spec for _, spec in ins],
            out_specs=[spec for _, spec in outs],
            scratch_shapes=scratch,
        ),
        compiler_params=pltpu.CompilerParams(
            dimension_semantics=("arbitrary",), vmem_limit_bytes=VMEM
        ),
        cost_estimate=pl.CostEstimate(flops=flops, bytes_accessed=moved, transcendentals=0),
        name=name,
    )(*scalars, *arrays)


def slots_of(ids, vblock, devices):
    owner = ids // vblock
    here = jnp.arange(ids.shape[0])
    same = ids[None, :] == ids[:, None]
    first = jnp.sum(jnp.logical_and(same, here[None, :] < here[:, None]), axis=1) == 0
    below = jnp.logical_and(owner[None, :] == owner[:, None], ids[None, :] < ids[:, None])
    rank = jnp.sum(jnp.logical_and(below, first[None, :]), axis=1).astype(i32)
    return owner, first, rank


def fetch_round(turn, capacity, devices, owner, first, rank, local, low_table):
    slot = jnp.where(rank // capacity == turn, owner * capacity + rank % capacity, -1)
    seats = jnp.arange(devices * capacity)
    chosen = jnp.logical_and(seats[:, None] == slot[None, :], first[None, :])
    request = jnp.sum(jnp.where(chosen, local[None, :] + 1, 0), axis=1) - 1
    message = jnp.full((devices, 128), jnp.max(rank), i32)
    message = message.at[:, :capacity].set(request.reshape(devices, capacity))
    got = lax.all_to_all(message, ALL, 0, 0, tiled=True)
    asked = got[:, :capacity].reshape(-1)
    served = (asked[:, None] == jnp.arange(low_table.shape[0])[None, :]).astype(bf16)
    rows = dot_plain(served, low_table).astype(bf16)
    rows = lax.all_to_all(rows, ALL, 0, 0, tiled=True)
    mine = (slot[:, None] == seats[None, :]).astype(bf16)
    return dot_plain(mine, rows).astype(bf16), mine, served, jnp.max(got[:, capacity])


def return_round(mine, served, grad_word):
    sent = select_sum(mine, grad_word)
    got = lax.all_to_all(sent, ALL, 0, 0, tiled=True)
    return select_sum(served, got)


def body(
    token_ids,
    seg_split,
    lengths,
    mlm_pos,
    mlm_labels,
    sop_labels,
    owner,
    step_count,
    table,
    table_m,
    table_v,
    unit_master,
    unit_m,
    unit_v,
    small,
    small_m,
    small_v,
    taps,
    taps_m,
    taps_v,
):
    mp_count = lax.axis_size(MP)
    dp_count = lax.axis_size(DP)
    devices = mp_count * dp_count
    mp_index = lax.axis_index(MP)
    dp_index = lax.axis_index(DP)
    group_seqs, length = token_ids.shape
    width = small.shape[1]
    part = unit_master.shape[1]
    vblock = table.shape[0]
    cap_slots = unit_master.shape[0]
    matrices = owner.shape[0]
    seqs = group_seqs // mp_count
    tokens = seqs * length
    masks = mlm_pos.shape[1]
    total_seqs = group_seqs * dp_count
    count_all = total_seqs * masks

    def my(x):
        return lax.dynamic_slice_in_dim(x, mp_index * seqs, seqs, 0)

    token_ids, seg_split, lengths = my(token_ids), my(seg_split), my(lengths)
    mlm_pos, mlm_labels, sop_labels = my(mlm_pos), my(mlm_labels), my(sop_labels)

    earlier = jnp.arange(matrices)[:, None] > jnp.arange(matrices)[None, :]
    slot_rank = jnp.sum(jnp.logical_and(earlier, owner[:, None] == owner[None, :]), axis=1)
    slot_index = owner * cap_slots + slot_rank
    selector = jnp.logical_and(
        owner[None, :] == dp_index, slot_rank[None, :] == jnp.arange(cap_slots)[:, None]
    ).astype(f32)
    rest = part // dp_count
    low_slots = unit_master.astype(bf16).reshape(cap_slots, dp_count, rest, width)
    got_slots = lax.all_to_all(jnp.moveaxis(low_slots, 1, 0), DP, 0, 0, tiled=True)
    got_slots = got_slots.reshape(dp_count * cap_slots, rest, width)
    picked = jnp.stack(
        [lax.dynamic_index_in_dim(got_slots, slot_index[k], 0, False) for k in range(matrices)]
    )
    shards = jnp.moveaxis(lax.all_gather(picked, DP, axis=0), 0, 1)
    shards = shards.reshape(matrices, part, width)
    first_units = lax.all_gather(shards[:3], MP, axis=0)
    last_units = lax.all_gather(shards[3:], MP, axis=0)
    low_table = table.astype(bf16)
    vocab = lax.all_gather(low_table, RG, axis=0, tiled=True)

    ids = token_ids.reshape(-1)
    capacity = max(8, -(-1280 // devices))
    home, first, rank = slots_of(ids, vblock, devices)
    local = ids % vblock
    fetch = partial(
        fetch_round,
        capacity=capacity,
        devices=devices,
        owner=home,
        first=first,
        rank=rank,
        local=local,
        low_table=low_table,
    )
    word_rows, mine, served, top_rank = fetch(0)
    turns = top_rank // capacity + 1

    def more(state):
        return state[0] < turns

    def fetch_more(state):
        return (state[0] + 1, state[1] + fetch(state[0])[0])

    _, word_rows = lax.while_loop(more, fetch_more, (jnp.int32(1), word_rows))

    words_in = word_rows.reshape(seqs, length, width)
    places = small[6 : 6 + length]
    edge = jnp.concatenate([small[:6], small[6 + length : 8 + length]])
    span = (HEADS - FIRST) * DH
    taps_span = [
        taps[:, CONV.index(h) * DH : (CONV.index(h) + 1) * DH]
        if h in CONV
        else jnp.zeros((taps.shape[0], DH), f32)
        for h in range(FIRST, HEADS)
    ]
    taps_span = jnp.concatenate(taps_span, axis=1)
    act = (length, width)
    flop = 2 * tokens * width * width
    embedded, qkv, lse, heads = run(
        forward_heads,
        (seg_split, lengths),
        [
            (words_in, each(act)),
            (places, fixed(places.shape)),
            (edge, fixed(edge.shape)),
            (taps_span, fixed(taps_span.shape)),
            (first_units, fixed(first_units.shape)),
        ],
        [
            (((seqs,) + act, f32), each(act)),
            (((seqs, length, 3 * width), bf16), each((length, 3 * width))),
            (((seqs, length, 128), f32), each((length, 128))),
            (((seqs,) + act, bf16), each(act)),
        ],
        [pltpu.VMEM((length + 16, span), f32)],
        8 * flop,
        "forward_heads",
    )
    spots = mlm_pos[:, :, None]
    one, two, masked_rows, cls_rows = run(
        forward_ffn,
        (),
        [
            (spots, each((masks, 1))),
            (heads, each(act)),
            (embedded, each(act)),
            (edge, fixed(edge.shape)),
            (last_units, fixed(last_units.shape)),
        ],
        [
            (((seqs,) + act, f32), each(act)),
            (((seqs,) + act, f32), each(act)),
            (((seqs, masks, width), bf16), each((masks, width))),
            (((seqs, 8, width), f32), each((8, width))),
        ],
        [],
        8 * flop,
        "forward_ffn",
    )
    masked_rows = masked_rows.reshape(seqs * masks, width)

    all_masked = grow(grow(masked_rows, "dh"), "mh")
    all_labels = grow(grow(mlm_labels.reshape(-1), "dh"), "mh")
    logits = dot_right(all_masked, vocab)
    group_count = lax.axis_size(VG)
    block = all_labels // vblock
    block_ml = block % lax.axis_size("ml")
    block_mh = block // lax.axis_size("ml") % lax.axis_size("mh")
    block_dl = block // mp_count % lax.axis_size("dl")
    block_dh = block // (mp_count * lax.axis_size("dl"))
    label_mine = jnp.logical_and(
        block_dh == lax.axis_index("dh"), block_mh == lax.axis_index("mh")
    )
    label_row = (block_dl * lax.axis_size("ml") + block_ml) * vblock + all_labels % vblock
    onehot = jnp.logical_and(
        jnp.arange(vocab.shape[0])[None, :] == label_row[:, None], label_mine[:, None]
    )
    top = jnp.max(logits, axis=1)
    total = jnp.sum(jnp.exp(logits - top[:, None]), axis=1)
    target = jnp.sum(jnp.where(onehot, logits, 0.0), axis=1)
    order = lax.axis_index("mh") * lax.axis_size("dh") + lax.axis_index("dh")
    stats = jnp.stack([top, total, target]).reshape(3, group_count, -1)
    stats = relative(jnp.moveaxis(stats, 1, 0), order)
    stats = stats.reshape(lax.axis_size("mh"), lax.axis_size("dh"), 3, -1)
    stats = jnp.moveaxis(stats, 0, 1).reshape(group_count, 3, -1)
    stats = everyone(stats, VG)
    top_all = jnp.max(stats[:, :, 0], axis=0)
    total_all = jnp.sum(stats[:, :, 1] * jnp.exp(stats[:, :, 0] - top_all), axis=0)
    log_all = top_all + jnp.log(total_all)
    log_sum = log_all.reshape(lax.axis_size("dh"), lax.axis_size("mh"), -1)
    log_sum = jnp.moveaxis(log_sum, 0, 1).reshape(group_count, -1)
    log_sum = relative(log_sum, order).reshape(-1)
    target_all = jnp.sum(stats[:, :, 2], axis=0)
    mlm_part = jnp.sum(log_all - target_all) / count_all / group_count
    grad_logits = (
        (jnp.exp(logits - log_sum[:, None]) - onehot.astype(f32)) / count_all
    ).astype(bf16)
    grad_masked = shrink(shrink(dot_plain(grad_logits, vocab), "mh"), "dh")
    grad_table = dot_left(grad_logits, all_masked).reshape(2, 2, vblock, width)
    grad_table = fold(fold(grad_table, "ml", 0, 1), "dl", 0, 0)
    sop_part, sop_pull = jax.vjp(
        partial(sop_loss, labels=sop_labels, denom=total_seqs, length=length), cls_rows[:, 0], small
    )
    grad_cls, grad_small_sop = sop_pull(jnp.ones((), f32))
    grad_cls = jnp.pad(grad_cls[:, None], ((0, 0), (0, 7), (0, 0)))
    sum_one, grad_heads, wide_last, edge_last = run(
        backward_ffn,
        (),
        [
            (spots, each((masks, 1))),
            (grad_masked.reshape(seqs, masks, width), each((masks, width))),
            (grad_cls, each((8, width))),
            (one, each(act)),
            (two, each(act)),
            (heads, each(act)),
            (edge, fixed(edge.shape)),
            (last_units, fixed(last_units.shape)),
        ],
        [
            (((seqs,) + act, f32), each(act)),
            (((seqs,) + act, bf16), each(act)),
            ((last_units.shape, f32), fixed(last_units.shape)),
            ((edge.shape, f32), fixed(edge.shape)),
        ],
        [],
        16 * flop,
        "backward_ffn",
    )
    grad_word, grad_places, edge_first, grad_taps, wide_first = run(
        backward_heads,
        (seg_split, lengths),
        [
            (words_in, each(act)),
            (places, fixed(places.shape)),
            (edge, fixed(edge.shape)),
            (taps_span, fixed(taps_span.shape)),
            (first_units, fixed(first_units.shape)),
            (qkv, each((length, 3 * width))),
            (lse, each((length, 128))),
            (grad_heads, each(act)),
            (sum_one, each(act)),
        ],
        [
            (((seqs,) + act, f32), each(act)),
            ((act, f32), fixed(act)),
            ((edge.shape, f32), fixed(edge.shape)),
            ((taps_span.shape, f32), fixed(taps_span.shape)),
            ((first_units.shape, f32), fixed(first_units.shape)),
        ],
        [pltpu.VMEM((length + 16, span), f32)] * 2,
        20 * flop,
        "backward_heads",
    )
    grad_taps = jnp.concatenate(
        [grad_taps[:, (h - FIRST) * DH : (h - FIRST + 1) * DH] for h in CONV], axis=1
    )
    grad_word = grad_word.reshape(tokens, width)

    words = return_round(mine, served, grad_word)

    def return_more(state):
        _, mine_r, served_r, _ = fetch(state[0])
        return (state[0] + 1, state[1] + return_round(mine_r, served_r, grad_word))

    _, words = lax.while_loop(more, return_more, (jnp.int32(1), words))
    grad_table_own = grad_table + words

    def reduce_units(x, axes):
        many = x.shape[1]
        x = x.reshape(2, 2, many, dp_count, rest, width)
        dims = {"mh": 0, "ml": 1}
        for axis in axes:
            if axis in dims:
                x = fold(x, axis, 0, dims.pop(axis))
                dims = {name: 0 for name in dims}
            else:
                where = x.ndim - 3
                lead = x.shape[:where]
                if axis == "dl":
                    x = x.reshape(lead + (x.shape[where] // 2, 2) + x.shape[-2:])
                    x = fold(x, "dl", 0, where + 1)
                else:
                    for bit in reversed(range(bits_of("dh"))):
                        x = x.reshape(lead + (2, x.shape[where] // 2) + x.shape[-2:])
                        x = fold(x, "dh", bit, where)
        return x.reshape(many, rest, width)

    pieces_last = lax.psum_scatter(
        wide_last.reshape(-1, width), MP, scatter_dimension=0, tiled=True
    )
    pieces_last = jnp.moveaxis(pieces_last.reshape(-1, dp_count, rest, width), 1, 0)
    pieces_last = lax.psum_scatter(
        pieces_last.reshape(-1, width), DP, scatter_dimension=0, tiled=True
    ).reshape(-1, rest, width)
    pieces_first = reduce_units(wide_first, ("ml", "dl", "mh", "dh"))
    summed = jnp.concatenate([pieces_first, pieces_last])
    seat = (slot_index[None, :] == jnp.arange(dp_count * cap_slots)[:, None]).astype(f32)
    slotted = sum(seat[:, k, None, None] * summed[k][None] for k in range(matrices))
    slotted = slotted.reshape(dp_count, cap_slots, rest, width)
    grad_slots = lax.all_to_all(slotted, DP, 0, 0, tiled=True)
    grad_slots = jnp.moveaxis(grad_slots, 0, 1).reshape(cap_slots, part, width)

    edge_sum = edge_first + edge_last
    same = devices // 2
    half = fold(grad_places.reshape(2, length // 2, width), "ml", 0, 0)
    piece = -(-(length // 2) // same)
    half = jnp.pad(half, ((0, piece * same - length // 2), (0, 0)))
    got = lax.all_to_all(half.reshape(same, piece, width), CHIPS, 0, 0, tiled=True)
    places_own = jnp.sum(got, axis=0)
    places_half = everyone(places_own, CHIPS).reshape(same * piece, width)[: length // 2]
    other = swap(places_half, "ml", 0)
    low_first = lax.axis_index("ml") == 0
    places_sum = jnp.concatenate(
        [jnp.where(low_first, places_half, other), jnp.where(low_first, other, places_half)]
    )
    misc = jnp.concatenate(
        [
            edge_sum.reshape(-1),
            grad_small_sop[8 + length :].reshape(-1),
            grad_taps.reshape(-1),
            jnp.reshape(mlm_part + sop_part, (1,)),
        ]
    )
    size = misc.shape[0]
    lane = -(-size // (devices * 128)) * 128
    misc = jnp.pad(misc, (0, devices * lane - size)).reshape(devices, lane)
    misc_own = jnp.sum(lax.all_to_all(misc, ALL, 0, 0, tiled=True), axis=0)
    misc = everyone(misc_own, ALL).reshape(-1)
    ends = (small.shape[0] - length) * width
    ends_sum = misc[:ends].reshape(-1, width)
    small_sum = jnp.concatenate([ends_sum[:6], places_sum, ends_sum[6:]])
    taps_sum = misc[ends : size - 1].reshape(taps.shape)
    loss = misc[size - 1]
    square = (
        jnp.sum(grad_table_own * grad_table_own)
        + jnp.sum(grad_slots * grad_slots)
        + jnp.sum(places_own * places_own)
        + (jnp.sum(ends_sum * ends_sum) + jnp.sum(taps_sum * taps_sum)) / devices
    )
    squares = everyone(jnp.full((128,), square, f32), ALL)
    grad_norm = jnp.sqrt(jnp.sum(squares[:, 0]))
    scale = clip_bound / jnp.maximum(grad_norm, clip_bound)
    count = step_count[0].astype(f32)
    table_new, table_m_new, table_v_new = adam(
        table, table_m, table_v, grad_table_own * scale, count
    )
    used = jnp.sum(selector, axis=1)[:, None, None]
    unit_new, unit_m_new, unit_v_new = adam(unit_master, unit_m, unit_v, grad_slots * scale, count)
    unit_new = unit_new * used
    unit_m_new = unit_m_new * used
    unit_v_new = unit_v_new * used
    small_new, small_m_new, small_v_new = adam(small, small_m, small_v, small_sum * scale, count)
    taps_new, taps_m_new, taps_v_new = adam(taps, taps_m, taps_v, taps_sum * scale, count)
    return (
        loss,
        grad_norm,
        table_new,
        table_m_new,
        table_v_new,
        table_new.astype(bf16),
        unit_new,
        unit_m_new,
        unit_v_new,
        unit_new.astype(bf16),
        small_new,
        small_m_new,
        small_v_new,
        taps_new,
        taps_m_new,
        taps_v_new,
    )


def solution(mesh):
    dp, mp = mesh.devices.shape
    fine = Mesh(mesh.devices.reshape(dp // 2, 2, mp // 2, 2), ALL)
    rows = P(DP)
    vocab = P(ALL)
    slots = P(DP, MP)
    placed = (rows,) * 6 + (P(),) * 2 + (vocab,) * 3 + (slots,) * 3 + (P(),) * 6
    return jax.shard_map(
        body,
        mesh=fine,
        in_specs=placed,
        out_specs=(P(),) * 2 + (vocab,) * 4 + (slots,) * 4 + (P(),) * 6,
        check_vma=False,
    )
```

```python
import math
from functools import partial

import jax
import jax.numpy as jnp
from jax import lax
from jax.experimental import pallas as pl
from jax.experimental.pallas import tpu as pltpu
from jax.sharding import Mesh, PartitionSpec as P

DH = 64
HEADS = 12
PER = 3
ATTN = tuple(h for h in range(HEADS) if h % PER < PER - h // PER)
CONV = tuple(h for h in range(HEADS) if h % PER >= PER - h // PER)

FIRST = min(CONV) // 2 * 2

DP = ("d2", "d1", "d0")
MP = ("m1", "m0")
ALL = DP + MP
CHIPS = DP + ("m1",)
VG = ("d1", "d0", "m1")
RG = ("d2", "m0")
ORDERS = (("d1", "d0", "m1"), ("d0", "m1", "d1"), ("m1", "d1", "d0"))

f32 = jnp.float32
bf16 = jnp.bfloat16
i32 = jnp.int32
highest = lax.Precision.HIGHEST
beta_one = 0.9
beta_two = 0.999
adam_eps = 1e-08
learn_rate = 0.03
weight_decay = 0.01
clip_bound = 0.02
norm_eps = 1e-06
VMEM = 60 << 20


def dot_right(left, right):
    return lax.dot_general(left, right, (((1,), (1,)), ((), ())), preferred_element_type=f32)


def dot_left(left, right):
    return lax.dot_general(left, right, (((0,), (0,)), ((), ())), preferred_element_type=f32)


def dot_plain(left, right):
    return lax.dot_general(left, right, (((1,), (0,)), ((), ())), preferred_element_type=f32)


def halves(x):
    high = lax.reduce_precision(x, 8, 7)
    return high.astype(bf16), (x - high).astype(bf16)


def select_sum(chosen, values):
    high, low = halves(values)
    return dot_left(chosen, high) + dot_left(chosen, low)


def sop_loss(cls_rows, pair, labels, denom):
    logits = jnp.dot(cls_rows, pair.T, precision=highest)
    chosen = jnp.take_along_axis(logits, labels[:, None], axis=1)[:, 0]
    return jnp.sum(jax.nn.logsumexp(logits, axis=-1) - chosen) / denom


def adam(weight, first, second, grad, count):
    first_new = beta_one * first + (1.0 - beta_one) * grad
    second_new = beta_two * second + (1.0 - beta_two) * grad * grad
    corr_one = 1.0 - jnp.power(beta_one, count)
    corr_two = 1.0 - jnp.power(beta_two, count)
    step = first_new / corr_one / (jnp.sqrt(second_new / corr_two) + adam_eps)
    return (weight - learn_rate * (step + weight_decay * weight), first_new, second_new)


def everyone(x, axes):
    count = lax.axis_size(axes)
    return lax.all_to_all(jnp.broadcast_to(x, (count,) + x.shape), axes, 0, 0, tiled=True)


def swap(x, axis, bit):
    count = lax.axis_size(axis)
    return lax.ppermute(x, axis, [(i, i ^ (1 << bit)) for i in range(count)])


def bits_of(axis):
    return lax.axis_size(axis).bit_length() - 1


def together(*arrays):
    return lax.optimization_barrier(arrays)


def bit_of(axis, bit):
    return (lax.axis_index(axis) >> bit) & 1


def fold_near(x, axis, dim):
    for bit in reversed(range(bits_of(axis))):
        lead, rest = x.shape[:dim], x.shape[dim + 1 :]
        x = x.reshape(lead + (2, x.shape[dim] // 2) + rest)
        sent = lax.index_in_dim(x, 1, dim, False)
        x = lax.index_in_dim(x, 0, dim, False) + swap(sent, axis, bit)
    return x.reshape(x.shape[:dim] + x.shape[dim + 1 :])


def slot_of(d, m, high):
    return ((((m & 1) * 2 + (d & 1)) * 2 + (m >> 1)) * 2 + ((d >> 1) & 1)) * high + (d >> 2)


def spread_axis(x, axis, dim):
    x = jnp.expand_dims(x, dim)
    for bit in range(bits_of(axis)):
        other = swap(x, axis, bit)
        me = bit_of(axis, bit) == 1
        x = jnp.concatenate([jnp.where(me, other, x), jnp.where(me, x, other)], axis=dim)
    return x


def grow(x, axis):
    for bit in range(bits_of(axis)):
        x = jnp.concatenate([x, swap(x, axis, bit)], axis=0)
    return x


def shrink(x, axis):
    for bit in reversed(range(bits_of(axis))):
        half = x.shape[0] // 2
        x = x[:half] + swap(x[half:], axis, bit)
    return x


def row_parts(count):
    most = -(-count // (8 * len(ORDERS))) * 8
    return [slice(at, min(at + most, count)) for at in range(0, count, most)]


def grow_parts(x):
    parts = [x[None, rows] for rows in row_parts(x.shape[0])]
    for stage in range(len(VG)):
        parts = [grow(p, order[stage]) for p, order in zip(parts, ORDERS)]
    return jnp.concatenate([p.reshape((-1,) + p.shape[2:]) for p in parts])


def cut_parts(x, count, dim=0):
    pieces, at = [], 0
    for rows in row_parts(count):
        size = (rows.stop - rows.start) << len(VG)
        piece = lax.slice_in_dim(x, at, at + size, axis=dim)
        pieces.append(piece.reshape(x.shape[:dim] + (1 << len(VG), -1) + x.shape[dim + 1 :]))
        at += size
    return pieces


def near_labels(got, own):
    x = got.reshape(tuple(lax.axis_size(a) for a in ALL) + (own,))
    x = lax.dynamic_index_in_dim(x, lax.axis_index("m0"), 4, False)
    x = lax.dynamic_index_in_dim(x, lax.axis_index("d2"), 0, False)
    for dim, axis in enumerate(VG):
        x = jnp.where(lax.axis_index(axis) == 1, jnp.flip(x, axis=dim), x)
    parts = []
    for rows, order in zip(row_parts(own), ORDERS):
        dims = [VG.index(axis) for axis in order[::-1]]
        parts.append(jnp.transpose(x[..., rows], dims + [len(VG)]).reshape(-1))
    return jnp.concatenate(parts)


def merge_stats(stats, count):
    for axis in VG:
        other = swap(stats, axis, 0)
        flipped = []
        for p, order in zip(cut_parts(other, count, 1), ORDERS):
            low = 1 << order.index(axis)
            y = p.reshape(3, p.shape[1] // (2 * low), 2, low, p.shape[2])
            flipped.append(jnp.flip(y, axis=2).reshape(3, -1))
        other = jnp.concatenate(flipped, axis=1)
        top = jnp.maximum(stats[0], other[0])
        total = stats[1] * jnp.exp(stats[0] - top) + other[1] * jnp.exp(other[0] - top)
        stats = jnp.stack([top, total, stats[2] + other[2]])
    return stats


def rows_norm(x):
    center = jnp.mean(x, axis=-1, keepdims=True)
    shifted = x - center
    inv = lax.rsqrt(jnp.mean(shifted * shifted, axis=-1, keepdims=True) + norm_eps)
    return shifted * inv, inv


def erf(x):
    x = jnp.clip(x, -3.832506856900711, 3.832506856900711)
    y = x * x
    top = jnp.float32(0.00022905065861350646)
    for c in (0.0034082910107109506, 0.050955695062380861, 0.18520832239976145, 1.128379143519084):
        top = top * y + c
    low = jnp.float32(-1.1791602954361697e-7)
    for c in (
        0.000023547966471313185,
        0.0010179625278914885,
        0.014070470171167667,
        0.11098505178285362,
        0.49746925110067538,
        1.0,
    ):
        low = low * y + c
    return x * top / low


def head_mask(rows, groups):
    row = lax.broadcasted_iota(i32, (rows, groups * DH), 0)
    col = lax.broadcasted_iota(i32, (rows, groups * DH), 1)
    return lax.rem(row, groups) == lax.div(col, DH)


def split3(x):
    a = x.astype(bf16)
    r = x - a.astype(f32)
    b = r.astype(bf16)
    c = (r - b.astype(f32)).astype(bf16)
    return a, b, c


def dot_exact(a, b, dims):
    return lax.dot_general(a, b, (dims, ((), ())), precision=highest, preferred_element_type=f32)


def conv_kernel_rows(prod, taps_ref, groups):
    width = taps_ref.shape[0]
    spread = jnp.concatenate(
        [jnp.broadcast_to(taps_ref[o : o + 1, :], (groups, prod.shape[1])) for o in range(width)], axis=0
    )
    spread = jnp.where(head_mask(width * groups, groups), spread, 0.0)
    logits = dot_exact(spread, prod, ((1,), (1,)))
    parts = [logits[o * groups : (o + 1) * groups] for o in range(width)]
    top = parts[0]
    for p in parts[1:]:
        top = jnp.maximum(top, p)
    weights = [jnp.exp(p - top) for p in parts]
    total = weights[0]
    for w in weights[1:]:
        total = total + w
    inv = 1.0 / total
    return [w * inv for w in weights], spread


def spread_rows(rows, groups):
    three = jnp.concatenate(split3(rows), axis=0)
    ones = head_mask(3 * groups, groups).astype(bf16)
    return lax.dot_general(three, ones, (((0,), (0,)), ((), ())), preferred_element_type=f32)


def forward_heads(
    split_ref, length_ref, word_ref, places_ref, edge_ref, taps_ref, units_ref,
    emb_ref, qkv_ref, lse_ref, heads_ref, pad_ref,
):
    at = pl.program_id(0)
    length, width = word_ref.shape[1:]
    later = lax.broadcasted_iota(i32, (length, 1), 0) > split_ref[at]
    summed = word_ref[0].astype(f32) + places_ref[...]
    summed = summed + jnp.where(later, edge_ref[7:8, :], edge_ref[6:7, :])
    normed, _ = rows_norm(summed)
    embedded = normed * edge_ref[0:1, :] + edge_ref[3:4, :]
    emb_ref[0] = embedded
    low_in = embedded.astype(bf16)
    part = units_ref.shape[2]
    for k in range(3):
        unit = units_ref[:, k].reshape(width, width)
        qkv_ref[0, :, k * width : (k + 1) * width] = dot_right(low_in, unit).astype(bf16)
    allowed = lax.broadcasted_iota(i32, (length, length), 1) < length_ref[at]
    lanes = lax.broadcasted_iota(i32, (length, 128), 1)
    lse = jnp.zeros((length, 128), f32)
    outs = {}
    for n, h in enumerate(ATTN):
        q = qkv_ref[0, :, h * DH : (h + 1) * DH]
        k = qkv_ref[0, :, width + h * DH : width + (h + 1) * DH]
        v = qkv_ref[0, :, 2 * width + h * DH : 2 * width + (h + 1) * DH]
        scores = jnp.where(allowed, dot_right(q, k) * (1.0 / math.sqrt(DH)), -1e30)
        top = jnp.max(scores, axis=1, keepdims=True)
        weights = jnp.exp(scores - top)
        total = jnp.sum(weights, axis=1, keepdims=True)
        probs = (weights * (1.0 / total)).astype(bf16)
        outs[h] = dot_plain(probs, v).astype(bf16)
        lse = jnp.where(lanes == n, top + jnp.log(total), lse)
    lse_ref[0] = lse
    groups = HEADS - FIRST
    base = FIRST * DH
    q = qkv_ref[0, :, base:width].astype(f32)
    k = qkv_ref[0, :, width + base : 2 * width].astype(f32)
    kernel, _ = conv_kernel_rows(q * k, taps_ref, groups)
    taps = len(kernel)
    pad_ref[0:8, :] = jnp.zeros((8, width - base), f32)
    pad_ref[8 + length : 16 + length, :] = jnp.zeros((8, width - base), f32)
    pad_ref[8 : 8 + length, :] = qkv_ref[0, :, 2 * width + base :].astype(f32)
    total = jnp.zeros((length, width - base), f32)
    for o in range(taps):
        start = 8 + o - taps // 2
        total = total + spread_rows(kernel[o], groups) * pad_ref[start : start + length, :]
    total = total.astype(bf16)
    for h in CONV:
        outs[h] = total[:, (h - FIRST) * DH : (h - FIRST + 1) * DH]
    heads_ref[0] = jnp.concatenate([outs[h] for h in range(HEADS)], axis=1)


def ffn_weights(units_ref, s, first):
    return jnp.concatenate([units_ref[s, first], units_ref[s, first + 1]], axis=0)


def forward_ffn(
    pos_ref, heads_ref, emb_ref, edge_ref, units_ref, one_ref, two_ref, mask_ref, cls_ref
):
    length, width = emb_ref.shape[1:]
    mp_count, part = units_ref.shape[0], units_ref.shape[2]
    unit = units_ref[:, 0].reshape(width, width)
    projected = dot_right(heads_ref[0], unit).astype(bf16).astype(f32)
    one = emb_ref[0] + projected
    one_ref[0] = one
    normed, _ = rows_norm(one)
    attended = normed * edge_ref[1:2, :] + edge_ref[4:5, :]
    low_mid = attended.astype(bf16)
    for g in range(2):
        cols = slice(2 * part * g, 2 * part * (g + 1))
        total = None
        for s in (2 * g, 2 * g + 1):
            pre = dot_plain(low_mid[:, cols], ffn_weights(units_ref, s, 1))
            hidden = (pre * (0.5 + 0.5 * erf(pre * math.sqrt(0.5)))).astype(bf16)
            out = dot_right(hidden, ffn_weights(units_ref, s, 3))
            total = out if total is None else total + out
        two_ref[0, :, cols] = attended[:, cols] + total
    normed, _ = rows_norm(two_ref[0])
    final = normed * edge_ref[2:3, :] + edge_ref[5:6, :]
    masks = mask_ref.shape[1]
    picked = lax.broadcasted_iota(i32, (masks, length), 1) == pos_ref[0][:, 0:1]
    mask_ref[0] = dot_plain(picked.astype(bf16), final.astype(bf16)).astype(bf16)
    cls_ref[0] = final[0:8]


def norm_grad(grad, normed, inv, gain):
    scaled = grad * gain
    mean = jnp.mean(scaled, axis=-1, keepdims=True)
    along = jnp.mean(scaled * normed, axis=-1, keepdims=True)
    return inv * (scaled - mean - normed * along)


def down(x):
    return jnp.sum(x, axis=0, keepdims=True)


def add_rows(ref, me, mp_count, at, matrix, rows):
    if len(ref.shape) == 4:
        ref[at, matrix] += rows
        return
    dp_count = ref.shape[0] // mp_count
    rest = rows.shape[0] // dp_count
    here = slice(matrix * rest, (matrix + 1) * rest)
    for d in range(dp_count):
        ref[slot_of(d, at, dp_count // 4) ^ me, here, :] += rows[d * rest : (d + 1) * rest]


def backward_ffn(
    me_ref, pos_ref, grad_ref, cls_ref, one_ref, two_ref, heads_ref, edge_ref, units_ref,
    sum_ref, back_ref, edges_ref, *wide_refs,
):
    at = pl.program_id(0)
    wide_ref = wide_refs[-1]
    length, width = one_ref.shape[1:]
    mp_count, part = units_ref.shape[0], units_ref.shape[2]

    @pl.when(at == 0)
    def _():
        wide_ref[...] = jnp.zeros_like(wide_ref)
        edges_ref[...] = jnp.zeros_like(edges_ref)

    masks = grad_ref.shape[1]
    picked = (lax.broadcasted_iota(i32, (masks, length), 1) == pos_ref[0][:, 0:1]).astype(bf16)
    high = grad_ref[0].astype(bf16)
    low = (grad_ref[0] - high.astype(f32)).astype(bf16)
    grad = dot_left(picked, high) + dot_left(picked, low)
    rows = lax.broadcasted_iota(i32, (length, 1), 0)
    grad = grad + jnp.where(rows == 0, cls_ref[0][0:1, :], 0.0)
    normed, inv = rows_norm(two_ref[0])
    edges_ref[2:3, :] += down(grad * normed)
    edges_ref[5:6, :] += down(grad)
    grad_two = norm_grad(grad, normed, inv, edge_ref[2:3, :])
    low_two = grad_two.astype(bf16)
    normed, inv = rows_norm(one_ref[0])
    low_mid = (normed * edge_ref[1:2, :] + edge_ref[4:5, :]).astype(bf16)
    backs = []
    for g in range(2):
        cols = slice(2 * part * g, 2 * part * (g + 1))
        total = None
        for s in (2 * g, 2 * g + 1):
            w_in = ffn_weights(units_ref, s, 1)
            w_out = ffn_weights(units_ref, s, 3)
            pre = dot_plain(low_mid[:, cols], w_in)
            half = 0.5 + 0.5 * erf(pre * math.sqrt(0.5))
            hidden = (pre * half).astype(bf16)
            slope = half + pre * (jnp.exp(-0.5 * pre * pre) * (1.0 / math.sqrt(2.0 * math.pi)))
            grad_hidden = dot_plain(low_two[:, cols], w_out)
            w = dot_left(low_two[:, cols], hidden)
            add_rows(wide_ref, me_ref[0], mp_count, s, 3, w[:part])
            add_rows(wide_ref, me_ref[0], mp_count, s, 4, w[part:])
            grad_pre = (grad_hidden * slope).astype(bf16)
            w = dot_left(low_mid[:, cols], grad_pre)
            add_rows(wide_ref, me_ref[0], mp_count, s, 1, w[:part])
            add_rows(wide_ref, me_ref[0], mp_count, s, 2, w[part:])
            back = dot_right(grad_pre, w_in)
            total = back if total is None else total + back
        backs.append(total)
    grad = grad_two + jnp.concatenate(backs, axis=1)
    edges_ref[1:2, :] += down(grad * normed)
    edges_ref[4:5, :] += down(grad)
    grad_one = norm_grad(grad, normed, inv, edge_ref[1:2, :])
    sum_ref[0] = grad_one
    low_one = grad_one.astype(bf16)
    w = dot_left(low_one, heads_ref[0])
    for s in range(mp_count):
        add_rows(wide_ref, me_ref[0], mp_count, s, 0, w[s * part : (s + 1) * part])
    unit = units_ref[:, 0].reshape(width, width)
    back_ref[0] = dot_plain(low_one, unit).astype(bf16)

    if len(wide_refs) > 1:

        @pl.when(at == pl.num_programs(0) - 1)
        def _():
            half = wide_ref.shape[0] // 2
            wide_refs[0][...] = wide_ref[:half]
            wide_refs[1][...] = wide_ref[half:]


def backward_heads(start, last, direct, *refs):
    (split_ref, length_ref, me_ref, word_ref, places_ref, edge_ref, taps_ref, units_ref) = refs[:8]
    (qkv_ref, lse_ref, back_ref, sum_ref, seat_ref, late_ref) = refs[8:14]
    refs = refs[14:]
    so_far = []
    if start > 0:
        count = 4 if direct else 5
        so_far, refs = refs[:count], refs[count:]
    gword_ref, gedge_ref, gtaps_ref, seats_ref = refs[:4]
    if direct and last:
        kept_ref, sent_ref, pad_ref, shift_ref, wide_ref = refs[4:]
        sums = [gedge_ref, gtaps_ref, seats_ref, wide_ref]
    else:
        *sums, pad_ref, shift_ref = refs[1:]
        wide_ref = sums[3]
    at = pl.program_id(0) + start
    me = me_ref[0]
    mp_count = units_ref.shape[0]
    length, width = word_ref.shape[1:]
    for n, new in enumerate(sums):
        if n != 2:
            new[...] = so_far[n][...] if so_far else jnp.zeros_like(new)

    groups = HEADS - FIRST
    base = FIRST * DH
    span = width - base
    q = qkv_ref[0, :, base:width].astype(f32)
    k = qkv_ref[0, :, width + base : 2 * width].astype(f32)
    prod = q * k
    kernel, spread = conv_kernel_rows(prod, taps_ref, groups)
    taps = len(kernel)
    out = back_ref[0, :, base:].astype(f32)
    pad_ref[0:8, :] = jnp.zeros((8, span), f32)
    pad_ref[8 + length : 16 + length, :] = jnp.zeros((8, span), f32)
    pad_ref[8 : 8 + length, :] = qkv_ref[0, :, 2 * width + base :].astype(f32)
    shift_ref[0:8, :] = jnp.zeros((8, span), f32)
    shift_ref[8 + length : 16 + length, :] = jnp.zeros((8, span), f32)
    grad_values = jnp.zeros((length, span), f32)
    lanes = 128
    dots = jnp.zeros((length, lanes), f32)
    column = lax.broadcasted_iota(i32, (span, lanes), 0)
    lane = lax.broadcasted_iota(i32, (span, lanes), 1)
    for o in range(taps):
        start = 8 + o - taps // 2
        moved = out * pad_ref[start : start + length, :]
        high = moved.astype(bf16)
        low = (moved - high.astype(f32)).astype(bf16)
        ones = (lane == o * groups + lax.div(column, DH)).astype(bf16)
        dots = dots + dot_plain(high, ones) + dot_plain(low, ones)
        shift_ref[8 : 8 + length, :] = spread_rows(kernel[o], groups) * out
        back = 8 + taps // 2 - o
        grad_values = grad_values + shift_ref[back : back + length, :]
    dots = dots.T
    parts = [dots[o * groups : (o + 1) * groups] for o in range(taps)]
    along = kernel[0] * parts[0]
    for o in range(1, taps):
        along = along + kernel[o] * parts[o]
    grad_logits = jnp.concatenate([kernel[o] * (parts[o] - along) for o in range(taps)], axis=0)
    grad_prod = dot_exact(grad_logits, spread, ((0,), (0,)))
    grad_taps = dot_exact(grad_logits, prod, ((1,), (0,)))
    head = lax.div(lax.broadcasted_iota(i32, (taps * groups, span), 1), DH) + FIRST
    real = head_mask(taps * groups, groups)
    for h in range(FIRST, HEADS):
        if h not in CONV:
            real = jnp.logical_and(real, head != h)
    grad_taps = jnp.where(real, grad_taps, 0.0)
    for o in range(taps):
        gtaps_ref[o : o + 1, :] += down(grad_taps[o * groups : (o + 1) * groups])
    grads = [(grad_prod * k).astype(bf16), (grad_prod * q).astype(bf16), grad_values.astype(bf16)]
    pieces = [[None] * HEADS for _ in range(3)]
    for h in CONV:
        for n in range(3):
            pieces[n][h] = grads[n][:, (h - FIRST) * DH : (h - FIRST + 1) * DH]

    allowed = lax.broadcasted_iota(i32, (length, length), 1) < length_ref[at]
    scale = 1.0 / math.sqrt(DH)
    for n, h in enumerate(ATTN):
        qh = qkv_ref[0, :, h * DH : (h + 1) * DH]
        kh = qkv_ref[0, :, width + h * DH : width + (h + 1) * DH]
        vh = qkv_ref[0, :, 2 * width + h * DH : 2 * width + (h + 1) * DH]
        gh = back_ref[0, :, h * DH : (h + 1) * DH]
        scores = jnp.where(allowed, dot_right(qh, kh) * scale, -1e30)
        probs = jnp.exp(scores - lse_ref[0][:, n : n + 1])
        grad_probs = dot_right(gh, vh)
        total = jnp.sum(probs * grad_probs, axis=1, keepdims=True)
        grad_scores = (probs * (grad_probs - total)).astype(bf16)
        pieces[0][h] = (dot_plain(grad_scores, kh) * scale).astype(bf16)
        pieces[1][h] = (dot_left(grad_scores, qh) * scale).astype(bf16)
        pieces[2][h] = dot_left(probs.astype(bf16), gh).astype(bf16)
    later = lax.broadcasted_iota(i32, (length, 1), 0) > split_ref[at]
    summed = word_ref[0].astype(f32) + places_ref[...]
    summed = summed + jnp.where(later, edge_ref[7:8, :], edge_ref[6:7, :])
    normed, inv = rows_norm(summed)
    low_in = (normed * edge_ref[0:1, :] + edge_ref[3:4, :]).astype(bf16)
    grad = sum_ref[0]
    for n in range(3):
        g = jnp.concatenate(pieces[n], axis=1)
        w = dot_left(g, low_in)
        part = units_ref.shape[2]
        for s in range(mp_count):
            add_rows(wide_ref, me, mp_count, s, n, w[s * part : (s + 1) * part])
        grad = grad + dot_plain(g, units_ref[:, n].reshape(width, width))
    gedge_ref[0:1, :] += down(grad * normed)
    gedge_ref[3:4, :] += down(grad)
    grad = norm_grad(grad, normed, inv, edge_ref[0:1, :])
    gword_ref[0] = grad
    second = down(jnp.where(later, grad, 0.0))
    gedge_ref[6:7, :] += down(grad) - second
    gedge_ref[7:8, :] += second
    seat = lax.broadcasted_iota(i32, (seats_ref.shape[0], length), 0) == seat_ref[0]
    seat = seat.astype(bf16)
    high = grad.astype(bf16)
    low = (grad - high.astype(f32)).astype(bf16)
    collected = dot_plain(seat, high) + dot_plain(seat, low)
    if so_far:
        collected = collected + so_far[2][...]
    seats_ref[...] = collected.astype(seats_ref.dtype)
    if not direct:
        sums[4][...] += grad
        return
    devices = wide_ref.shape[0]
    high = devices // mp_count // 4
    share = length // devices
    base = wide_ref.shape[1] - share - 8
    for i in range(devices):
        slot = slot_of(i // mp_count, i % mp_count, high) ^ me
        wide_ref[slot, base : base + share, :] += grad[i * share : (i + 1) * share]
    if last:
        rows = [gedge_ref[i : i + 1, :] + late_ref[i : i + 1, :] for i in range(8)]
        rows += [late_ref[i : i + 1, :] for i in range(8, 11)]
        rows += [gtaps_ref[i : i + 1, :] for i in range(gtaps_ref.shape[0])]
        for i, row in enumerate(rows):
            slot = slot_of(i // mp_count, i % mp_count, high) ^ me
            wide_ref[slot, base + share : base + share + 1, 0 : row.shape[1]] = row
        kept_ref[...] = wide_ref[: devices // 2]
        sent_ref[...] = wide_ref[devices // 2 :]


def fixed(shape):
    return pl.BlockSpec(shape, lambda b, *_: (0,) * len(shape), pipeline_mode=pl.Buffered(1))


def each(shape, start=0):
    return pl.BlockSpec((1,) + shape, lambda b, *_: (b + start,) + (0,) * len(shape))


def run(kernel, scalars, ins, outs, scratch, name, steps, micros, aliases={}):
    return pl.pallas_call(
        kernel,
        out_shape=[jax.ShapeDtypeStruct(shape, dtype) for (shape, dtype), _ in outs],
        grid_spec=pltpu.PrefetchScalarGridSpec(
            num_scalar_prefetch=len(scalars),
            grid=(steps,),
            in_specs=[spec for _, spec in ins],
            out_specs=[spec for _, spec in outs],
            scratch_shapes=scratch,
        ),
        compiler_params=pltpu.CompilerParams(
            dimension_semantics=("arbitrary",), vmem_limit_bytes=VMEM
        ),
        input_output_aliases={len(scalars) + i: o for i, o in aliases.items()},
        cost_estimate=pl.CostEstimate(
            flops=micros * 1150000000, bytes_accessed=1 << 20, transcendentals=0
        ),
        name=name,
    )(*scalars, *[x for x, _ in ins])


def slots_of(ids, vblock, devices):
    owner = ids // vblock
    here = jnp.arange(ids.shape[0])
    same = ids[None, :] == ids[:, None]
    first = jnp.sum(jnp.logical_and(same, here[None, :] < here[:, None]), axis=1) == 0
    below = jnp.logical_and(owner[None, :] == owner[:, None], ids[None, :] < ids[:, None])
    rank = jnp.sum(jnp.logical_and(below, first[None, :]), axis=1).astype(i32)
    return owner, first, rank


def fetch_round(turn, capacity, devices, owner, first, rank, local, extra, low_table, hooks):
    slot = jnp.where(rank // capacity == turn, owner * capacity + rank % capacity, -1)
    seats = jnp.arange(devices * capacity)
    chosen = jnp.logical_and(seats[:, None] == slot[None, :], first[None, :])
    request = jnp.sum(jnp.where(chosen, local[None, :] + 1, 0), axis=1) - 1
    beside = jnp.concatenate([jnp.max(rank)[None], extra])
    beside = jnp.pad(beside, (0, -(capacity + beside.shape[0]) % 128))
    message = jnp.concatenate(
        [
            request.reshape(devices, capacity),
            jnp.broadcast_to(beside[None], (devices, beside.shape[0])),
        ],
        axis=1,
    )
    message = hooks[0](message)
    got = lax.all_to_all(message, ALL, 0, 0, tiled=True)
    asked = got[:, :capacity].reshape(-1)
    served = (asked[:, None] == jnp.arange(low_table.shape[0])[None, :]).astype(bf16)
    sending = dot_plain(served, low_table).astype(bf16)
    sending = hooks[1](sending)
    rows = lax.all_to_all(sending, ALL, 0, 0, tiled=True)
    mine = (slot[:, None] == seats[None, :]).astype(bf16)
    return dot_plain(mine, rows).astype(bf16), slot, mine, served, got[:, capacity:]


def body(
    token_ids,
    seg_split,
    lengths,
    mlm_pos,
    mlm_labels,
    sop_labels,
    owner,
    step_count,
    table,
    table_m,
    table_v,
    unit_master,
    unit_m,
    unit_v,
    small,
    small_m,
    small_v,
    taps,
    taps_m,
    taps_v,
):
    mp_count = lax.axis_size(MP)
    dp_count = lax.axis_size(DP)
    devices = mp_count * dp_count
    mp_index = lax.axis_index(MP)
    dp_index = lax.axis_index(DP)
    group_seqs, length = token_ids.shape
    width = small.shape[1]
    part = unit_master.shape[1]
    vblock = table.shape[0]
    cap_slots = unit_master.shape[0]
    matrices = owner.shape[0]
    seqs = group_seqs // mp_count
    tokens = seqs * length
    masks = mlm_pos.shape[1]
    total_seqs = group_seqs * dp_count
    count_all = total_seqs * masks

    def my(x):
        return lax.dynamic_slice_in_dim(x, mp_index * seqs, seqs, 0)

    token_ids, seg_split, lengths = my(token_ids), my(seg_split), my(lengths)
    mlm_pos, mlm_labels, sop_labels = my(mlm_pos), my(mlm_labels), my(sop_labels)

    earlier = jnp.arange(matrices)[:, None] > jnp.arange(matrices)[None, :]
    slot_rank = jnp.sum(jnp.logical_and(earlier, owner[:, None] == owner[None, :]), axis=1)
    slot_index = owner * cap_slots + slot_rank
    selector = jnp.logical_and(
        owner[None, :] == dp_index, slot_rank[None, :] == jnp.arange(cap_slots)[:, None]
    ).astype(f32)
    rest = part // dp_count
    own = seqs * masks
    low_slots = unit_master.astype(bf16).reshape(cap_slots, dp_count, rest, width)
    low_slots = jnp.moveaxis(low_slots, 1, 0)
    got_slots = lax.all_to_all(low_slots, DP, 0, 0, tiled=True)
    got_slots = got_slots.reshape(dp_count * cap_slots, rest, width)
    low_table = table.astype(bf16)

    ids = token_ids.reshape(-1)
    capacity = max(8, -(-1280 // devices))
    home, first, rank = slots_of(ids, vblock, devices)
    fetch = partial(
        fetch_round,
        capacity=capacity,
        devices=devices,
        owner=home,
        first=first,
        rank=rank,
        local=ids % vblock,
        extra=mlm_labels.reshape(-1),
        low_table=low_table,
    )
    shards = None

    def same(x):
        return x

    def after_slots(message):
        nonlocal shards
        message, got = together(message, got_slots)
        seats_at = slot_index[:, None] == jnp.arange(dp_count * cap_slots)[None, :]
        picked = jnp.sum(
            jnp.where(seats_at[:, :, None, None], got[None].astype(f32), 0.0), axis=1
        ).astype(bf16)
        shards = lax.all_gather(picked, DP, axis=0)
        return message

    def after_shards(sending):
        nonlocal shards
        sending, shards = together(sending, shards)
        return sending

    word_rows, slot, mine, served, beside = fetch(0, hooks=(after_slots, after_shards))
    turns = jnp.max(beside[:, 0]) // capacity + 1
    all_labels = near_labels(beside[:, 1 : 1 + own], own)

    shards = jnp.moveaxis(shards, 0, 1).reshape(matrices, part, width)
    first_units = lax.all_gather(shards[:3], MP, axis=0)
    last_units = spread_axis(shards[3:], "m1", 0)
    vocab = lax.all_gather(low_table, RG, axis=0, tiled=True)

    def more(state):
        return state[0] < turns

    def fetch_more(state):
        return (state[0] + 1, state[1] + fetch(state[0], hooks=(same, same))[0])

    _, word_rows = lax.while_loop(more, fetch_more, (jnp.int32(1), word_rows))
    word_rows, last_units = together(word_rows, last_units)
    last_units = spread_axis(last_units, "m0", 1).reshape(mp_count, -1, part, width)

    words_in = word_rows.reshape(seqs, length, width)
    places = small[6 : 6 + length]
    edge = jnp.concatenate([small[:6], small[6 + length : 8 + length]])
    span = (HEADS - FIRST) * DH
    taps_span = [
        taps[:, CONV.index(h) * DH : (CONV.index(h) + 1) * DH]
        if h in CONV
        else jnp.zeros((taps.shape[0], DH), f32)
        for h in range(FIRST, HEADS)
    ]
    taps_span = jnp.concatenate(taps_span, axis=1)
    act = (length, width)
    embedded, qkv, lse, heads = run(
        forward_heads,
        (seg_split, lengths),
        [
            (words_in, each(act)),
            (places, fixed(places.shape)),
            (edge, fixed(edge.shape)),
            (taps_span, fixed(taps_span.shape)),
            (first_units, fixed(first_units.shape)),
        ],
        [
            (((seqs,) + act, f32), each(act)),
            (((seqs, length, 3 * width), bf16), each((length, 3 * width))),
            (((seqs, length, 128), f32), each((length, 128))),
            (((seqs,) + act, bf16), each(act)),
        ],
        [pltpu.VMEM((length + 16, span), f32)],
        "forward_heads",
        seqs,
        20,
    )
    spots = mlm_pos[:, :, None]
    one, two, masked_rows, cls_rows = run(
        forward_ffn,
        (),
        [
            (spots, each((masks, 1))),
            (heads, each(act)),
            (embedded, each(act)),
            (edge, fixed(edge.shape)),
            (last_units, fixed(last_units.shape)),
        ],
        [
            (((seqs,) + act, f32), each(act)),
            (((seqs,) + act, f32), each(act)),
            (((seqs, masks, width), bf16), each((masks, width))),
            (((seqs, 8, width), f32), each((8, width))),
        ],
        [],
        "forward_ffn",
        seqs,
        23,
    )
    masked_rows = masked_rows.reshape(seqs * masks, width)

    all_masked = grow_parts(masked_rows)
    logits = dot_right(all_masked, vocab)
    block = all_labels // vblock
    at = {}
    for axis in ALL[::-1]:
        at[axis] = block % lax.axis_size(axis)
        block = block // lax.axis_size(axis)
    label_mine = jnp.ones_like(all_labels, dtype=bool)
    for axis in VG:
        label_mine = jnp.logical_and(label_mine, at[axis] == lax.axis_index(axis))
    label_block = at["d2"] * lax.axis_size("m0") + at["m0"]
    label_row = label_block * vblock + all_labels % vblock
    onehot = jnp.logical_and(
        jnp.arange(vocab.shape[0])[None, :] == label_row[:, None], label_mine[:, None]
    )
    top = jnp.max(logits, axis=1)
    total = jnp.sum(jnp.exp(logits - top[:, None]), axis=1)
    target = jnp.sum(jnp.where(onehot, logits, 0.0), axis=1)
    stats = merge_stats(jnp.stack([top, total, target]), own)
    log_sum = stats[0] + jnp.log(stats[1])
    losses = [p[0] for p in cut_parts(log_sum - stats[2], own)]
    mlm_part = sum(jnp.sum(p) for p in losses) / count_all
    grad_logits = (
        (jnp.exp(logits - log_sum[:, None]) - onehot.astype(f32)) / count_all
    ).astype(bf16)
    parts = cut_parts(dot_plain(grad_logits, vocab), own)
    for stage in reversed(range(len(VG))):
        parts = [shrink(p, order[stage]) for p, order in zip(parts, ORDERS)]
        if stage == len(VG) - 1:
            grad_logits, *parts = together(grad_logits, *parts)
            grad_table = dot_left(grad_logits, all_masked)
    grad_masked = jnp.concatenate([p[0] for p in parts])
    grad_masked, grad_table = together(grad_masked, grad_table)
    grad_table = lax.psum_scatter(grad_table, RG, scatter_dimension=0, tiled=True)
    sop_part, sop_pull = jax.vjp(
        partial(sop_loss, labels=sop_labels, denom=total_seqs),
        cls_rows[:, 0],
        small[8 + length :],
    )
    grad_cls, grad_pair = sop_pull(jnp.ones((), f32))
    grad_cls = jnp.pad(grad_cls[:, None], ((0, 0), (0, 7), (0, 0)))
    direct = rest % 8 == 0 and length % (8 * devices) == 0 and devices >= 20
    share = length // devices if direct else -(-length // devices)
    me = slot_of(dp_index, mp_index, dp_count // 4)[None].astype(i32)

    def wide(many, extra):
        if direct:
            return (devices, many * rest + extra, width)
        return (mp_count, many, part, width)

    def wide_outs(many, extra):
        shape = wide(many, extra)
        if direct:
            shape = (shape[0] // 2,) + shape[1:]
        return [((shape, f32), fixed(shape))] * (2 if direct else 1)

    sum_one, grad_heads, edge_last, *wide_last = run(
        backward_ffn,
        (me,),
        [
            (spots, each((masks, 1))),
            (grad_masked.reshape(seqs, masks, width), each((masks, width))),
            (grad_cls, each((8, width))),
            (one, each(act)),
            (two, each(act)),
            (heads, each(act)),
            (edge, fixed(edge.shape)),
            (last_units, fixed(last_units.shape)),
        ],
        [
            (((seqs,) + act, f32), each(act)),
            (((seqs,) + act, bf16), each(act)),
            ((edge.shape, f32), fixed(edge.shape)),
        ]
        + wide_outs(5, 0),
        [pltpu.VMEM(wide(5, 0), f32)] if direct else [],
        "backward_ffn",
        seqs,
        46,
    )
    names = ["m0", "d0", "m1", "d1", "d2"]
    sizes = tuple(lax.axis_size(a) for a in names)

    def near(x):
        x = x.reshape(tuple(lax.axis_size(a) for a in ALL) + x.shape[1:])
        x = jnp.transpose(x, [ALL.index(a) for a in names] + list(range(5, x.ndim)))
        for dim, axis in enumerate(names):
            for bit in range(bits_of(axis)):
                lead, tail = x.shape[:dim], x.shape[dim + 1 :]
                y = x.reshape(lead + (x.shape[dim] >> (bit + 1), 2, 1 << bit) + tail)
                flipped = jnp.flip(y, axis=dim + 1)
                x = jnp.where(bit_of(axis, bit) == 1, flipped, y).reshape(x.shape)
        return x

    def by_device(x):
        x = x.reshape(mp_count, -1, dp_count, rest, width)
        return jnp.transpose(x, (2, 0, 1, 3, 4)).reshape(devices, -1, width)

    tracks = (["d0", "m1", "d1", "d2"], ["m1", "d0", "d1", "d2"])

    def pair_of(kept, sent):
        x = kept + swap(sent, "m0", 0)
        x = x.reshape(sizes[1:] + x.shape[1:])
        return [x[..., : width // 2], x[..., width // 2 :]]

    def fold_stage(pair, stage):
        done = []
        for x, track in zip(pair, tracks):
            left = [a for a in names[1:] if a not in track[:stage]]
            done.append(fold_near(x, track[stage], left.index(track[stage])))
        return done

    loss_row = jnp.pad(jnp.reshape(mlm_part + sop_part, (1, 1)), ((0, 0), (0, width - 1)))
    late = jnp.concatenate([edge_last, grad_pair, loss_row])
    late = jnp.pad(late, ((0, 16 - late.shape[0]), (0, 0)))
    seat_rows = slot.reshape(seqs, 1, length)
    seat_count = (devices * capacity, width)
    ways = wide(3, share + 8)

    def heads_call(start, sums, back):
        last = start == seqs - 1
        some = [
            (words_in, each(act, start)),
            (places, fixed(places.shape)),
            (edge, fixed(edge.shape)),
            (taps_span, fixed(taps_span.shape)),
            (first_units, fixed(first_units.shape)),
            (qkv, each((length, 3 * width), start)),
            (lse, each((length, 128), start)),
            (back, each(act, start)),
            (sum_one, each(act, start)),
            (seat_rows, each((1, length), start)),
            (late, fixed(late.shape)),
        ]
        count = len(some)
        outs = [
            (((1,) + act, f32), each(act)),
            ((edge.shape, f32), fixed(edge.shape)),
            ((taps_span.shape, f32), fixed(taps_span.shape)),
            ((seat_count, bf16 if last else f32), fixed(seat_count)),
        ]
        scratch = [pltpu.VMEM((length + 16, span), f32)] * 2
        kept_whole = [0, 1, 3, 4]
        if direct and last:
            outs += wide_outs(3, share + 8)
            scratch.append(pltpu.VMEM(ways, f32))
            kept_whole = [0, 1]
        else:
            outs.append(((ways, f32), fixed(ways)))
        if not direct:
            outs.append(((act, f32), fixed(act)))
        return run(
            partial(backward_heads, start, last, direct),
            (seg_split, lengths, me),
            some + [(x, fixed(x.shape)) for x in sums],
            outs,
            scratch,
            "backward_heads",
            1,
            33,
            {count + i: 1 + i for i in range(len(sums)) if i in kept_whole},
        )

    if not direct:
        wide_last = near(by_device(wide_last[0])).reshape(2, devices // 2, -1, width)
    pair_last = pair_of(*wide_last)
    back = grad_heads
    grad_words, sums = [], []
    for start in range(seqs):
        if start == 1:
            back, *pair_last = together(back, *pair_last)
            pair_last = fold_stage(pair_last, 0)
        word, *sums = heads_call(start, sums, back)
        grad_words.append(word.reshape(length, width))
    if seqs == 1:
        pair_last = fold_stage(pair_last, 0)
    edge_first, grad_taps, sent, *wide_first = sums
    if not direct:
        rows = jnp.pad(wide_first[1], ((0, share * devices - length), (0, 0)))
        tops = jnp.pad(grad_taps, ((0, 0), (0, width - span)))
        small_rows = jnp.concatenate([edge_first + late[:8], late[8:11], tops])
        small_rows = jnp.pad(small_rows, ((0, devices - small_rows.shape[0]), (0, 0)))
        small_rows = jnp.pad(small_rows[:, None], ((0, 0), (0, 7), (0, 0)))
        rows = rows.reshape(devices, share, width)
        wide_first = near(
            jnp.concatenate([by_device(wide_first[0]), rows, small_rows], axis=1)
        ).reshape(2, devices // 2, -1, width)

    sent, a, b, *pair_last = together(sent, *wide_first, *pair_last)
    wide_first = [a, b]
    words = dot_left(served, lax.all_to_all(sent, ALL, 0, 0, tiled=True))

    def return_more(state):
        _, _, mine_r, served_r, _ = fetch(state[0], hooks=(same, same))
        live = (state[0] > 0).astype(f32)
        sent_r = sum(
            select_sum(mine_r[at * length : (at + 1) * length], g * live)
            for at, g in enumerate(grad_words)
        ).astype(bf16)
        got = lax.all_to_all(sent_r, ALL, 0, 0, tiled=True)
        return (state[0] + 1, state[1] + dot_left(served_r, got))

    grad_table, *pair_first = together(grad_table, *pair_of(*wide_first))
    pair_last = fold_stage(pair_last, 1)
    pair_first = fold_stage(pair_first, 0)
    pair_last = fold_stage(pair_last, 2)
    pair_first = fold_stage(pair_first, 1)
    _, words = lax.while_loop(more, return_more, (jnp.int32(1), words))
    grad_table_own = grad_table + words
    square = jnp.sum(grad_table_own * grad_table_own)
    square, *pair_first = together(square, *pair_first)
    pair_last = fold_stage(pair_last, 3)
    pair_first = fold_stage(pair_first, 2)
    pair_first = fold_stage(pair_first, 3)
    piece_first = jnp.concatenate(pair_first, axis=-1)
    pieces_last = jnp.concatenate(pair_last, axis=-1)
    summed = jnp.concatenate([piece_first[: 3 * rest], pieces_last]).reshape(-1, rest, width)
    seat = (slot_index[None, :] == jnp.arange(dp_count * cap_slots)[:, None]).astype(f32)
    slotted = sum(seat[:, k, None, None] * summed[k][None] for k in range(matrices))
    slotted = slotted.reshape(dp_count, cap_slots, rest, width)
    grad_slots = lax.all_to_all(slotted, DP, 0, 0, tiled=True)
    grad_slots = jnp.moveaxis(grad_slots, 0, 1).reshape(cap_slots, part, width)

    lone_row = piece_first[3 * rest + share]
    loss_at = lax.axis_index(ALL) == 10
    square = (
        square
        + jnp.sum(summed * summed)
        + jnp.sum(piece_first[3 * rest : 3 * rest + share] ** 2)
        + jnp.where(loss_at, 0.0, jnp.sum(lone_row * lone_row))
    )
    row = jnp.arange(share + 8)[:, None] == share + 1
    pieces = jnp.where(row, square, piece_first[3 * rest :])
    for axis in ("d2", "d1", "d0"):
        pieces = spread_axis(pieces, axis, {"d2": 0, "d1": 1, "d0": 2}[axis])
    for axis in ("m1", "m0"):
        pieces = spread_axis(pieces, axis, {"m1": 3, "m0": 4}[axis])
    pieces = pieces.reshape(devices, share + 8, width)
    place_sum = pieces[:, :share].reshape(-1, width)[:length]
    lone = pieces[:, share]
    small_sum = jnp.concatenate([lone[:6], place_sum, lone[6:10]])
    taps_rows = lone[11 : 11 + taps.shape[0], :span]
    taps_sum = jnp.concatenate(
        [taps_rows[:, (h - FIRST) * DH : (h - FIRST + 1) * DH] for h in CONV], axis=1
    )
    loss = lone[10, 0]
    grad_norm = jnp.sqrt(jnp.sum(pieces[:, share + 1, 0]))
    scale = clip_bound / jnp.maximum(grad_norm, clip_bound)
    count = step_count[0].astype(f32)
    table_new, table_m_new, table_v_new = adam(
        table, table_m, table_v, grad_table_own * scale, count
    )
    used = jnp.sum(selector, axis=1)[:, None, None]
    unit_new, unit_m_new, unit_v_new = adam(unit_master, unit_m, unit_v, grad_slots * scale, count)
    unit_new = unit_new * used
    unit_m_new = unit_m_new * used
    unit_v_new = unit_v_new * used
    small_new, small_m_new, small_v_new = adam(small, small_m, small_v, small_sum * scale, count)
    taps_new, taps_m_new, taps_v_new = adam(taps, taps_m, taps_v, taps_sum * scale, count)
    return (
        loss,
        grad_norm,
        table_new,
        table_m_new,
        table_v_new,
        table_new.astype(bf16),
        unit_new,
        unit_m_new,
        unit_v_new,
        unit_new.astype(bf16),
        small_new,
        small_m_new,
        small_v_new,
        taps_new,
        taps_m_new,
        taps_v_new,
    )


def solution(mesh):
    dp, mp = mesh.devices.shape
    fine = Mesh(mesh.devices.reshape(dp // 4, 2, 2, mp // 2, 2), ALL)
    rows = P(DP)
    vocab = P(ALL)
    slots = P(DP, MP)
    placed = (rows,) * 6 + (P(),) * 2 + (vocab,) * 3 + (slots,) * 3 + (P(),) * 6
    return jax.shard_map(
        body,
        mesh=fine,
        in_specs=placed,
        out_specs=(P(),) * 2 + (vocab,) * 4 + (slots,) * 4 + (P(),) * 6,
        check_vma=False,
    )
```

```python
import math
from functools import partial

import jax
import jax.numpy as jnp
from jax import lax
from jax.experimental import pallas as pl
from jax.experimental.pallas import tpu as pltpu
from jax.sharding import Mesh, PartitionSpec as P

DH = 64
HEADS = 12
PER = 3
ATTN = tuple(h for h in range(HEADS) if h % PER < PER - h // PER)
CONV = tuple(h for h in range(HEADS) if h % PER >= PER - h // PER)

FIRST = min(CONV) // 2 * 2

DP = ("d2", "d1", "d0")
MP = ("m1", "m0")
ALL = DP + MP
CHIPS = DP + ("m1",)
VG = ("d1", "d0", "m1")
RG = ("d2", "m0")
ORDERS = (("d1", "d0", "m1"), ("d0", "m1", "d1"), ("m1", "d1", "d0"))

f32 = jnp.float32
bf16 = jnp.bfloat16
i32 = jnp.int32
highest = lax.Precision.HIGHEST
beta_one = 0.9
beta_two = 0.999
adam_eps = 1e-08
learn_rate = 0.03
weight_decay = 0.01
clip_bound = 0.02
norm_eps = 1e-06
VMEM = 60 << 20


def dot_right(left, right):
    return lax.dot_general(left, right, (((1,), (1,)), ((), ())), preferred_element_type=f32)


def dot_left(left, right):
    return lax.dot_general(left, right, (((0,), (0,)), ((), ())), preferred_element_type=f32)


def dot_plain(left, right):
    return lax.dot_general(left, right, (((1,), (0,)), ((), ())), preferred_element_type=f32)


def halves(x):
    high = lax.reduce_precision(x, 8, 7)
    return high.astype(bf16), (x - high).astype(bf16)


def select_sum(chosen, values):
    high, low = halves(values)
    return dot_left(chosen, high) + dot_left(chosen, low)


def sop_loss(cls_rows, pair, labels, denom):
    logits = jnp.dot(cls_rows, pair.T, precision=highest)
    chosen = jnp.take_along_axis(logits, labels[:, None], axis=1)[:, 0]
    return jnp.sum(jax.nn.logsumexp(logits, axis=-1) - chosen) / denom


def adam(weight, first, second, grad, count):
    first_new = beta_one * first + (1.0 - beta_one) * grad
    second_new = beta_two * second + (1.0 - beta_two) * grad * grad
    corr_one = 1.0 - jnp.power(beta_one, count)
    corr_two = 1.0 - jnp.power(beta_two, count)
    step = first_new / corr_one / (jnp.sqrt(second_new / corr_two) + adam_eps)
    return (weight - learn_rate * (step + weight_decay * weight), first_new, second_new)


def everyone(x, axes):
    count = lax.axis_size(axes)
    return lax.all_to_all(jnp.broadcast_to(x, (count,) + x.shape), axes, 0, 0, tiled=True)


def swap(x, axis, bit):
    count = lax.axis_size(axis)
    return lax.ppermute(x, axis, [(i, i ^ (1 << bit)) for i in range(count)])


def bits_of(axis):
    return lax.axis_size(axis).bit_length() - 1


def together(*arrays):
    return lax.optimization_barrier(arrays)


def bit_of(axis, bit):
    return (lax.axis_index(axis) >> bit) & 1


def fold_near(x, axis, dim, beside=()):
    for bit in reversed(range(bits_of(axis))):
        lead, rest = x.shape[:dim], x.shape[dim + 1 :]
        x = x.reshape(lead + (2, x.shape[dim] // 2) + rest)
        sent = lax.index_in_dim(x, 1, dim, False)
        kept = lax.index_in_dim(x, 0, dim, False)
        if beside:
            kept, *beside = together(kept, *beside)
        x = kept + swap(sent, axis, bit)
    return (x.reshape(x.shape[:dim] + x.shape[dim + 1 :]), *beside)


def slot_of(d, m, high):
    return ((((m & 1) * 2 + (d & 1)) * 2 + (m >> 1)) * 2 + ((d >> 1) & 1)) * high + (d >> 2)


def spread_axis(x, axis, dim):
    x = jnp.expand_dims(x, dim)
    for bit in range(bits_of(axis)):
        other = swap(x, axis, bit)
        me = bit_of(axis, bit) == 1
        x = jnp.concatenate([jnp.where(me, other, x), jnp.where(me, x, other)], axis=dim)
    return x


def grow(x, axis):
    for bit in range(bits_of(axis)):
        x = jnp.concatenate([x, swap(x, axis, bit)], axis=0)
    return x


def shrink(x, axis):
    for bit in reversed(range(bits_of(axis))):
        half = x.shape[0] // 2
        x = x[:half] + swap(x[half:], axis, bit)
    return x


def row_parts(count):
    most = -(-count // (8 * len(ORDERS))) * 8
    return [slice(at, min(at + most, count)) for at in range(0, count, most)]


def grow_parts(x):
    parts = [x[None, rows] for rows in row_parts(x.shape[0])]
    for stage in range(len(VG)):
        parts = [grow(p, order[stage]) for p, order in zip(parts, ORDERS)]
    return jnp.concatenate([p.reshape((-1,) + p.shape[2:]) for p in parts])


def cut_parts(x, count, dim=0):
    pieces, at = [], 0
    for rows in row_parts(count):
        size = (rows.stop - rows.start) << len(VG)
        piece = lax.slice_in_dim(x, at, at + size, axis=dim)
        pieces.append(piece.reshape(x.shape[:dim] + (1 << len(VG), -1) + x.shape[dim + 1 :]))
        at += size
    return pieces


def near_labels(got, own):
    x = got.reshape(tuple(lax.axis_size(a) for a in ALL) + (own,))
    x = lax.dynamic_index_in_dim(x, lax.axis_index("m0"), 4, False)
    x = lax.dynamic_index_in_dim(x, lax.axis_index("d2"), 0, False)
    for dim, axis in enumerate(VG):
        x = jnp.where(lax.axis_index(axis) == 1, jnp.flip(x, axis=dim), x)
    parts = []
    for rows, order in zip(row_parts(own), ORDERS):
        dims = [VG.index(axis) for axis in order[::-1]]
        parts.append(jnp.transpose(x[..., rows], dims + [len(VG)]).reshape(-1))
    return jnp.concatenate(parts)


def merge_stats(stats, count):
    for axis in VG:
        other = swap(stats, axis, 0)
        flipped = []
        for p, order in zip(cut_parts(other, count, 1), ORDERS):
            low = 1 << order.index(axis)
            y = p.reshape(3, p.shape[1] // (2 * low), 2, low, p.shape[2])
            flipped.append(jnp.flip(y, axis=2).reshape(3, -1))
        other = jnp.concatenate(flipped, axis=1)
        top = jnp.maximum(stats[0], other[0])
        total = stats[1] * jnp.exp(stats[0] - top) + other[1] * jnp.exp(other[0] - top)
        stats = jnp.stack([top, total, stats[2] + other[2]])
    return stats


def rows_norm(x):
    center = jnp.mean(x, axis=-1, keepdims=True)
    shifted = x - center
    inv = lax.rsqrt(jnp.mean(shifted * shifted, axis=-1, keepdims=True) + norm_eps)
    return shifted * inv, inv


def erf(x):
    x = jnp.clip(x, -3.832506856900711, 3.832506856900711)
    y = x * x
    top = jnp.float32(0.00022905065861350646)
    for c in (0.0034082910107109506, 0.050955695062380861, 0.18520832239976145, 1.128379143519084):
        top = top * y + c
    low = jnp.float32(-1.1791602954361697e-7)
    for c in (
        0.000023547966471313185,
        0.0010179625278914885,
        0.014070470171167667,
        0.11098505178285362,
        0.49746925110067538,
        1.0,
    ):
        low = low * y + c
    return x * top / low


def head_mask(rows, groups):
    row = lax.broadcasted_iota(i32, (rows, groups * DH), 0)
    col = lax.broadcasted_iota(i32, (rows, groups * DH), 1)
    return lax.rem(row, groups) == lax.div(col, DH)


def split3(x):
    a = x.astype(bf16)
    r = x - a.astype(f32)
    b = r.astype(bf16)
    c = (r - b.astype(f32)).astype(bf16)
    return a, b, c


def dot_exact(a, b, dims):
    return lax.dot_general(a, b, (dims, ((), ())), precision=highest, preferred_element_type=f32)


def conv_kernel_rows(prod, taps_ref, groups):
    width = taps_ref.shape[0]
    spread = jnp.concatenate(
        [jnp.broadcast_to(taps_ref[o : o + 1, :], (groups, prod.shape[1])) for o in range(width)], axis=0
    )
    spread = jnp.where(head_mask(width * groups, groups), spread, 0.0)
    logits = dot_exact(spread, prod, ((1,), (1,)))
    parts = [logits[o * groups : (o + 1) * groups] for o in range(width)]
    top = parts[0]
    for p in parts[1:]:
        top = jnp.maximum(top, p)
    weights = [jnp.exp(p - top) for p in parts]
    total = weights[0]
    for w in weights[1:]:
        total = total + w
    inv = 1.0 / total
    return [w * inv for w in weights], spread


def spread_rows(rows, groups):
    three = jnp.concatenate(split3(rows), axis=0)
    ones = head_mask(3 * groups, groups).astype(bf16)
    return lax.dot_general(three, ones, (((0,), (0,)), ((), ())), preferred_element_type=f32)


def forward_heads(
    split_ref, length_ref, word_ref, places_ref, edge_ref, taps_ref, units_ref,
    emb_ref, qkv_ref, lse_ref, heads_ref, pad_ref,
):
    at = pl.program_id(0)
    length, width = word_ref.shape[1:]
    later = lax.broadcasted_iota(i32, (length, 1), 0) > split_ref[at]
    summed = word_ref[0].astype(f32) + places_ref[...]
    summed = summed + jnp.where(later, edge_ref[7:8, :], edge_ref[6:7, :])
    normed, _ = rows_norm(summed)
    embedded = normed * edge_ref[0:1, :] + edge_ref[3:4, :]
    emb_ref[0] = embedded
    low_in = embedded.astype(bf16)
    for k in range(3):
        unit = whole_unit(units_ref, k)
        qkv_ref[0, :, k * width : (k + 1) * width] = dot_right(low_in, unit).astype(bf16)
    allowed = lax.broadcasted_iota(i32, (length, length), 1) < length_ref[at]
    lanes = lax.broadcasted_iota(i32, (length, 128), 1)
    lse = jnp.zeros((length, 128), f32)
    outs = {}
    for n, h in enumerate(ATTN):
        q = qkv_ref[0, :, h * DH : (h + 1) * DH]
        k = qkv_ref[0, :, width + h * DH : width + (h + 1) * DH]
        v = qkv_ref[0, :, 2 * width + h * DH : 2 * width + (h + 1) * DH]
        scores = jnp.where(allowed, dot_right(q, k) * (1.0 / math.sqrt(DH)), -1e30)
        top = jnp.max(scores, axis=1, keepdims=True)
        weights = jnp.exp(scores - top)
        total = jnp.sum(weights, axis=1, keepdims=True)
        probs = (weights * (1.0 / total)).astype(bf16)
        outs[h] = dot_plain(probs, v).astype(bf16)
        lse = jnp.where(lanes == n, top + jnp.log(total), lse)
    lse_ref[0] = lse
    groups = HEADS - FIRST
    base = FIRST * DH
    q = qkv_ref[0, :, base:width].astype(f32)
    k = qkv_ref[0, :, width + base : 2 * width].astype(f32)
    kernel, _ = conv_kernel_rows(q * k, taps_ref, groups)
    taps = len(kernel)
    pad_ref[0:8, :] = jnp.zeros((8, width - base), f32)
    pad_ref[8 + length : 16 + length, :] = jnp.zeros((8, width - base), f32)
    pad_ref[8 : 8 + length, :] = qkv_ref[0, :, 2 * width + base :].astype(f32)
    total = jnp.zeros((length, width - base), f32)
    for o in range(taps):
        start = 8 + o - taps // 2
        total = total + spread_rows(kernel[o], groups) * pad_ref[start : start + length, :]
    total = total.astype(bf16)
    for h in CONV:
        outs[h] = total[:, (h - FIRST) * DH : (h - FIRST + 1) * DH]
    heads_ref[0] = jnp.concatenate([outs[h] for h in range(HEADS)], axis=1)


def ffn_weights(units_ref, s, first):
    at = units_ref.at[s % 2, s // 2]
    return jnp.concatenate([at[first], at[first + 1]], axis=0)


def whole_unit(units_ref, k):
    count = units_ref.shape[0] * units_ref.shape[1]
    return jnp.concatenate([units_ref[s % 2, s // 2, k] for s in range(count)], axis=0)


def forward_ffn(
    pos_ref, heads_ref, emb_ref, edge_ref, units_ref, one_ref, two_ref, mask_ref, cls_ref
):
    length, width = emb_ref.shape[1:]
    part = units_ref.shape[3]
    unit = whole_unit(units_ref, 0)
    projected = dot_right(heads_ref[0], unit).astype(bf16).astype(f32)
    one = emb_ref[0] + projected
    one_ref[0] = one
    normed, _ = rows_norm(one)
    attended = normed * edge_ref[1:2, :] + edge_ref[4:5, :]
    low_mid = attended.astype(bf16)
    for g in range(2):
        cols = slice(2 * part * g, 2 * part * (g + 1))
        total = None
        for s in (2 * g, 2 * g + 1):
            pre = dot_plain(low_mid[:, cols], ffn_weights(units_ref, s, 1))
            hidden = (pre * (0.5 + 0.5 * erf(pre * math.sqrt(0.5)))).astype(bf16)
            out = dot_right(hidden, ffn_weights(units_ref, s, 3))
            total = out if total is None else total + out
        two_ref[0, :, cols] = attended[:, cols] + total
    normed, _ = rows_norm(two_ref[0])
    final = normed * edge_ref[2:3, :] + edge_ref[5:6, :]
    masks = mask_ref.shape[1]
    picked = lax.broadcasted_iota(i32, (masks, length), 1) == pos_ref[0][:, 0:1]
    mask_ref[0] = dot_plain(picked.astype(bf16), final.astype(bf16)).astype(bf16)
    cls_ref[0] = final[0:8]


def norm_grad(grad, normed, inv, gain):
    scaled = grad * gain
    mean = jnp.mean(scaled, axis=-1, keepdims=True)
    along = jnp.mean(scaled * normed, axis=-1, keepdims=True)
    return inv * (scaled - mean - normed * along)


def down(x):
    return jnp.sum(x, axis=0, keepdims=True)


def add_rows(ref, me, mp_count, at, matrix, rows):
    if len(ref.shape) == 4:
        ref[at, matrix] += rows
        return
    dp_count = ref.shape[0] // mp_count
    rest = rows.shape[0] // dp_count
    here = slice(matrix * rest, (matrix + 1) * rest)
    for d in range(dp_count):
        ref[slot_of(d, at, dp_count // 4) ^ me, here, :] += rows[d * rest : (d + 1) * rest]


def backward_ffn(
    me_ref, pos_ref, grad_ref, cls_ref, one_ref, two_ref, heads_ref, edge_ref, units_ref,
    sum_ref, back_ref, edges_ref, *wide_refs,
):
    at = pl.program_id(0)
    wide_ref = wide_refs[-1]
    length, width = one_ref.shape[1:]
    mp_count, part = units_ref.shape[0] * units_ref.shape[1], units_ref.shape[3]

    @pl.when(at == 0)
    def _():
        wide_ref[...] = jnp.zeros_like(wide_ref)
        edges_ref[...] = jnp.zeros_like(edges_ref)

    masks = grad_ref.shape[1]
    picked = (lax.broadcasted_iota(i32, (masks, length), 1) == pos_ref[0][:, 0:1]).astype(bf16)
    high = grad_ref[0].astype(bf16)
    low = (grad_ref[0] - high.astype(f32)).astype(bf16)
    grad = dot_left(picked, high) + dot_left(picked, low)
    rows = lax.broadcasted_iota(i32, (length, 1), 0)
    grad = grad + jnp.where(rows == 0, cls_ref[0][0:1, :], 0.0)
    normed, inv = rows_norm(two_ref[0])
    edges_ref[2:3, :] += down(grad * normed)
    edges_ref[5:6, :] += down(grad)
    grad_two = norm_grad(grad, normed, inv, edge_ref[2:3, :])
    low_two = grad_two.astype(bf16)
    normed, inv = rows_norm(one_ref[0])
    low_mid = (normed * edge_ref[1:2, :] + edge_ref[4:5, :]).astype(bf16)
    backs = []
    for g in range(2):
        cols = slice(2 * part * g, 2 * part * (g + 1))
        total = None
        for s in (2 * g, 2 * g + 1):
            w_in = ffn_weights(units_ref, s, 1)
            w_out = ffn_weights(units_ref, s, 3)
            pre = dot_plain(low_mid[:, cols], w_in)
            half = 0.5 + 0.5 * erf(pre * math.sqrt(0.5))
            hidden = (pre * half).astype(bf16)
            slope = half + pre * (jnp.exp(-0.5 * pre * pre) * (1.0 / math.sqrt(2.0 * math.pi)))
            grad_hidden = dot_plain(low_two[:, cols], w_out)
            w = dot_left(low_two[:, cols], hidden)
            add_rows(wide_ref, me_ref[0], mp_count, s, 3, w[:part])
            add_rows(wide_ref, me_ref[0], mp_count, s, 4, w[part:])
            grad_pre = (grad_hidden * slope).astype(bf16)
            w = dot_left(low_mid[:, cols], grad_pre)
            add_rows(wide_ref, me_ref[0], mp_count, s, 1, w[:part])
            add_rows(wide_ref, me_ref[0], mp_count, s, 2, w[part:])
            back = dot_right(grad_pre, w_in)
            total = back if total is None else total + back
        backs.append(total)
    grad = grad_two + jnp.concatenate(backs, axis=1)
    edges_ref[1:2, :] += down(grad * normed)
    edges_ref[4:5, :] += down(grad)
    grad_one = norm_grad(grad, normed, inv, edge_ref[1:2, :])
    sum_ref[0] = grad_one
    low_one = grad_one.astype(bf16)
    w = dot_left(low_one, heads_ref[0])
    for s in range(mp_count):
        add_rows(wide_ref, me_ref[0], mp_count, s, 0, w[s * part : (s + 1) * part])
    unit = whole_unit(units_ref, 0)
    back_ref[0] = dot_plain(low_one, unit).astype(bf16)

    if len(wide_refs) > 1:

        @pl.when(at == pl.num_programs(0) - 1)
        def _():
            half = wide_ref.shape[0] // 2
            wide_refs[0][...] = wide_ref[:half]
            wide_refs[1][...] = wide_ref[half:]


def backward_heads(start, last, direct, *refs):
    (split_ref, length_ref, me_ref, word_ref, places_ref, edge_ref, taps_ref, units_ref) = refs[:8]
    (qkv_ref, lse_ref, back_ref, sum_ref, seat_ref, late_ref) = refs[8:14]
    refs = refs[14:]
    so_far = []
    if start > 0:
        count = 4 if direct else 5
        so_far, refs = refs[:count], refs[count:]
    gword_ref, gedge_ref, gtaps_ref, seats_ref = refs[:4]
    if direct and last:
        kept_ref, sent_ref, pad_ref, shift_ref, wide_ref = refs[4:]
        sums = [gedge_ref, gtaps_ref, seats_ref, wide_ref]
    else:
        *sums, pad_ref, shift_ref = refs[1:]
        wide_ref = sums[3]
    at = pl.program_id(0) + start
    me = me_ref[0]
    mp_count = units_ref.shape[0] * units_ref.shape[1]
    length, width = word_ref.shape[1:]
    for n, new in enumerate(sums):
        if n != 2:
            new[...] = so_far[n][...] if so_far else jnp.zeros_like(new)

    groups = HEADS - FIRST
    base = FIRST * DH
    span = width - base
    q = qkv_ref[0, :, base:width].astype(f32)
    k = qkv_ref[0, :, width + base : 2 * width].astype(f32)
    prod = q * k
    kernel, spread = conv_kernel_rows(prod, taps_ref, groups)
    taps = len(kernel)
    out = back_ref[0, :, base:].astype(f32)
    pad_ref[0:8, :] = jnp.zeros((8, span), f32)
    pad_ref[8 + length : 16 + length, :] = jnp.zeros((8, span), f32)
    pad_ref[8 : 8 + length, :] = qkv_ref[0, :, 2 * width + base :].astype(f32)
    shift_ref[0:8, :] = jnp.zeros((8, span), f32)
    shift_ref[8 + length : 16 + length, :] = jnp.zeros((8, span), f32)
    grad_values = jnp.zeros((length, span), f32)
    lanes = 128
    dots = jnp.zeros((length, lanes), f32)
    column = lax.broadcasted_iota(i32, (span, lanes), 0)
    lane = lax.broadcasted_iota(i32, (span, lanes), 1)
    for o in range(taps):
        start = 8 + o - taps // 2
        moved = out * pad_ref[start : start + length, :]
        high = moved.astype(bf16)
        low = (moved - high.astype(f32)).astype(bf16)
        ones = (lane == o * groups + lax.div(column, DH)).astype(bf16)
        dots = dots + dot_plain(high, ones) + dot_plain(low, ones)
        shift_ref[8 : 8 + length, :] = spread_rows(kernel[o], groups) * out
        back = 8 + taps // 2 - o
        grad_values = grad_values + shift_ref[back : back + length, :]
    dots = dots.T
    parts = [dots[o * groups : (o + 1) * groups] for o in range(taps)]
    along = kernel[0] * parts[0]
    for o in range(1, taps):
        along = along + kernel[o] * parts[o]
    grad_logits = jnp.concatenate([kernel[o] * (parts[o] - along) for o in range(taps)], axis=0)
    grad_prod = dot_exact(grad_logits, spread, ((0,), (0,)))
    grad_taps = dot_exact(grad_logits, prod, ((1,), (0,)))
    head = lax.div(lax.broadcasted_iota(i32, (taps * groups, span), 1), DH) + FIRST
    real = head_mask(taps * groups, groups)
    for h in range(FIRST, HEADS):
        if h not in CONV:
            real = jnp.logical_and(real, head != h)
    grad_taps = jnp.where(real, grad_taps, 0.0)
    for o in range(taps):
        gtaps_ref[o : o + 1, :] += down(grad_taps[o * groups : (o + 1) * groups])
    grads = [(grad_prod * k).astype(bf16), (grad_prod * q).astype(bf16), grad_values.astype(bf16)]
    pieces = [[None] * HEADS for _ in range(3)]
    for h in CONV:
        for n in range(3):
            pieces[n][h] = grads[n][:, (h - FIRST) * DH : (h - FIRST + 1) * DH]

    allowed = lax.broadcasted_iota(i32, (length, length), 1) < length_ref[at]
    scale = 1.0 / math.sqrt(DH)
    for n, h in enumerate(ATTN):
        qh = qkv_ref[0, :, h * DH : (h + 1) * DH]
        kh = qkv_ref[0, :, width + h * DH : width + (h + 1) * DH]
        vh = qkv_ref[0, :, 2 * width + h * DH : 2 * width + (h + 1) * DH]
        gh = back_ref[0, :, h * DH : (h + 1) * DH]
        scores = jnp.where(allowed, dot_right(qh, kh) * scale, -1e30)
        probs = jnp.exp(scores - lse_ref[0][:, n : n + 1])
        grad_probs = dot_right(gh, vh)
        total = jnp.sum(probs * grad_probs, axis=1, keepdims=True)
        grad_scores = (probs * (grad_probs - total)).astype(bf16)
        pieces[0][h] = (dot_plain(grad_scores, kh) * scale).astype(bf16)
        pieces[1][h] = (dot_left(grad_scores, qh) * scale).astype(bf16)
        pieces[2][h] = dot_left(probs.astype(bf16), gh).astype(bf16)
    later = lax.broadcasted_iota(i32, (length, 1), 0) > split_ref[at]
    summed = word_ref[0].astype(f32) + places_ref[...]
    summed = summed + jnp.where(later, edge_ref[7:8, :], edge_ref[6:7, :])
    normed, inv = rows_norm(summed)
    low_in = (normed * edge_ref[0:1, :] + edge_ref[3:4, :]).astype(bf16)
    grad = sum_ref[0]
    for n in range(3):
        g = jnp.concatenate(pieces[n], axis=1)
        w = dot_left(g, low_in)
        part = units_ref.shape[3]
        for s in range(mp_count):
            add_rows(wide_ref, me, mp_count, s, n, w[s * part : (s + 1) * part])
        grad = grad + dot_plain(g, whole_unit(units_ref, n))
    gedge_ref[0:1, :] += down(grad * normed)
    gedge_ref[3:4, :] += down(grad)
    grad = norm_grad(grad, normed, inv, edge_ref[0:1, :])
    gword_ref[0] = grad
    second = down(jnp.where(later, grad, 0.0))
    gedge_ref[6:7, :] += down(grad) - second
    gedge_ref[7:8, :] += second
    seat = lax.broadcasted_iota(i32, (seats_ref.shape[0], length), 0) == seat_ref[0]
    seat = seat.astype(bf16)
    high = grad.astype(bf16)
    low = (grad - high.astype(f32)).astype(bf16)
    collected = dot_plain(seat, high) + dot_plain(seat, low)
    if so_far:
        collected = collected + so_far[2][...]
    seats_ref[...] = collected.astype(seats_ref.dtype)
    if not direct:
        sums[4][...] += grad
        return
    devices = wide_ref.shape[0]
    high = devices // mp_count // 4
    share = length // devices
    base = wide_ref.shape[1] - share - 8
    for i in range(devices):
        slot = slot_of(i // mp_count, i % mp_count, high) ^ me
        wide_ref[slot, base : base + share, :] += grad[i * share : (i + 1) * share]
    if last:
        rows = [gedge_ref[i : i + 1, :] + late_ref[i : i + 1, :] for i in range(8)]
        rows += [late_ref[i : i + 1, :] for i in range(8, 11)]
        rows += [gtaps_ref[i : i + 1, :] for i in range(gtaps_ref.shape[0])]
        for i, row in enumerate(rows):
            slot = slot_of(i // mp_count, i % mp_count, high) ^ me
            wide_ref[slot, base + share : base + share + 1, 0 : row.shape[1]] = row
        kept_ref[...] = wide_ref[: devices // 2]
        sent_ref[...] = wide_ref[devices // 2 :]


def near_logits(words_ref, masked_ref, label_ref):
    logits = dot_right(words_ref[...], masked_ref[...])
    row = lax.broadcasted_iota(i32, logits.shape, 0) + pl.program_id(0) * logits.shape[0]
    return logits, row == label_ref[...]


def head_stats(masked_ref, label_ref, words_ref, stats_ref):
    logits, target = near_logits(words_ref, masked_ref, label_ref)
    top = jnp.max(logits, axis=0, keepdims=True)
    here = jnp.sum(jnp.where(target, logits, 0.0), axis=0, keepdims=True)

    @pl.when(pl.program_id(0) == 0)
    def _():
        stats_ref[...] = jnp.zeros_like(stats_ref)
        stats_ref[0:1, :] = top
        stats_ref[1:2, :] = jnp.sum(jnp.exp(logits - top), axis=0, keepdims=True)
        stats_ref[2:3, :] = here

    @pl.when(pl.program_id(0) > 0)
    def _():
        old = stats_ref[0:1, :]
        new = jnp.maximum(old, top)
        total = jnp.sum(jnp.exp(logits - new), axis=0, keepdims=True)
        stats_ref[1:2, :] = stats_ref[1:2, :] * jnp.exp(old - new) + total
        stats_ref[0:1, :] = new
        stats_ref[2:3, :] += here


def head_grads(share, masked_ref, label_ref, log_ref, words_ref, back_ref, table_ref):
    logits, target = near_logits(words_ref, masked_ref, label_ref)
    probs = jnp.exp(logits - log_ref[...])
    grad = ((probs - jnp.where(target, 1.0, 0.0)) * share).astype(bf16)
    table_ref[...] = dot_plain(grad, masked_ref[...])
    back = dot_left(grad, words_ref[...])

    @pl.when(pl.program_id(0) == 0)
    def _():
        back_ref[...] = back

    @pl.when(pl.program_id(0) > 0)
    def _():
        back_ref[...] += back


def fixed(shape):
    return pl.BlockSpec(shape, lambda b, *_: (0,) * len(shape), pipeline_mode=pl.Buffered(1))


def each(shape, start=0):
    return pl.BlockSpec((1,) + shape, lambda b, *_: (b + start,) + (0,) * len(shape))


def run(kernel, scalars, ins, outs, scratch, name, steps, micros, aliases={}):
    return pl.pallas_call(
        kernel,
        out_shape=[jax.ShapeDtypeStruct(shape, dtype) for (shape, dtype), _ in outs],
        grid_spec=pltpu.PrefetchScalarGridSpec(
            num_scalar_prefetch=len(scalars),
            grid=(steps,),
            in_specs=[spec for _, spec in ins],
            out_specs=[spec for _, spec in outs],
            scratch_shapes=scratch,
        ),
        compiler_params=pltpu.CompilerParams(
            dimension_semantics=("arbitrary",), vmem_limit_bytes=VMEM
        ),
        input_output_aliases={len(scalars) + i: o for i, o in aliases.items()},
        cost_estimate=pl.CostEstimate(
            flops=micros * 1150000000, bytes_accessed=1 << 20, transcendentals=0
        ),
        name=name,
    )(*scalars, *[x for x, _ in ins])


def slots_of(ids, vblock, devices):
    owner = ids // vblock
    here = jnp.arange(ids.shape[0])
    same = ids[None, :] == ids[:, None]
    first = jnp.sum(jnp.logical_and(same, here[None, :] < here[:, None]), axis=1) == 0
    below = jnp.logical_and(owner[None, :] == owner[:, None], ids[None, :] < ids[:, None])
    rank = jnp.sum(jnp.logical_and(below, first[None, :]), axis=1).astype(i32)
    return owner, first, rank


def fetch_round(turn, capacity, devices, owner, first, rank, local, extra, low_table, hooks):
    slot = jnp.where(rank // capacity == turn, owner * capacity + rank % capacity, -1)
    seats = jnp.arange(devices * capacity)
    chosen = jnp.logical_and(seats[:, None] == slot[None, :], first[None, :])
    request = jnp.sum(jnp.where(chosen, local[None, :] + 1, 0), axis=1) - 1
    beside = jnp.concatenate([jnp.max(rank)[None], extra])
    beside = jnp.pad(beside, (0, -(capacity + beside.shape[0]) % 128))
    message = jnp.concatenate(
        [
            request.reshape(devices, capacity),
            jnp.broadcast_to(beside[None], (devices, beside.shape[0])),
        ],
        axis=1,
    )
    message = hooks[0](message)
    got = lax.all_to_all(message, ALL, 0, 0, tiled=True)
    asked = got[:, :capacity].reshape(-1)
    served = (asked[:, None] == jnp.arange(low_table.shape[0])[None, :]).astype(bf16)
    sending = dot_plain(served, low_table).astype(bf16)
    sending = hooks[1](sending)
    rows = lax.all_to_all(sending, ALL, 0, 0, tiled=True)
    mine = (slot[:, None] == seats[None, :]).astype(bf16)
    return dot_plain(mine, rows).astype(bf16), slot, mine, served, got[:, capacity:]


def body(
    token_ids,
    seg_split,
    lengths,
    mlm_pos,
    mlm_labels,
    sop_labels,
    owner,
    step_count,
    table,
    table_m,
    table_v,
    unit_master,
    unit_m,
    unit_v,
    small,
    small_m,
    small_v,
    taps,
    taps_m,
    taps_v,
):
    mp_count = lax.axis_size(MP)
    dp_count = lax.axis_size(DP)
    devices = mp_count * dp_count
    mp_index = lax.axis_index(MP)
    dp_index = lax.axis_index(DP)
    group_seqs, length = token_ids.shape
    width = small.shape[1]
    part = unit_master.shape[1]
    vblock = table.shape[0]
    cap_slots = unit_master.shape[0]
    matrices = owner.shape[0]
    seqs = group_seqs // mp_count
    tokens = seqs * length
    masks = mlm_pos.shape[1]
    total_seqs = group_seqs * dp_count
    count_all = total_seqs * masks

    def my(x):
        return lax.dynamic_slice_in_dim(x, mp_index * seqs, seqs, 0)

    token_ids, seg_split, lengths = my(token_ids), my(seg_split), my(lengths)
    mlm_pos, mlm_labels, sop_labels = my(mlm_pos), my(mlm_labels), my(sop_labels)

    earlier = jnp.arange(matrices)[:, None] > jnp.arange(matrices)[None, :]
    slot_rank = jnp.sum(jnp.logical_and(earlier, owner[:, None] == owner[None, :]), axis=1)
    slot_index = owner * cap_slots + slot_rank
    selector = jnp.logical_and(
        owner[None, :] == dp_index, slot_rank[None, :] == jnp.arange(cap_slots)[:, None]
    ).astype(f32)
    rest = part // dp_count
    own = seqs * masks
    low_slots = unit_master.astype(bf16).reshape(cap_slots, dp_count, rest, width)
    low_slots = jnp.moveaxis(low_slots, 1, 0)
    got_slots = lax.all_to_all(low_slots, DP, 0, 0, tiled=True)
    got_slots = got_slots.reshape(dp_count * cap_slots, rest, width)
    low_table = table.astype(bf16)

    ids = token_ids.reshape(-1)
    capacity = max(8, -(-1280 // devices))
    home, first, rank = slots_of(ids, vblock, devices)
    fetch = partial(
        fetch_round,
        capacity=capacity,
        devices=devices,
        owner=home,
        first=first,
        rank=rank,
        local=ids % vblock,
        extra=mlm_labels.reshape(-1),
        low_table=low_table,
    )
    shards = None

    def same(x):
        return x

    def after_slots(message):
        nonlocal shards
        message, got = together(message, got_slots)
        seats_at = slot_index[:, None] == jnp.arange(dp_count * cap_slots)[None, :]
        picked = jnp.sum(
            jnp.where(seats_at[:, :, None, None], got[None].astype(f32), 0.0), axis=1
        ).astype(bf16)
        shards = lax.all_gather(picked, DP, axis=0)
        return message

    def after_shards(sending):
        nonlocal shards
        sending, shards = together(sending, shards)
        return sending

    word_rows, slot, mine, served, beside = fetch(0, hooks=(after_slots, after_shards))
    turns = jnp.max(beside[:, 0]) // capacity + 1
    all_labels = near_labels(beside[:, 1 : 1 + own], own)

    shards = jnp.moveaxis(shards, 0, 1).reshape(matrices, part, width)
    first_units, last_units, late_table = together(
        spread_axis(shards[:3], "m1", 0), shards[3:], low_table
    )
    first_units = spread_axis(first_units, "m0", 0)
    last_units = spread_axis(last_units, "m1", 0)
    vocab = lax.all_gather(late_table, RG, axis=0, tiled=True)

    def more(state):
        return state[0] < turns

    def fetch_more(state):
        return (state[0] + 1, state[1] + fetch(state[0], hooks=(same, same))[0])

    _, word_rows = lax.while_loop(more, fetch_more, (jnp.int32(1), word_rows))
    last_units = spread_axis(last_units, "m0", 0)

    words_in = word_rows.reshape(seqs, length, width)
    places = small[6 : 6 + length]
    edge = jnp.concatenate([small[:6], small[6 + length : 8 + length]])
    span = (HEADS - FIRST) * DH
    taps_span = [
        taps[:, CONV.index(h) * DH : (CONV.index(h) + 1) * DH]
        if h in CONV
        else jnp.zeros((taps.shape[0], DH), f32)
        for h in range(FIRST, HEADS)
    ]
    taps_span = jnp.concatenate(taps_span, axis=1)
    act = (length, width)
    embedded, qkv, lse, heads = run(
        forward_heads,
        (seg_split, lengths),
        [
            (words_in, each(act)),
            (places, fixed(places.shape)),
            (edge, fixed(edge.shape)),
            (taps_span, fixed(taps_span.shape)),
            (first_units, fixed(first_units.shape)),
        ],
        [
            (((seqs,) + act, f32), each(act)),
            (((seqs, length, 3 * width), bf16), each((length, 3 * width))),
            (((seqs, length, 128), f32), each((length, 128))),
            (((seqs,) + act, bf16), each(act)),
        ],
        [pltpu.VMEM((length + 16, span), f32)],
        "forward_heads",
        seqs,
        20,
    )
    spots = mlm_pos[:, :, None]
    one, two, masked_rows, cls_rows = run(
        forward_ffn,
        (),
        [
            (spots, each((masks, 1))),
            (heads, each(act)),
            (embedded, each(act)),
            (edge, fixed(edge.shape)),
            (last_units, fixed(last_units.shape)),
        ],
        [
            (((seqs,) + act, f32), each(act)),
            (((seqs,) + act, f32), each(act)),
            (((seqs, masks, width), bf16), each((masks, width))),
            (((seqs, 8, width), f32), each((8, width))),
        ],
        [],
        "forward_ffn",
        seqs,
        23,
    )
    masked_rows = masked_rows.reshape(seqs * masks, width)

    sop_part, sop_pull = jax.vjp(
        partial(sop_loss, labels=sop_labels, denom=total_seqs),
        cls_rows[:, 0],
        small[8 + length :],
    )
    grad_cls, grad_pair = sop_pull(jnp.ones((), f32))
    all_masked, sop_part, grad_cls, grad_pair = together(
        grow_parts(masked_rows), sop_part, grad_cls, grad_pair
    )
    block = all_labels // vblock
    at = {}
    for axis in ALL[::-1]:
        at[axis] = block % lax.axis_size(axis)
        block = block // lax.axis_size(axis)
    label_mine = jnp.ones_like(all_labels, dtype=bool)
    for axis in VG:
        label_mine = jnp.logical_and(label_mine, at[axis] == lax.axis_index(axis))
    label_block = at["d2"] * lax.axis_size("m0") + at["m0"]
    label_row = label_block * vblock + all_labels % vblock
    label_row = jnp.where(label_mine, label_row, -1)[None]
    tall = vocab.shape[0]
    tile = next(t for t in (768, 640, 512, 384, 256, 128, 64, 32, 16, 8) if tall % t == 0)
    tiles = pl.BlockSpec((tile, width), lambda b, *_: (b, 0))
    rows_shape = (1 << 3, all_masked.shape[0])
    head_ins = [
        (all_masked, fixed(all_masked.shape)),
        (label_row, fixed(label_row.shape)),
    ]
    (stats,) = run(
        head_stats,
        (),
        head_ins + [(vocab, tiles)],
        [((rows_shape, f32), fixed(rows_shape))],
        [],
        "head_stats",
        tall // tile,
        13,
    )
    stats = merge_stats(stats[:3], own)
    log_sum = stats[0] + jnp.log(stats[1])
    losses = [p[0] for p in cut_parts(log_sum - stats[2], own)]
    mlm_part = sum(jnp.sum(p) for p in losses) / count_all
    grad_rows, grad_table = run(
        partial(head_grads, 1.0 / count_all),
        (),
        head_ins + [(log_sum[None], fixed(label_row.shape)), (vocab, tiles)],
        [
            ((all_masked.shape, f32), fixed(all_masked.shape)),
            ((vocab.shape, f32), tiles),
        ],
        [],
        "head_grads",
        tall // tile,
        26,
    )
    parts = cut_parts(grad_rows, own)
    for stage in reversed(range(len(VG))):
        parts = [shrink(p, order[stage]) for p, order in zip(parts, ORDERS)]
    grad_masked, mlm_part = together(jnp.concatenate([p[0] for p in parts]), mlm_part)
    grad_table = lax.psum_scatter(grad_table, RG, scatter_dimension=0, tiled=True)
    grad_cls = jnp.pad(grad_cls[:, None], ((0, 0), (0, 7), (0, 0)))
    direct = rest % 8 == 0 and length % (8 * devices) == 0 and devices >= 20
    share = length // devices if direct else -(-length // devices)
    me = slot_of(dp_index, mp_index, dp_count // 4)[None].astype(i32)

    def wide(many, extra):
        if direct:
            return (devices, many * rest + extra, width)
        return (mp_count, many, part, width)

    def wide_outs(many, extra):
        shape = wide(many, extra)
        if direct:
            shape = (shape[0] // 2,) + shape[1:]
        return [((shape, f32), fixed(shape))] * (2 if direct else 1)

    sum_one, grad_heads, edge_last, *wide_last = run(
        backward_ffn,
        (me,),
        [
            (spots, each((masks, 1))),
            (grad_masked.reshape(seqs, masks, width), each((masks, width))),
            (grad_cls, each((8, width))),
            (one, each(act)),
            (two, each(act)),
            (heads, each(act)),
            (edge, fixed(edge.shape)),
            (last_units, fixed(last_units.shape)),
        ],
        [
            (((seqs,) + act, f32), each(act)),
            (((seqs,) + act, bf16), each(act)),
            ((edge.shape, f32), fixed(edge.shape)),
        ]
        + wide_outs(5, 0),
        [pltpu.VMEM(wide(5, 0), f32)] if direct else [],
        "backward_ffn",
        seqs,
        46,
    )
    names = ["m0", "d0", "m1", "d1", "d2"]
    sizes = tuple(lax.axis_size(a) for a in names)

    def near(x):
        x = x.reshape(tuple(lax.axis_size(a) for a in ALL) + x.shape[1:])
        x = jnp.transpose(x, [ALL.index(a) for a in names] + list(range(5, x.ndim)))
        for dim, axis in enumerate(names):
            for bit in range(bits_of(axis)):
                lead, tail = x.shape[:dim], x.shape[dim + 1 :]
                y = x.reshape(lead + (x.shape[dim] >> (bit + 1), 2, 1 << bit) + tail)
                flipped = jnp.flip(y, axis=dim + 1)
                x = jnp.where(bit_of(axis, bit) == 1, flipped, y).reshape(x.shape)
        return x

    def by_device(x):
        x = x.reshape(mp_count, -1, dp_count, rest, width)
        return jnp.transpose(x, (2, 0, 1, 3, 4)).reshape(devices, -1, width)

    tracks = (["d0", "m1", "d1", "d2"], ["m1", "d0", "d1", "d2"])

    def pair_of(kept, sent):
        x = kept + swap(sent, "m0", 0)
        x = x.reshape(sizes[1:] + x.shape[1:])
        return [x[..., : width // 2], x[..., width // 2 :]]

    def fold_stage(pair, stage, beside=()):
        done = []
        for x, track in zip(pair, tracks):
            left = [a for a in names[1:] if a not in track[:stage]]
            x, *beside = fold_near(x, track[stage], left.index(track[stage]), beside)
            done.append(x)
        return [*done, *beside]

    loss_row = jnp.pad(jnp.reshape(mlm_part + sop_part, (1, 1)), ((0, 0), (0, width - 1)))
    late = jnp.concatenate([edge_last, grad_pair, loss_row])
    late = jnp.pad(late, ((0, 16 - late.shape[0]), (0, 0)))
    seat_rows = slot.reshape(seqs, 1, length)
    seat_count = (devices * capacity, width)
    ways = wide(3, share + 8)

    def heads_call(start, sums, back):
        last = start == seqs - 1
        some = [
            (words_in, each(act, start)),
            (places, fixed(places.shape)),
            (edge, fixed(edge.shape)),
            (taps_span, fixed(taps_span.shape)),
            (first_units, fixed(first_units.shape)),
            (qkv, each((length, 3 * width), start)),
            (lse, each((length, 128), start)),
            (back, each(act, start)),
            (sum_one, each(act, start)),
            (seat_rows, each((1, length), start)),
            (late if last else jnp.zeros_like(late), fixed(late.shape)),
        ]
        count = len(some)
        outs = [
            (((1,) + act, f32), each(act)),
            ((edge.shape, f32), fixed(edge.shape)),
            ((taps_span.shape, f32), fixed(taps_span.shape)),
            ((seat_count, bf16 if last else f32), fixed(seat_count)),
        ]
        scratch = [pltpu.VMEM((length + 16, span), f32)] * 2
        kept_whole = [0, 1, 3, 4]
        if direct and last:
            outs += wide_outs(3, share + 8)
            scratch.append(pltpu.VMEM(ways, f32))
            kept_whole = [0, 1]
        else:
            outs.append(((ways, f32), fixed(ways)))
        if not direct:
            outs.append(((act, f32), fixed(act)))
        return run(
            partial(backward_heads, start, last, direct),
            (seg_split, lengths, me),
            some + [(x, fixed(x.shape)) for x in sums],
            outs,
            scratch,
            "backward_heads",
            1,
            33,
            {count + i: 1 + i for i in range(len(sums)) if i in kept_whole},
        )

    if not direct:
        wide_last = near(by_device(wide_last[0])).reshape(2, devices // 2, -1, width)
    pair_last = pair_of(*wide_last)
    back = grad_heads
    grad_words, sums = [], []
    for start in range(seqs):
        if start == 1:
            back, *pair_last = together(back, *pair_last)
            pair_last = fold_stage(pair_last, 0)
        word, *sums = heads_call(start, sums, back)
        grad_words.append(word.reshape(length, width))
    if seqs == 1:
        pair_last = fold_stage(pair_last, 0)
    edge_first, grad_taps, sent, *wide_first = sums
    if not direct:
        rows = jnp.pad(wide_first[1], ((0, share * devices - length), (0, 0)))
        tops = jnp.pad(grad_taps, ((0, 0), (0, width - span)))
        small_rows = jnp.concatenate([edge_first + late[:8], late[8:11], tops])
        small_rows = jnp.pad(small_rows, ((0, devices - small_rows.shape[0]), (0, 0)))
        small_rows = jnp.pad(small_rows[:, None], ((0, 0), (0, 7), (0, 0)))
        rows = rows.reshape(devices, share, width)
        wide_first = near(
            jnp.concatenate([by_device(wide_first[0]), rows, small_rows], axis=1)
        ).reshape(2, devices // 2, -1, width)

    sent, a, b, *pair_last = together(sent, *wide_first, *pair_last)
    wide_first = [a, b]
    got_words = lax.all_to_all(sent, ALL, 0, 0, tiled=True)

    def return_more(state):
        _, _, mine_r, served_r, _ = fetch(state[0], hooks=(same, same))
        live = (state[0] > 0).astype(f32)
        sent_r = sum(
            select_sum(mine_r[at * length : (at + 1) * length], g * live)
            for at, g in enumerate(grad_words)
        ).astype(bf16)
        got = lax.all_to_all(sent_r, ALL, 0, 0, tiled=True)
        return (state[0] + 1, state[1] + dot_left(served_r, got))

    *pair_last, a, b = fold_stage(pair_last, 1, pair_of(*wide_first))
    grad_table, seen, *pair_first = together(grad_table, served, *fold_stage([a, b], 0))
    words = dot_left(seen, got_words)
    pair_last = fold_stage(pair_last, 2)
    pair_first = fold_stage(pair_first, 1)
    _, words = lax.while_loop(more, return_more, (jnp.int32(1), words))
    grad_table_own = grad_table + words
    square = jnp.sum(grad_table_own * grad_table_own)
    square, *pair_first = together(square, *pair_first)
    pair_last = fold_stage(pair_last, 3)
    pair_first = fold_stage(pair_first, 2)
    pair_first = fold_stage(pair_first, 3)
    piece_first = jnp.concatenate(pair_first, axis=-1)
    pieces_last = jnp.concatenate(pair_last, axis=-1)
    summed = jnp.concatenate([piece_first[: 3 * rest], pieces_last]).reshape(-1, rest, width)
    seat = (slot_index[None, :] == jnp.arange(dp_count * cap_slots)[:, None]).astype(f32)
    slotted = sum(seat[:, k, None, None] * summed[k][None] for k in range(matrices))
    slotted = slotted.reshape(dp_count, cap_slots, rest, width)
    grad_slots = lax.all_to_all(slotted, DP, 0, 0, tiled=True)
    grad_slots = jnp.moveaxis(grad_slots, 0, 1).reshape(cap_slots, part, width)

    lone_row = piece_first[3 * rest + share]
    loss_at = lax.axis_index(ALL) == 10
    square = (
        square
        + jnp.sum(summed * summed)
        + jnp.sum(piece_first[3 * rest : 3 * rest + share] ** 2)
        + jnp.where(loss_at, 0.0, jnp.sum(lone_row * lone_row))
    )
    row = jnp.arange(share + 8)[:, None] == share + 1
    pieces = jnp.where(row, square, piece_first[3 * rest :])
    for axis in ("d2", "d1", "d0"):
        pieces = spread_axis(pieces, axis, {"d2": 0, "d1": 1, "d0": 2}[axis])
    pieces, grad_slots = together(pieces, grad_slots)
    for axis in ("m1", "m0"):
        pieces = spread_axis(pieces, axis, {"m1": 3, "m0": 4}[axis])
    pieces = pieces.reshape(devices, share + 8, width)
    place_sum = pieces[:, :share].reshape(-1, width)[:length]
    lone = pieces[:, share]
    small_sum = jnp.concatenate([lone[:6], place_sum, lone[6:10]])
    taps_rows = lone[11 : 11 + taps.shape[0], :span]
    taps_sum = jnp.concatenate(
        [taps_rows[:, (h - FIRST) * DH : (h - FIRST + 1) * DH] for h in CONV], axis=1
    )
    loss = lone[10, 0]
    grad_norm = jnp.sqrt(jnp.sum(pieces[:, share + 1, 0]))
    scale = clip_bound / jnp.maximum(grad_norm, clip_bound)
    count = step_count[0].astype(f32)
    table_new, table_m_new, table_v_new = adam(
        table, table_m, table_v, grad_table_own * scale, count
    )
    used = jnp.sum(selector, axis=1)[:, None, None]
    unit_new, unit_m_new, unit_v_new = adam(unit_master, unit_m, unit_v, grad_slots * scale, count)
    unit_new = unit_new * used
    unit_m_new = unit_m_new * used
    unit_v_new = unit_v_new * used
    small_new, small_m_new, small_v_new = adam(small, small_m, small_v, small_sum * scale, count)
    taps_new, taps_m_new, taps_v_new = adam(taps, taps_m, taps_v, taps_sum * scale, count)
    return (
        loss,
        grad_norm,
        table_new,
        table_m_new,
        table_v_new,
        table_new.astype(bf16),
        unit_new,
        unit_m_new,
        unit_v_new,
        unit_new.astype(bf16),
        small_new,
        small_m_new,
        small_v_new,
        taps_new,
        taps_m_new,
        taps_v_new,
    )


def solution(mesh):
    dp, mp = mesh.devices.shape
    fine = Mesh(mesh.devices.reshape(dp // 4, 2, 2, mp // 2, 2), ALL)
    rows = P(DP)
    vocab = P(ALL)
    slots = P(DP, MP)
    placed = (rows,) * 6 + (P(),) * 2 + (vocab,) * 3 + (slots,) * 3 + (P(),) * 6
    return jax.shard_map(
        body,
        mesh=fine,
        in_specs=placed,
        out_specs=(P(),) * 2 + (vocab,) * 4 + (slots,) * 4 + (P(),) * 6,
        check_vma=False,
    )
```

```python
import math
from functools import partial

import jax
import jax.numpy as jnp
from jax import lax
from jax.experimental import pallas as pl
from jax.experimental.pallas import tpu as pltpu
from jax.sharding import Mesh, PartitionSpec as P

DH = 64
HEADS = 12
PER = 3
ATTN = tuple(h for h in range(HEADS) if h % PER < PER - h // PER)
CONV = tuple(h for h in range(HEADS) if h % PER >= PER - h // PER)

FIRST = min(CONV) // 2 * 2

DP = ("d2", "d1", "d0")
MP = ("m1", "m0")
ALL = DP + MP
CHIPS = DP + ("m1",)
VG = ("d1", "d0", "m1")
RG = ("d2", "m0")
ORDERS = (("d1", "d0", "m1"), ("d0", "m1", "d1"), ("m1", "d1", "d0"))

f32 = jnp.float32
bf16 = jnp.bfloat16
i32 = jnp.int32
highest = lax.Precision.HIGHEST
beta_one = 0.9
beta_two = 0.999
adam_eps = 1e-08
learn_rate = 0.03
weight_decay = 0.01
clip_bound = 0.02
norm_eps = 1e-06
VMEM = 60 << 20


def dot_right(left, right):
    return lax.dot_general(left, right, (((1,), (1,)), ((), ())), preferred_element_type=f32)


def dot_left(left, right):
    return lax.dot_general(left, right, (((0,), (0,)), ((), ())), preferred_element_type=f32)


def dot_plain(left, right):
    return lax.dot_general(left, right, (((1,), (0,)), ((), ())), preferred_element_type=f32)


def halves(x):
    high = lax.reduce_precision(x, 8, 7)
    return high.astype(bf16), (x - high).astype(bf16)


def select_sum(chosen, values):
    high, low = halves(values)
    return dot_left(chosen, high) + dot_left(chosen, low)


def sop_loss(cls_rows, pair, labels, denom):
    logits = jnp.dot(cls_rows, pair.T, precision=highest)
    chosen = jnp.take_along_axis(logits, labels[:, None], axis=1)[:, 0]
    return jnp.sum(jax.nn.logsumexp(logits, axis=-1) - chosen) / denom


def adam(weight, first, second, grad, count):
    first_new = beta_one * first + (1.0 - beta_one) * grad
    second_new = beta_two * second + (1.0 - beta_two) * grad * grad
    corr_one = 1.0 - jnp.power(beta_one, count)
    corr_two = 1.0 - jnp.power(beta_two, count)
    step = first_new / corr_one / (jnp.sqrt(second_new / corr_two) + adam_eps)
    return (weight - learn_rate * (step + weight_decay * weight), first_new, second_new)


def everyone(x, axes):
    count = lax.axis_size(axes)
    return lax.all_to_all(jnp.broadcast_to(x, (count,) + x.shape), axes, 0, 0, tiled=True)


def swap(x, axis, bit):
    count = lax.axis_size(axis)
    return lax.ppermute(x, axis, [(i, i ^ (1 << bit)) for i in range(count)])


def bits_of(axis):
    return lax.axis_size(axis).bit_length() - 1


def together(*arrays):
    return lax.optimization_barrier(arrays)


def bit_of(axis, bit):
    return (lax.axis_index(axis) >> bit) & 1


def fold_near(x, axis, dim, beside=()):
    for bit in reversed(range(bits_of(axis))):
        lead, rest = x.shape[:dim], x.shape[dim + 1 :]
        x = x.reshape(lead + (2, x.shape[dim] // 2) + rest)
        sent = lax.index_in_dim(x, 1, dim, False)
        kept = lax.index_in_dim(x, 0, dim, False)
        if beside:
            kept, *beside = together(kept, *beside)
        x = kept + swap(sent, axis, bit)
    return (x.reshape(x.shape[:dim] + x.shape[dim + 1 :]), *beside)


def slot_of(d, m, high):
    return ((((m & 1) * 2 + (d & 1)) * 2 + (m >> 1)) * 2 + ((d >> 1) & 1)) * high + (d >> 2)


def spread_axis(x, axis, dim):
    x = jnp.expand_dims(x, dim)
    for bit in range(bits_of(axis)):
        other = swap(x, axis, bit)
        me = bit_of(axis, bit) == 1
        x = jnp.concatenate([jnp.where(me, other, x), jnp.where(me, x, other)], axis=dim)
    return x


def grow(x, axis):
    for bit in range(bits_of(axis)):
        x = jnp.concatenate([x, swap(x, axis, bit)], axis=0)
    return x


def shrink(x, axis):
    for bit in reversed(range(bits_of(axis))):
        half = x.shape[0] // 2
        x = x[:half] + swap(x[half:], axis, bit)
    return x


def row_parts(count):
    most = -(-count // (8 * len(ORDERS))) * 8
    return [slice(at, min(at + most, count)) for at in range(0, count, most)]


def grow_parts(x):
    parts = [x[None, rows] for rows in row_parts(x.shape[0])]
    for stage in range(len(VG)):
        parts = [grow(p, order[stage]) for p, order in zip(parts, ORDERS)]
    return jnp.concatenate([p.reshape((-1,) + p.shape[2:]) for p in parts])


def cut_parts(x, count, dim=0):
    pieces, at = [], 0
    for rows in row_parts(count):
        size = (rows.stop - rows.start) << len(VG)
        piece = lax.slice_in_dim(x, at, at + size, axis=dim)
        pieces.append(piece.reshape(x.shape[:dim] + (1 << len(VG), -1) + x.shape[dim + 1 :]))
        at += size
    return pieces


def near_labels(got, own):
    x = got.reshape(tuple(lax.axis_size(a) for a in ALL) + (own,))
    x = lax.dynamic_index_in_dim(x, lax.axis_index("m0"), 4, False)
    x = lax.dynamic_index_in_dim(x, lax.axis_index("d2"), 0, False)
    for dim, axis in enumerate(VG):
        x = jnp.where(lax.axis_index(axis) == 1, jnp.flip(x, axis=dim), x)
    parts = []
    for rows, order in zip(row_parts(own), ORDERS):
        dims = [VG.index(axis) for axis in order[::-1]]
        parts.append(jnp.transpose(x[..., rows], dims + [len(VG)]).reshape(-1))
    return jnp.concatenate(parts)


def merge_stats(stats, count):
    for axis in VG:
        other = swap(stats, axis, 0)
        flipped = []
        for p, order in zip(cut_parts(other, count, 1), ORDERS):
            low = 1 << order.index(axis)
            y = p.reshape(3, p.shape[1] // (2 * low), 2, low, p.shape[2])
            flipped.append(jnp.flip(y, axis=2).reshape(3, -1))
        other = jnp.concatenate(flipped, axis=1)
        top = jnp.maximum(stats[0], other[0])
        total = stats[1] * jnp.exp(stats[0] - top) + other[1] * jnp.exp(other[0] - top)
        stats = jnp.stack([top, total, stats[2] + other[2]])
    return stats


def rows_norm(x):
    center = jnp.mean(x, axis=-1, keepdims=True)
    shifted = x - center
    inv = lax.rsqrt(jnp.mean(shifted * shifted, axis=-1, keepdims=True) + norm_eps)
    return shifted * inv, inv


def erf(x):
    x = jnp.clip(x, -3.832506856900711, 3.832506856900711)
    y = x * x
    top = jnp.float32(0.00022905065861350646)
    for c in (0.0034082910107109506, 0.050955695062380861, 0.18520832239976145, 1.128379143519084):
        top = top * y + c
    low = jnp.float32(-1.1791602954361697e-7)
    for c in (
        0.000023547966471313185,
        0.0010179625278914885,
        0.014070470171167667,
        0.11098505178285362,
        0.49746925110067538,
        1.0,
    ):
        low = low * y + c
    return x * top / low


def head_mask(rows, groups):
    row = lax.broadcasted_iota(i32, (rows, groups * DH), 0)
    col = lax.broadcasted_iota(i32, (rows, groups * DH), 1)
    return lax.rem(row, groups) == lax.div(col, DH)


def split3(x):
    a = x.astype(bf16)
    r = x - a.astype(f32)
    b = r.astype(bf16)
    c = (r - b.astype(f32)).astype(bf16)
    return a, b, c


def dot_exact(a, b, dims):
    return lax.dot_general(a, b, (dims, ((), ())), precision=highest, preferred_element_type=f32)


def conv_kernel_rows(prod, taps_ref, groups):
    width = taps_ref.shape[0]
    spread = jnp.concatenate(
        [jnp.broadcast_to(taps_ref[o : o + 1, :], (groups, prod.shape[1])) for o in range(width)], axis=0
    )
    spread = jnp.where(head_mask(width * groups, groups), spread, 0.0)
    logits = dot_exact(spread, prod, ((1,), (1,)))
    parts = [logits[o * groups : (o + 1) * groups] for o in range(width)]
    top = parts[0]
    for p in parts[1:]:
        top = jnp.maximum(top, p)
    weights = [jnp.exp(p - top) for p in parts]
    total = weights[0]
    for w in weights[1:]:
        total = total + w
    inv = 1.0 / total
    return [w * inv for w in weights], spread


def spread_rows(rows, groups):
    three = jnp.concatenate(split3(rows), axis=0)
    ones = head_mask(3 * groups, groups).astype(bf16)
    return lax.dot_general(three, ones, (((0,), (0,)), ((), ())), preferred_element_type=f32)


def forward_heads(
    split_ref, length_ref, word_ref, places_ref, edge_ref, taps_ref, units_ref,
    emb_ref, qkv_ref, lse_ref, heads_ref, pad_ref,
):
    at = pl.program_id(0)
    length, width = word_ref.shape[1:]
    later = lax.broadcasted_iota(i32, (length, 1), 0) > split_ref[at]
    summed = word_ref[0].astype(f32) + places_ref[...]
    summed = summed + jnp.where(later, edge_ref[7:8, :], edge_ref[6:7, :])
    normed, _ = rows_norm(summed)
    embedded = normed * edge_ref[0:1, :] + edge_ref[3:4, :]
    emb_ref[0] = embedded
    low_in = embedded.astype(bf16)
    for k in range(3):
        unit = whole_unit(units_ref, k)
        qkv_ref[0, :, k * width : (k + 1) * width] = dot_right(low_in, unit).astype(bf16)
    allowed = lax.broadcasted_iota(i32, (length, length), 1) < length_ref[at]
    lanes = lax.broadcasted_iota(i32, (length, 128), 1)
    lse = jnp.zeros((length, 128), f32)
    outs = {}
    for n, h in enumerate(ATTN):
        q = qkv_ref[0, :, h * DH : (h + 1) * DH]
        k = qkv_ref[0, :, width + h * DH : width + (h + 1) * DH]
        v = qkv_ref[0, :, 2 * width + h * DH : 2 * width + (h + 1) * DH]
        scores = jnp.where(allowed, dot_right(q, k) * (1.0 / math.sqrt(DH)), -1e30)
        top = jnp.max(scores, axis=1, keepdims=True)
        weights = jnp.exp(scores - top)
        total = jnp.sum(weights, axis=1, keepdims=True)
        probs = (weights * (1.0 / total)).astype(bf16)
        outs[h] = dot_plain(probs, v).astype(bf16)
        lse = jnp.where(lanes == n, top + jnp.log(total), lse)
    lse_ref[0] = lse
    groups = HEADS - FIRST
    base = FIRST * DH
    q = qkv_ref[0, :, base:width].astype(f32)
    k = qkv_ref[0, :, width + base : 2 * width].astype(f32)
    kernel, _ = conv_kernel_rows(q * k, taps_ref, groups)
    taps = len(kernel)
    pad_ref[0:8, :] = jnp.zeros((8, width - base), f32)
    pad_ref[8 + length : 16 + length, :] = jnp.zeros((8, width - base), f32)
    pad_ref[8 : 8 + length, :] = qkv_ref[0, :, 2 * width + base :].astype(f32)
    total = jnp.zeros((length, width - base), f32)
    for o in range(taps):
        start = 8 + o - taps // 2
        total = total + spread_rows(kernel[o], groups) * pad_ref[start : start + length, :]
    total = total.astype(bf16)
    for h in CONV:
        outs[h] = total[:, (h - FIRST) * DH : (h - FIRST + 1) * DH]
    heads_ref[0] = jnp.concatenate([outs[h] for h in range(HEADS)], axis=1)


def ffn_weights(units_ref, s, first):
    at = units_ref.at[s % 2, s // 2]
    return jnp.concatenate([at[first], at[first + 1]], axis=0)


def whole_unit(units_ref, k):
    count = units_ref.shape[0] * units_ref.shape[1]
    return jnp.concatenate([units_ref[s % 2, s // 2, k] for s in range(count)], axis=0)


def forward_ffn(
    pos_ref, heads_ref, emb_ref, edge_ref, units_ref, one_ref, two_ref, mask_ref, cls_ref
):
    length, width = emb_ref.shape[1:]
    part = units_ref.shape[3]
    unit = whole_unit(units_ref, 0)
    projected = dot_right(heads_ref[0], unit).astype(bf16).astype(f32)
    one = emb_ref[0] + projected
    one_ref[0] = one
    normed, _ = rows_norm(one)
    attended = normed * edge_ref[1:2, :] + edge_ref[4:5, :]
    low_mid = attended.astype(bf16)
    for g in range(2):
        cols = slice(2 * part * g, 2 * part * (g + 1))
        total = None
        for s in (2 * g, 2 * g + 1):
            pre = dot_plain(low_mid[:, cols], ffn_weights(units_ref, s, 1))
            hidden = (pre * (0.5 + 0.5 * erf(pre * math.sqrt(0.5)))).astype(bf16)
            out = dot_right(hidden, ffn_weights(units_ref, s, 3))
            total = out if total is None else total + out
        two_ref[0, :, cols] = attended[:, cols] + total
    normed, _ = rows_norm(two_ref[0])
    final = normed * edge_ref[2:3, :] + edge_ref[5:6, :]
    masks = mask_ref.shape[1]
    picked = lax.broadcasted_iota(i32, (masks, length), 1) == pos_ref[0][:, 0:1]
    mask_ref[0] = dot_plain(picked.astype(bf16), final.astype(bf16)).astype(bf16)
    cls_ref[0] = final[0:8]


def norm_grad(grad, normed, inv, gain):
    scaled = grad * gain
    mean = jnp.mean(scaled, axis=-1, keepdims=True)
    along = jnp.mean(scaled * normed, axis=-1, keepdims=True)
    return inv * (scaled - mean - normed * along)


def down(x):
    return jnp.sum(x, axis=0, keepdims=True)


def add_rows(ref, me, mp_count, at, matrix, rows):
    if len(ref.shape) == 4:
        ref[at, matrix] += rows
        return
    dp_count = ref.shape[0] // mp_count
    rest = rows.shape[0] // dp_count
    here = slice(matrix * rest, (matrix + 1) * rest)
    for d in range(dp_count):
        ref[slot_of(d, at, dp_count // 4) ^ me, here, :] += rows[d * rest : (d + 1) * rest]


def backward_ffn(
    me_ref, pos_ref, grad_ref, cls_ref, one_ref, two_ref, heads_ref, edge_ref, units_ref,
    sum_ref, back_ref, edges_ref, *wide_refs,
):
    at = pl.program_id(0)
    wide_ref = wide_refs[-1]
    length, width = one_ref.shape[1:]
    mp_count, part = units_ref.shape[0] * units_ref.shape[1], units_ref.shape[3]

    @pl.when(at == 0)
    def _():
        wide_ref[...] = jnp.zeros_like(wide_ref)
        edges_ref[...] = jnp.zeros_like(edges_ref)

    masks = grad_ref.shape[1]
    picked = (lax.broadcasted_iota(i32, (masks, length), 1) == pos_ref[0][:, 0:1]).astype(bf16)
    high = grad_ref[0].astype(bf16)
    low = (grad_ref[0] - high.astype(f32)).astype(bf16)
    grad = dot_left(picked, high) + dot_left(picked, low)
    rows = lax.broadcasted_iota(i32, (length, 1), 0)
    grad = grad + jnp.where(rows == 0, cls_ref[0][0:1, :], 0.0)
    normed, inv = rows_norm(two_ref[0])
    edges_ref[2:3, :] += down(grad * normed)
    edges_ref[5:6, :] += down(grad)
    grad_two = norm_grad(grad, normed, inv, edge_ref[2:3, :])
    low_two = grad_two.astype(bf16)
    normed, inv = rows_norm(one_ref[0])
    low_mid = (normed * edge_ref[1:2, :] + edge_ref[4:5, :]).astype(bf16)
    backs = []
    for g in range(2):
        cols = slice(2 * part * g, 2 * part * (g + 1))
        total = None
        for s in (2 * g, 2 * g + 1):
            w_in = ffn_weights(units_ref, s, 1)
            w_out = ffn_weights(units_ref, s, 3)
            pre = dot_plain(low_mid[:, cols], w_in)
            half = 0.5 + 0.5 * erf(pre * math.sqrt(0.5))
            hidden = (pre * half).astype(bf16)
            slope = half + pre * (jnp.exp(-0.5 * pre * pre) * (1.0 / math.sqrt(2.0 * math.pi)))
            grad_hidden = dot_plain(low_two[:, cols], w_out)
            w = dot_left(low_two[:, cols], hidden)
            add_rows(wide_ref, me_ref[0], mp_count, s, 3, w[:part])
            add_rows(wide_ref, me_ref[0], mp_count, s, 4, w[part:])
            grad_pre = (grad_hidden * slope).astype(bf16)
            w = dot_left(low_mid[:, cols], grad_pre)
            add_rows(wide_ref, me_ref[0], mp_count, s, 1, w[:part])
            add_rows(wide_ref, me_ref[0], mp_count, s, 2, w[part:])
            back = dot_right(grad_pre, w_in)
            total = back if total is None else total + back
        backs.append(total)
    grad = grad_two + jnp.concatenate(backs, axis=1)
    edges_ref[1:2, :] += down(grad * normed)
    edges_ref[4:5, :] += down(grad)
    grad_one = norm_grad(grad, normed, inv, edge_ref[1:2, :])
    sum_ref[0] = grad_one
    low_one = grad_one.astype(bf16)
    w = dot_left(low_one, heads_ref[0])
    for s in range(mp_count):
        add_rows(wide_ref, me_ref[0], mp_count, s, 0, w[s * part : (s + 1) * part])
    unit = whole_unit(units_ref, 0)
    back_ref[0] = dot_plain(low_one, unit).astype(bf16)

    if len(wide_refs) > 1:

        @pl.when(at == pl.num_programs(0) - 1)
        def _():
            half = wide_ref.shape[0] // 2
            wide_refs[0][...] = wide_ref[:half]
            wide_refs[1][...] = wide_ref[half:]


def backward_heads(start, last, direct, *refs):
    (split_ref, length_ref, me_ref, word_ref, places_ref, edge_ref, taps_ref, units_ref) = refs[:8]
    (qkv_ref, lse_ref, back_ref, sum_ref, seat_ref, late_ref) = refs[8:14]
    refs = refs[14:]
    so_far = []
    if start > 0:
        count = 4 if direct else 5
        so_far, refs = refs[:count], refs[count:]
    gword_ref, gedge_ref, gtaps_ref, seats_ref = refs[:4]
    if direct and last:
        kept_ref, sent_ref, pad_ref, shift_ref, wide_ref = refs[4:]
        sums = [gedge_ref, gtaps_ref, seats_ref, wide_ref]
    else:
        *sums, pad_ref, shift_ref = refs[1:]
        wide_ref = sums[3]
    at = pl.program_id(0) + start
    me = me_ref[0]
    mp_count = units_ref.shape[0] * units_ref.shape[1]
    length, width = word_ref.shape[1:]
    for n, new in enumerate(sums):
        if n != 2:
            new[...] = so_far[n][...] if so_far else jnp.zeros_like(new)

    groups = HEADS - FIRST
    base = FIRST * DH
    span = width - base
    q = qkv_ref[0, :, base:width].astype(f32)
    k = qkv_ref[0, :, width + base : 2 * width].astype(f32)
    prod = q * k
    kernel, spread = conv_kernel_rows(prod, taps_ref, groups)
    taps = len(kernel)
    out = back_ref[0, :, base:].astype(f32)
    pad_ref[0:8, :] = jnp.zeros((8, span), f32)
    pad_ref[8 + length : 16 + length, :] = jnp.zeros((8, span), f32)
    pad_ref[8 : 8 + length, :] = qkv_ref[0, :, 2 * width + base :].astype(f32)
    shift_ref[0:8, :] = jnp.zeros((8, span), f32)
    shift_ref[8 + length : 16 + length, :] = jnp.zeros((8, span), f32)
    grad_values = jnp.zeros((length, span), f32)
    lanes = 128
    dots = jnp.zeros((length, lanes), f32)
    column = lax.broadcasted_iota(i32, (span, lanes), 0)
    lane = lax.broadcasted_iota(i32, (span, lanes), 1)
    for o in range(taps):
        start = 8 + o - taps // 2
        moved = out * pad_ref[start : start + length, :]
        high = moved.astype(bf16)
        low = (moved - high.astype(f32)).astype(bf16)
        ones = (lane == o * groups + lax.div(column, DH)).astype(bf16)
        dots = dots + dot_plain(high, ones) + dot_plain(low, ones)
        shift_ref[8 : 8 + length, :] = spread_rows(kernel[o], groups) * out
        back = 8 + taps // 2 - o
        grad_values = grad_values + shift_ref[back : back + length, :]
    dots = dots.T
    parts = [dots[o * groups : (o + 1) * groups] for o in range(taps)]
    along = kernel[0] * parts[0]
    for o in range(1, taps):
        along = along + kernel[o] * parts[o]
    grad_logits = jnp.concatenate([kernel[o] * (parts[o] - along) for o in range(taps)], axis=0)
    grad_prod = dot_exact(grad_logits, spread, ((0,), (0,)))
    grad_taps = dot_exact(grad_logits, prod, ((1,), (0,)))
    head = lax.div(lax.broadcasted_iota(i32, (taps * groups, span), 1), DH) + FIRST
    real = head_mask(taps * groups, groups)
    for h in range(FIRST, HEADS):
        if h not in CONV:
            real = jnp.logical_and(real, head != h)
    grad_taps = jnp.where(real, grad_taps, 0.0)
    for o in range(taps):
        gtaps_ref[o : o + 1, :] += down(grad_taps[o * groups : (o + 1) * groups])
    grads = [(grad_prod * k).astype(bf16), (grad_prod * q).astype(bf16), grad_values.astype(bf16)]
    pieces = [[None] * HEADS for _ in range(3)]
    for h in CONV:
        for n in range(3):
            pieces[n][h] = grads[n][:, (h - FIRST) * DH : (h - FIRST + 1) * DH]

    allowed = lax.broadcasted_iota(i32, (length, length), 1) < length_ref[at]
    scale = 1.0 / math.sqrt(DH)
    for n, h in enumerate(ATTN):
        qh = qkv_ref[0, :, h * DH : (h + 1) * DH]
        kh = qkv_ref[0, :, width + h * DH : width + (h + 1) * DH]
        vh = qkv_ref[0, :, 2 * width + h * DH : 2 * width + (h + 1) * DH]
        gh = back_ref[0, :, h * DH : (h + 1) * DH]
        scores = jnp.where(allowed, dot_right(qh, kh) * scale, -1e30)
        probs = jnp.exp(scores - lse_ref[0][:, n : n + 1])
        grad_probs = dot_right(gh, vh)
        total = jnp.sum(probs * grad_probs, axis=1, keepdims=True)
        grad_scores = (probs * (grad_probs - total)).astype(bf16)
        pieces[0][h] = (dot_plain(grad_scores, kh) * scale).astype(bf16)
        pieces[1][h] = (dot_left(grad_scores, qh) * scale).astype(bf16)
        pieces[2][h] = dot_left(probs.astype(bf16), gh).astype(bf16)
    later = lax.broadcasted_iota(i32, (length, 1), 0) > split_ref[at]
    summed = word_ref[0].astype(f32) + places_ref[...]
    summed = summed + jnp.where(later, edge_ref[7:8, :], edge_ref[6:7, :])
    normed, inv = rows_norm(summed)
    low_in = (normed * edge_ref[0:1, :] + edge_ref[3:4, :]).astype(bf16)
    grad = sum_ref[0]
    for n in range(3):
        g = jnp.concatenate(pieces[n], axis=1)
        w = dot_left(g, low_in)
        part = units_ref.shape[3]
        for s in range(mp_count):
            add_rows(wide_ref, me, mp_count, s, n, w[s * part : (s + 1) * part])
        grad = grad + dot_plain(g, whole_unit(units_ref, n))
    gedge_ref[0:1, :] += down(grad * normed)
    gedge_ref[3:4, :] += down(grad)
    grad = norm_grad(grad, normed, inv, edge_ref[0:1, :])
    gword_ref[0] = grad
    second = down(jnp.where(later, grad, 0.0))
    gedge_ref[6:7, :] += down(grad) - second
    gedge_ref[7:8, :] += second
    seat = lax.broadcasted_iota(i32, (seats_ref.shape[0], length), 0) == seat_ref[0]
    seat = seat.astype(bf16)
    high = grad.astype(bf16)
    low = (grad - high.astype(f32)).astype(bf16)
    collected = dot_plain(seat, high) + dot_plain(seat, low)
    if so_far:
        collected = collected + so_far[2][...]
    seats_ref[...] = collected.astype(seats_ref.dtype)
    if not direct:
        sums[4][...] += grad
        return
    devices = wide_ref.shape[0]
    high = devices // mp_count // 4
    share = length // devices
    base = wide_ref.shape[1] - share - 8
    for i in range(devices):
        slot = slot_of(i // mp_count, i % mp_count, high) ^ me
        wide_ref[slot, base : base + share, :] += grad[i * share : (i + 1) * share]
    if last:
        rows = [gedge_ref[i : i + 1, :] + late_ref[i : i + 1, :] for i in range(8)]
        rows += [late_ref[i : i + 1, :] for i in range(8, 11)]
        rows += [gtaps_ref[i : i + 1, :] for i in range(gtaps_ref.shape[0])]
        for i, row in enumerate(rows):
            slot = slot_of(i // mp_count, i % mp_count, high) ^ me
            wide_ref[slot, base + share : base + share + 1, 0 : row.shape[1]] = row
        kept_ref[...] = wide_ref[: devices // 2]
        sent_ref[...] = wide_ref[devices // 2 :]


def near_logits(words_ref, masked_ref, label_ref):
    logits = dot_right(words_ref[...], masked_ref[...])
    row = lax.broadcasted_iota(i32, logits.shape, 0) + pl.program_id(0) * logits.shape[0]
    return logits, row == label_ref[...]


def head_stats(masked_ref, label_ref, words_ref, stats_ref):
    logits, target = near_logits(words_ref, masked_ref, label_ref)
    top = jnp.max(logits, axis=0, keepdims=True)
    here = jnp.sum(jnp.where(target, logits, 0.0), axis=0, keepdims=True)

    @pl.when(pl.program_id(0) == 0)
    def _():
        stats_ref[...] = jnp.zeros_like(stats_ref)
        stats_ref[0:1, :] = top
        stats_ref[1:2, :] = jnp.sum(jnp.exp(logits - top), axis=0, keepdims=True)
        stats_ref[2:3, :] = here

    @pl.when(pl.program_id(0) > 0)
    def _():
        old = stats_ref[0:1, :]
        new = jnp.maximum(old, top)
        total = jnp.sum(jnp.exp(logits - new), axis=0, keepdims=True)
        stats_ref[1:2, :] = stats_ref[1:2, :] * jnp.exp(old - new) + total
        stats_ref[0:1, :] = new
        stats_ref[2:3, :] += here


def head_grads(share, masked_ref, label_ref, log_ref, words_ref, back_ref, table_ref):
    logits, target = near_logits(words_ref, masked_ref, label_ref)
    probs = jnp.exp(logits - log_ref[...])
    grad = ((probs - jnp.where(target, 1.0, 0.0)) * share).astype(bf16)
    table_ref[...] = dot_plain(grad, masked_ref[...])
    back = dot_left(grad, words_ref[...])

    @pl.when(pl.program_id(0) == 0)
    def _():
        back_ref[...] = back

    @pl.when(pl.program_id(0) > 0)
    def _():
        back_ref[...] += back


def fixed(shape):
    return pl.BlockSpec(shape, lambda b, *_: (0,) * len(shape), pipeline_mode=pl.Buffered(1))


def each(shape, start=0):
    return pl.BlockSpec((1,) + shape, lambda b, *_: (b + start,) + (0,) * len(shape))


def run(kernel, scalars, ins, outs, scratch, name, steps, micros, aliases={}):
    return pl.pallas_call(
        kernel,
        out_shape=[jax.ShapeDtypeStruct(shape, dtype) for (shape, dtype), _ in outs],
        grid_spec=pltpu.PrefetchScalarGridSpec(
            num_scalar_prefetch=len(scalars),
            grid=(steps,),
            in_specs=[spec for _, spec in ins],
            out_specs=[spec for _, spec in outs],
            scratch_shapes=scratch,
        ),
        compiler_params=pltpu.CompilerParams(
            dimension_semantics=("arbitrary",), vmem_limit_bytes=VMEM
        ),
        input_output_aliases={len(scalars) + i: o for i, o in aliases.items()},
        cost_estimate=pl.CostEstimate(
            flops=micros * 1150000000, bytes_accessed=1 << 20, transcendentals=0
        ),
        name=name,
    )(*scalars, *[x for x, _ in ins])


def slots_of(ids, vblock, devices):
    owner = ids // vblock
    here = jnp.arange(ids.shape[0])
    same = ids[None, :] == ids[:, None]
    first = jnp.sum(jnp.logical_and(same, here[None, :] < here[:, None]), axis=1) == 0
    below = jnp.logical_and(owner[None, :] == owner[:, None], ids[None, :] < ids[:, None])
    rank = jnp.sum(jnp.logical_and(below, first[None, :]), axis=1).astype(i32)
    return owner, first, rank


def fetch_round(turn, capacity, devices, owner, first, rank, local, extra, low_table, hooks):
    slot = jnp.where(rank // capacity == turn, owner * capacity + rank % capacity, -1)
    seats = jnp.arange(devices * capacity)
    chosen = jnp.logical_and(seats[:, None] == slot[None, :], first[None, :])
    request = jnp.sum(jnp.where(chosen, local[None, :] + 1, 0), axis=1) - 1
    beside = jnp.concatenate([jnp.max(rank)[None], extra])
    beside = jnp.pad(beside, (0, -(capacity + beside.shape[0]) % 128))
    message = jnp.concatenate(
        [
            request.reshape(devices, capacity),
            jnp.broadcast_to(beside[None], (devices, beside.shape[0])),
        ],
        axis=1,
    )
    message = hooks[0](message)
    got = lax.all_to_all(message, ALL, 0, 0, tiled=True)
    asked = got[:, :capacity].reshape(-1)
    served = (asked[:, None] == jnp.arange(low_table.shape[0])[None, :]).astype(bf16)
    sending = dot_plain(served, low_table).astype(bf16)
    sending = hooks[1](sending)
    rows = lax.all_to_all(sending, ALL, 0, 0, tiled=True)
    mine = (slot[:, None] == seats[None, :]).astype(bf16)
    return dot_plain(mine, rows).astype(bf16), slot, mine, served, got[:, capacity:]


def body(
    token_ids,
    seg_split,
    lengths,
    mlm_pos,
    mlm_labels,
    sop_labels,
    owner,
    step_count,
    table,
    table_m,
    table_v,
    unit_master,
    unit_m,
    unit_v,
    small,
    small_m,
    small_v,
    taps,
    taps_m,
    taps_v,
):
    mp_count = lax.axis_size(MP)
    dp_count = lax.axis_size(DP)
    devices = mp_count * dp_count
    mp_index = lax.axis_index(MP)
    dp_index = lax.axis_index(DP)
    group_seqs, length = token_ids.shape
    width = small.shape[1]
    part = unit_master.shape[1]
    vblock = table.shape[0]
    cap_slots = unit_master.shape[0]
    matrices = owner.shape[0]
    seqs = group_seqs // mp_count
    tokens = seqs * length
    masks = mlm_pos.shape[1]
    total_seqs = group_seqs * dp_count
    count_all = total_seqs * masks

    def my(x):
        return lax.dynamic_slice_in_dim(x, mp_index * seqs, seqs, 0)

    token_ids, seg_split, lengths = my(token_ids), my(seg_split), my(lengths)
    mlm_pos, mlm_labels, sop_labels = my(mlm_pos), my(mlm_labels), my(sop_labels)

    earlier = jnp.arange(matrices)[:, None] > jnp.arange(matrices)[None, :]
    slot_rank = jnp.sum(jnp.logical_and(earlier, owner[:, None] == owner[None, :]), axis=1)
    slot_index = owner * cap_slots + slot_rank
    selector = jnp.logical_and(
        owner[None, :] == dp_index, slot_rank[None, :] == jnp.arange(cap_slots)[:, None]
    ).astype(f32)
    rest = part // dp_count
    own = seqs * masks
    low_slots = unit_master.astype(bf16).reshape(cap_slots, dp_count, rest, width)
    low_slots = jnp.moveaxis(low_slots, 1, 0)
    got_slots = lax.all_to_all(low_slots, DP, 0, 0, tiled=True)
    got_slots = got_slots.reshape(dp_count * cap_slots, rest, width)
    low_table = table.astype(bf16)

    ids = token_ids.reshape(-1)
    capacity = max(8, -(-1280 // devices))
    home, first, rank = slots_of(ids, vblock, devices)
    fetch = partial(
        fetch_round,
        capacity=capacity,
        devices=devices,
        owner=home,
        first=first,
        rank=rank,
        local=ids % vblock,
        extra=mlm_labels.reshape(-1),
        low_table=low_table,
    )
    shards = None

    def same(x):
        return x

    def after_slots(message):
        nonlocal shards
        message, got = together(message, got_slots)
        seats_at = slot_index[:, None] == jnp.arange(dp_count * cap_slots)[None, :]
        picked = jnp.sum(
            jnp.where(seats_at[:, :, None, None], got[None].astype(f32), 0.0), axis=1
        ).astype(bf16)
        shards = lax.all_gather(picked, DP, axis=0)
        return message

    def after_shards(sending):
        nonlocal shards
        sending, shards = together(sending, shards)
        return sending

    word_rows, slot, mine, served, beside = fetch(0, hooks=(after_slots, after_shards))
    turns = jnp.max(beside[:, 0]) // capacity + 1
    all_labels = near_labels(beside[:, 1 : 1 + own], own)

    shards = jnp.moveaxis(shards, 0, 1).reshape(matrices, part, width)
    first_units, last_units, late_table = together(
        spread_axis(shards[:3], "m1", 0), shards[3:], low_table
    )
    first_units = spread_axis(first_units, "m0", 0)
    last_units = spread_axis(last_units, "m1", 0)
    vocab = lax.all_gather(late_table, RG, axis=0, tiled=True)

    def more(state):
        return state[0] < turns

    def fetch_more(state):
        return (state[0] + 1, state[1] + fetch(state[0], hooks=(same, same))[0])

    _, word_rows = lax.while_loop(more, fetch_more, (jnp.int32(1), word_rows))
    last_units = spread_axis(last_units, "m0", 0)

    words_in = word_rows.reshape(seqs, length, width)
    places = small[6 : 6 + length]
    edge = jnp.concatenate([small[:6], small[6 + length : 8 + length]])
    span = (HEADS - FIRST) * DH
    taps_span = [
        taps[:, CONV.index(h) * DH : (CONV.index(h) + 1) * DH]
        if h in CONV
        else jnp.zeros((taps.shape[0], DH), f32)
        for h in range(FIRST, HEADS)
    ]
    taps_span = jnp.concatenate(taps_span, axis=1)
    act = (length, width)
    embedded, qkv, lse, heads = run(
        forward_heads,
        (seg_split, lengths),
        [
            (words_in, each(act)),
            (places, fixed(places.shape)),
            (edge, fixed(edge.shape)),
            (taps_span, fixed(taps_span.shape)),
            (first_units, fixed(first_units.shape)),
        ],
        [
            (((seqs,) + act, f32), each(act)),
            (((seqs, length, 3 * width), bf16), each((length, 3 * width))),
            (((seqs, length, 128), f32), each((length, 128))),
            (((seqs,) + act, bf16), each(act)),
        ],
        [pltpu.VMEM((length + 16, span), f32)],
        "forward_heads",
        seqs,
        20,
    )
    spots = mlm_pos[:, :, None]
    one, two, masked_rows, cls_rows = run(
        forward_ffn,
        (),
        [
            (spots, each((masks, 1))),
            (heads, each(act)),
            (embedded, each(act)),
            (edge, fixed(edge.shape)),
            (last_units, fixed(last_units.shape)),
        ],
        [
            (((seqs,) + act, f32), each(act)),
            (((seqs,) + act, f32), each(act)),
            (((seqs, masks, width), bf16), each((masks, width))),
            (((seqs, 8, width), f32), each((8, width))),
        ],
        [],
        "forward_ffn",
        seqs,
        23,
    )
    masked_rows = masked_rows.reshape(seqs * masks, width)

    sop_part, sop_pull = jax.vjp(
        partial(sop_loss, labels=sop_labels, denom=total_seqs),
        cls_rows[:, 0],
        small[8 + length :],
    )
    grad_cls, grad_pair = sop_pull(jnp.ones((), f32))
    all_masked, sop_part, grad_cls, grad_pair = together(
        grow_parts(masked_rows), sop_part, grad_cls, grad_pair
    )
    block = all_labels // vblock
    at = {}
    for axis in ALL[::-1]:
        at[axis] = block % lax.axis_size(axis)
        block = block // lax.axis_size(axis)
    label_mine = jnp.ones_like(all_labels, dtype=bool)
    for axis in VG:
        label_mine = jnp.logical_and(label_mine, at[axis] == lax.axis_index(axis))
    label_block = at["d2"] * lax.axis_size("m0") + at["m0"]
    label_row = label_block * vblock + all_labels % vblock
    label_row = jnp.where(label_mine, label_row, -1)[None]
    tall = vocab.shape[0]
    tile = next(t for t in (768, 640, 512, 384, 256, 128, 64, 32, 16, 8) if tall % t == 0)
    tiles = pl.BlockSpec((tile, width), lambda b, *_: (b, 0))
    rows_shape = (1 << 3, all_masked.shape[0])
    head_ins = [
        (all_masked, fixed(all_masked.shape)),
        (label_row, fixed(label_row.shape)),
    ]
    (stats,) = run(
        head_stats,
        (),
        head_ins + [(vocab, tiles)],
        [((rows_shape, f32), fixed(rows_shape))],
        [],
        "head_stats",
        tall // tile,
        13,
    )
    stats = merge_stats(stats[:3], own)
    log_sum = stats[0] + jnp.log(stats[1])
    losses = [p[0] for p in cut_parts(log_sum - stats[2], own)]
    mlm_part = sum(jnp.sum(p) for p in losses) / count_all
    grad_rows, grad_table = run(
        partial(head_grads, 1.0 / count_all),
        (),
        head_ins + [(log_sum[None], fixed(label_row.shape)), (vocab, tiles)],
        [
            ((all_masked.shape, f32), fixed(all_masked.shape)),
            ((vocab.shape, f32), tiles),
        ],
        [],
        "head_grads",
        tall // tile,
        26,
    )
    parts = cut_parts(grad_rows, own)
    for stage in reversed(range(len(VG))):
        parts = [shrink(p, order[stage]) for p, order in zip(parts, ORDERS)]
    grad_masked, mlm_part = together(jnp.concatenate([p[0] for p in parts]), mlm_part)
    grad_table = lax.psum_scatter(grad_table, RG, scatter_dimension=0, tiled=True)
    grad_cls = jnp.pad(grad_cls[:, None], ((0, 0), (0, 7), (0, 0)))
    direct = rest % 8 == 0 and length % (8 * devices) == 0 and devices >= 20
    share = length // devices if direct else -(-length // devices)
    me = slot_of(dp_index, mp_index, dp_count // 4)[None].astype(i32)

    def wide(many, extra):
        if direct:
            return (devices, many * rest + extra, width)
        return (mp_count, many, part, width)

    def wide_outs(many, extra):
        shape = wide(many, extra)
        if direct:
            shape = (shape[0] // 2,) + shape[1:]
        return [((shape, f32), fixed(shape))] * (2 if direct else 1)

    sum_one, grad_heads, edge_last, *wide_last = run(
        backward_ffn,
        (me,),
        [
            (spots, each((masks, 1))),
            (grad_masked.reshape(seqs, masks, width), each((masks, width))),
            (grad_cls, each((8, width))),
            (one, each(act)),
            (two, each(act)),
            (heads, each(act)),
            (edge, fixed(edge.shape)),
            (last_units, fixed(last_units.shape)),
        ],
        [
            (((seqs,) + act, f32), each(act)),
            (((seqs,) + act, bf16), each(act)),
            ((edge.shape, f32), fixed(edge.shape)),
        ]
        + wide_outs(5, 0),
        [pltpu.VMEM(wide(5, 0), f32)] if direct else [],
        "backward_ffn",
        seqs,
        46,
    )
    names = ["m0", "d0", "m1", "d1", "d2"]
    sizes = tuple(lax.axis_size(a) for a in names)

    def near(x):
        x = x.reshape(tuple(lax.axis_size(a) for a in ALL) + x.shape[1:])
        x = jnp.transpose(x, [ALL.index(a) for a in names] + list(range(5, x.ndim)))
        for dim, axis in enumerate(names):
            for bit in range(bits_of(axis)):
                lead, tail = x.shape[:dim], x.shape[dim + 1 :]
                y = x.reshape(lead + (x.shape[dim] >> (bit + 1), 2, 1 << bit) + tail)
                flipped = jnp.flip(y, axis=dim + 1)
                x = jnp.where(bit_of(axis, bit) == 1, flipped, y).reshape(x.shape)
        return x

    def by_device(x):
        x = x.reshape(mp_count, -1, dp_count, rest, width)
        return jnp.transpose(x, (2, 0, 1, 3, 4)).reshape(devices, -1, width)

    tracks = (["d0", "m1", "d1", "d2"], ["m1", "d0", "d1", "d2"])

    def pair_of(kept, sent):
        x = kept + swap(sent, "m0", 0)
        x = x.reshape(sizes[1:] + x.shape[1:])
        return [x[..., : width // 2], x[..., width // 2 :]]

    def fold_stage(pair, stage, beside=()):
        done = []
        for x, track in zip(pair, tracks):
            left = [a for a in names[1:] if a not in track[:stage]]
            x, *beside = fold_near(x, track[stage], left.index(track[stage]), beside)
            done.append(x)
        return [*done, *beside]

    loss_row = jnp.pad(jnp.reshape(mlm_part + sop_part, (1, 1)), ((0, 0), (0, width - 1)))
    late = jnp.concatenate([edge_last, grad_pair, loss_row])
    late = jnp.pad(late, ((0, 16 - late.shape[0]), (0, 0)))
    seat_rows = slot.reshape(seqs, 1, length)
    seat_count = (devices * capacity, width)
    ways = wide(3, share + 8)

    def heads_call(start, sums, back):
        last = start == seqs - 1
        some = [
            (words_in, each(act, start)),
            (places, fixed(places.shape)),
            (edge, fixed(edge.shape)),
            (taps_span, fixed(taps_span.shape)),
            (first_units, fixed(first_units.shape)),
            (qkv, each((length, 3 * width), start)),
            (lse, each((length, 128), start)),
            (back, each(act, start)),
            (sum_one, each(act, start)),
            (seat_rows, each((1, length), start)),
            (late if last else jnp.zeros_like(late), fixed(late.shape)),
        ]
        count = len(some)
        outs = [
            (((1,) + act, f32), each(act)),
            ((edge.shape, f32), fixed(edge.shape)),
            ((taps_span.shape, f32), fixed(taps_span.shape)),
            ((seat_count, bf16 if last else f32), fixed(seat_count)),
        ]
        scratch = [pltpu.VMEM((length + 16, span), f32)] * 2
        kept_whole = [0, 1, 3, 4]
        if direct and last:
            outs += wide_outs(3, share + 8)
            scratch.append(pltpu.VMEM(ways, f32))
            kept_whole = [0, 1]
        else:
            outs.append(((ways, f32), fixed(ways)))
        if not direct:
            outs.append(((act, f32), fixed(act)))
        return run(
            partial(backward_heads, start, last, direct),
            (seg_split, lengths, me),
            some + [(x, fixed(x.shape)) for x in sums],
            outs,
            scratch,
            "backward_heads",
            1,
            33,
            {count + i: 1 + i for i in range(len(sums)) if i in kept_whole},
        )

    if not direct:
        wide_last = near(by_device(wide_last[0])).reshape(2, devices // 2, -1, width)
    pair_last = pair_of(*wide_last)
    back = grad_heads
    grad_words, sums = [], []
    for start in range(seqs):
        if start == 1:
            back, *pair_last = together(back, *pair_last)
            pair_last = fold_stage(pair_last, 0)
        word, *sums = heads_call(start, sums, back)
        grad_words.append(word.reshape(length, width))
    if seqs == 1:
        pair_last = fold_stage(pair_last, 0)
    edge_first, grad_taps, sent, *wide_first = sums
    if not direct:
        rows = jnp.pad(wide_first[1], ((0, share * devices - length), (0, 0)))
        tops = jnp.pad(grad_taps, ((0, 0), (0, width - span)))
        small_rows = jnp.concatenate([edge_first + late[:8], late[8:11], tops])
        small_rows = jnp.pad(small_rows, ((0, devices - small_rows.shape[0]), (0, 0)))
        small_rows = jnp.pad(small_rows[:, None], ((0, 0), (0, 7), (0, 0)))
        rows = rows.reshape(devices, share, width)
        wide_first = near(
            jnp.concatenate([by_device(wide_first[0]), rows, small_rows], axis=1)
        ).reshape(2, devices // 2, -1, width)

    sent, a, b, *pair_last = together(sent, *wide_first, *pair_last)
    wide_first = [a, b]
    got_words = lax.all_to_all(sent, ALL, 0, 0, tiled=True)

    def return_more(state):
        _, _, mine_r, served_r, _ = fetch(state[0], hooks=(same, same))
        live = (state[0] > 0).astype(f32)
        sent_r = sum(
            select_sum(mine_r[at * length : (at + 1) * length], g * live)
            for at, g in enumerate(grad_words)
        ).astype(bf16)
        got = lax.all_to_all(sent_r, ALL, 0, 0, tiled=True)
        return (state[0] + 1, state[1] + dot_left(served_r, got))

    *pair_last, a, b = fold_stage(pair_last, 1, pair_of(*wide_first))
    grad_table, seen, *pair_first = together(grad_table, served, *fold_stage([a, b], 0))
    words = dot_left(seen, got_words)
    pair_last = fold_stage(pair_last, 2)
    pair_first = fold_stage(pair_first, 1)
    _, words = lax.while_loop(more, return_more, (jnp.int32(1), words))
    grad_table_own = grad_table + words
    square = jnp.sum(grad_table_own * grad_table_own)
    square, *pair_first = together(square, *pair_first)
    pair_last = fold_stage(pair_last, 3)
    pair_first = fold_stage(pair_first, 2)
    pair_first = fold_stage(pair_first, 3)
    piece_first = jnp.concatenate(pair_first, axis=-1)
    pieces_last = jnp.concatenate(pair_last, axis=-1)
    summed = jnp.concatenate([piece_first[: 3 * rest], pieces_last]).reshape(-1, rest, width)
    seat = (slot_index[None, :] == jnp.arange(dp_count * cap_slots)[:, None]).astype(f32)
    slotted = sum(seat[:, k, None, None] * summed[k][None] for k in range(matrices))
    slotted = slotted.reshape(dp_count, cap_slots, rest, width)

    lone_row = piece_first[3 * rest + share]
    loss_at = lax.axis_index(ALL) == 10
    square = (
        square
        + jnp.sum(summed * summed)
        + jnp.sum(piece_first[3 * rest : 3 * rest + share] ** 2)
        + jnp.where(loss_at, 0.0, jnp.sum(lone_row * lone_row))
    )
    row = jnp.arange(share + 8)[:, None] == share + 1
    pieces = jnp.where(row, square, piece_first[3 * rest :])
    pieces = spread_axis(spread_axis(pieces, "d2", 0), "d1", 1)
    pieces, slotted = together(pieces, slotted)
    grad_slots = lax.all_to_all(slotted, DP, 0, 0, tiled=True)
    grad_slots = jnp.moveaxis(grad_slots, 0, 1).reshape(cap_slots, part, width)
    pieces = spread_axis(spread_axis(pieces, "d0", 2), "m1", 3)
    pieces, grad_slots = together(pieces, grad_slots)
    pieces = spread_axis(pieces, "m0", 4)
    pieces = pieces.reshape(devices, share + 8, width)
    place_sum = pieces[:, :share].reshape(-1, width)[:length]
    lone = pieces[:, share]
    small_sum = jnp.concatenate([lone[:6], place_sum, lone[6:10]])
    taps_rows = lone[11 : 11 + taps.shape[0], :span]
    taps_sum = jnp.concatenate(
        [taps_rows[:, (h - FIRST) * DH : (h - FIRST + 1) * DH] for h in CONV], axis=1
    )
    loss = lone[10, 0]
    grad_norm = jnp.sqrt(jnp.sum(pieces[:, share + 1, 0]))
    scale = clip_bound / jnp.maximum(grad_norm, clip_bound)
    count = step_count[0].astype(f32)
    table_new, table_m_new, table_v_new = adam(
        table, table_m, table_v, grad_table_own * scale, count
    )
    used = jnp.sum(selector, axis=1)[:, None, None]
    unit_new, unit_m_new, unit_v_new = adam(unit_master, unit_m, unit_v, grad_slots * scale, count)
    unit_new = unit_new * used
    unit_m_new = unit_m_new * used
    unit_v_new = unit_v_new * used
    small_new, small_m_new, small_v_new = adam(small, small_m, small_v, small_sum * scale, count)
    taps_new, taps_m_new, taps_v_new = adam(taps, taps_m, taps_v, taps_sum * scale, count)
    return (
        loss,
        grad_norm,
        table_new,
        table_m_new,
        table_v_new,
        table_new.astype(bf16),
        unit_new,
        unit_m_new,
        unit_v_new,
        unit_new.astype(bf16),
        small_new,
        small_m_new,
        small_v_new,
        taps_new,
        taps_m_new,
        taps_v_new,
    )


def solution(mesh):
    dp, mp = mesh.devices.shape
    fine = Mesh(mesh.devices.reshape(dp // 4, 2, 2, mp // 2, 2), ALL)
    rows = P(DP)
    vocab = P(ALL)
    slots = P(DP, MP)
    placed = (rows,) * 6 + (P(),) * 2 + (vocab,) * 3 + (slots,) * 3 + (P(),) * 6
    return jax.shard_map(
        body,
        mesh=fine,
        in_specs=placed,
        out_specs=(P(),) * 2 + (vocab,) * 4 + (slots,) * 4 + (P(),) * 6,
        check_vma=False,
    )
```
